32 devices in a mesh: row: 4 (over z), col: 8 (over y, x, core).
Axes of the slice: x: 2, y: 2, z: 4, core: 2. Of those that a mesh axis runs over, the one named last changes fastest.
Arguments:
- block_cells: float32 [352, 5, 16, 256], P(('row', 'col')), may hold values from -0.6 to 1.4, as said below
- slot_blocks: int32 [32, 11], replicated, may hold values from -1 to 191, as said below
Outputs:
- new_cells: float32 [224, 5, 16, 256], P(('row', 'col'))
The draws below stay inside these ranges and needn't reach their ends.
Inputs may be any that keep to these rules, and one draw needn't show every extreme that they name: `slot_blocks`: row r * 8 + c lists the blocks held by device (r, c): block ids first, in slot order, then -1. Block b belongs to column group b // 24, and every block of column group c is held by exactly one device of that column group. Each device holds 1 to 11 blocks, the devices of a column group hold 24 blocks together, and in every column group one device holds 11 blocks and one holds 1. `block_cells`: fields 0 and 4 (density, pressure) lie in 0.7 to 1.4 and fields 1 to 3 (velocity) in -0.6 to 0.6. Slots marked -1 in slot_blocks hold values that no output depends on.
All inputs are finite; a program needn't handle non-finite values.
Results may differ from the reference program's by a relative error of at most 0.0001.
Values sent between devices are 32-bit elements; how exact they have to be, the bound alone decides.
A program may use at most 64 MiB of HBM per device.

```python
import jax
import jax.numpy as jnp
from jax import lax

B = 16
BLK_MEAN = 6
CAP = 11
OUT = 7
NBY = 24
NBLK = 192
N_ROW = 4
N_COL = 8


def draw_slot_blocks(key, part):
    row_count = N_ROW
    columns = N_COL
    per_group = BLK_MEAN * row_count
    slot_width = 2 * BLK_MEAN - 1

    def one_group(column):
        group_key = jax.random.fold_in(jax.random.fold_in(key, 17), column)
        order_key, delta_key, block_key = jax.random.split(group_key, 3)
        shuffle = jax.random.permutation(order_key, row_count)
        deltas = jax.random.randint(delta_key, (row_count // 2 - 1,), 0, BLK_MEAN).astype(jnp.int32)
        paired = jnp.stack([BLK_MEAN + deltas, BLK_MEAN - deltas], axis=1).reshape(-1)
        values = jnp.concatenate([jnp.array([slot_width, 1], jnp.int32), paired.astype(jnp.int32)])
        counts = jnp.zeros((row_count,), jnp.int32).at[shuffle].set(values)
        starts = jnp.cumsum(counts) - counts
        blocks = column * per_group + jax.random.permutation(block_key, per_group).astype(jnp.int32)
        slot_ids = jnp.arange(slot_width, dtype=jnp.int32)
        gather_at = jnp.clip(starts[:, None] + slot_ids[None, :], 0, per_group - 1)
        return jnp.where(slot_ids[None, :] < counts[:, None], blocks[gather_at], -1)
    layout = jax.vmap(one_group)(jnp.arange(columns, dtype=jnp.int32))
    return layout.transpose(1, 0, 2).reshape(row_count * columns, slot_width).astype(jnp.int32)


def draw_block_cells(key, part):
    total_slots = N_ROW * N_COL * CAP
    shape_one = (total_slots, 1, B, B * B)
    density_key, motion_key, pressure_key = jax.random.split(jax.random.fold_in(key, 29), 3)
    matter_per_volume = jax.random.uniform(density_key, shape_one, jnp.float32, 0.7, 1.4)
    velocity = jnp.clip(0.2 * jax.random.normal(motion_key, (total_slots, 3, B, B * B), jnp.float32), -0.6, 0.6)
    fluid_static_stress = jax.random.uniform(pressure_key, shape_one, jnp.float32, 0.7, 1.4)
    return jnp.concatenate([matter_per_volume, velocity, fluid_static_stress], axis=1).astype(jnp.float32)


def setup_inputs(seed: int = 0) -> dict:
    key_list = jax.random.split(jax.random.key(seed), 3)
    block_cells = draw_block_cells(jax.random.fold_in(key_list[2], 71), 0)
    slot_blocks = draw_slot_blocks(jax.random.fold_in(key_list[2], 71), 0)
    return {"block_cells": block_cells, "slot_blocks": slot_blocks}


heat_ratio = 1.4
time_step = 0.12
thermal_leading_multiplier = 0.2
thermal_power_law_index = 0.7

def rebalance_table(anchors, counts):
    row_count, columns, slot_width = anchors.shape
    slot_ids = jnp.arange(slot_width, dtype=jnp.int32)
    row_ids = jnp.arange(row_count, dtype=jnp.int32)
    for section_bit in range(row_count.bit_length() - 1):
        partner = row_ids ^ 1 << section_bit
        other_anchors = anchors[partner]
        other_counts = counts[partner]
        sending = jnp.maximum(counts - other_counts, 0) // 2
        taking = jnp.maximum(other_counts - counts, 0) // 2
        keeping = (counts - sending)[:, :, None]
        anchor_slot = other_counts[:, :, None] - taking[:, :, None] + slot_ids - keeping
        pulled = jnp.take_along_axis(other_anchors, jnp.clip(anchor_slot, 0, slot_width - 1), axis=2)
        anchors = jnp.where(slot_ids < keeping, anchors, jnp.where(slot_ids < keeping + taking[:, :, None], pulled, -1))
        counts = counts - sending + taking
    return (anchors, counts)

def to_conserved(primitive):
    matter_per_volume = primitive[0]
    velocity = primitive[1:4]
    fluid_static_stress = primitive[4]
    energy = fluid_static_stress / (heat_ratio - 1.0) + 0.5 * matter_per_volume * lax.optimization_barrier(jnp.sum(velocity * velocity, axis=0))
    return jnp.concatenate([matter_per_volume[None], matter_per_volume[None] * velocity, energy[None]], axis=0)

def to_primitive(conserved):
    matter_per_volume = conserved[0]
    velocity = conserved[1:4] / matter_per_volume
    fluid_static_stress = (heat_ratio - 1.0) * (conserved[4] - 0.5 * matter_per_volume * lax.optimization_barrier(jnp.sum(velocity * velocity, axis=0)))
    return jnp.concatenate([matter_per_volume[None], velocity, fluid_static_stress[None]], axis=0)

def cell_terms(conserved, normal):
    matter_per_volume = conserved[0]
    momentum = conserved[1:4]
    velocity = momentum / matter_per_volume
    fluid_static_stress = (heat_ratio - 1.0) * (conserved[4] - 0.5 * matter_per_volume * lax.optimization_barrier(jnp.sum(velocity * velocity, axis=0)))
    perpendicular_flow_rate = velocity[normal]
    moment_flux = momentum * perpendicular_flow_rate
    moment_flux = moment_flux.at[normal].add(fluid_static_stress)
    face_transport_amounts = jnp.concatenate([momentum[normal][None], moment_flux, ((conserved[4] + fluid_static_stress) * perpendicular_flow_rate)[None]], axis=0)
    sound_signal_rate = jnp.sqrt(heat_ratio * fluid_static_stress / matter_per_volume)
    fluid_thermal_state = fluid_static_stress / matter_per_volume
    thermal_diffusivity_factor = thermal_leading_multiplier * jnp.power(fluid_thermal_state, thermal_power_law_index)
    return (face_transport_amounts, jnp.abs(perpendicular_flow_rate) + sound_signal_rate, fluid_thermal_state, thermal_diffusivity_factor, fluid_static_stress)

def face_flux(lower_cons, lower_data, upper_cons, upper_data):
    wave_speed = jnp.maximum(lower_data[1], upper_data[1])
    face_transport_amounts = 0.5 * (lower_data[0] + upper_data[0]) - 0.5 * wave_speed[None] * (upper_cons - lower_cons)
    heat_flow = 0.5 * (lower_data[3] + upper_data[3]) * (upper_data[2] - lower_data[2])
    return face_transport_amounts.at[4].add(-heat_flow)

def wall_flux(fluid_static_stress, normal):
    nothing = jnp.zeros_like(fluid_static_stress)
    members = [nothing, nothing, nothing, nothing, nothing]
    members[normal + 1] = fluid_static_stress
    return jnp.stack(members, axis=0)

def tendency(conserved):
    changes = []
    for normal in range(2):
        axis_at = normal - 3
        cell_data = cell_terms(conserved, normal)
        ahead_data = jax.tree.map(lambda member: jnp.roll(member, -1, axis=axis_at), cell_data)
        face_transport_amounts = face_flux(conserved, cell_data, jnp.roll(conserved, -1, axis=axis_at), ahead_data)
        changes.append(face_transport_amounts - jnp.roll(face_transport_amounts, 1, axis=axis_at))
    cell_data = cell_terms(conserved, 2)
    lower_data = jax.tree.map(lambda member: member[..., :-1], cell_data)
    upper_data = jax.tree.map(lambda member: member[..., 1:], cell_data)
    interior = face_flux(conserved[..., :-1], lower_data, conserved[..., 1:], upper_data)
    fluid_static_stress = cell_data[4]
    faces = jnp.concatenate([wall_flux(fluid_static_stress[..., :1], 2), interior, wall_flux(fluid_static_stress[..., -1:], 2)], axis=-1)
    changes.append(faces[..., 1:] - faces[..., :-1])
    return -(changes[0] + changes[1] + changes[2])

def reference(block_cells, slot_blocks):
    row_count = N_ROW
    columns = N_COL
    slot_width = slot_blocks.shape[1]
    occupied = slot_blocks >= 0
    counts = lax.optimization_barrier(jnp.sum(occupied.astype(jnp.int32), axis=1)).reshape(row_count, columns)
    device_ids = jnp.arange(row_count * columns, dtype=jnp.int32)[:, None]
    anchors = jnp.where(occupied, device_ids * slot_width + jnp.arange(slot_width, dtype=jnp.int32)[None, :], -1)
    anchors = anchors.reshape(row_count, columns, slot_width)
    final_anchors, final_counts = rebalance_table(anchors, counts)
    final_anchors = final_anchors[:, :, :OUT].reshape(-1)
    every_slot = slot_blocks.reshape(-1)
    target = jnp.where(every_slot >= 0, every_slot, NBLK)
    every_block = jnp.zeros((NBLK + 1, 5, B, B * B), jnp.float32).at[target].set(block_cells)[:NBLK]
    grid_x = jnp.arange(columns, dtype=jnp.int32)[:, None]
    grid_y = jnp.arange(NBY, dtype=jnp.int32)[None, :]
    placed = (grid_x + grid_y) % columns * NBY + grid_y
    cell_grid = every_block[placed.reshape(-1)].reshape(columns, NBY, 5, B, B, B)
    cell_grid = cell_grid.transpose(2, 0, 3, 1, 4, 5).reshape(5, columns * B, NBY * B, B)
    initial = to_conserved(cell_grid)
    first_section = initial + time_step * tendency(initial)
    second_section = 0.75 * initial + 0.25 * (first_section + time_step * tendency(first_section))
    third_section = 1.0 / 3.0 * initial + 2.0 / 3.0 * (second_section + time_step * tendency(second_section))
    finished = to_primitive(third_section).reshape(5, columns, B, NBY, B, B)
    by_position = finished.transpose(1, 3, 0, 2, 4, 5).reshape(columns * NBY, 5, B, B * B)
    final_ids = jnp.where(final_anchors >= 0, every_slot[jnp.maximum(final_anchors, 0)], 0)
    column_of = final_ids // NBY
    along_y = final_ids % NBY
    position = (column_of - along_y) % columns * NBY + along_y
    result = by_position[position]
    return jnp.where((final_anchors >= 0)[:, None, None, None], result, jnp.zeros_like(result))
```

```python
import functools

import jax
import jax.numpy as jnp
from jax import lax
from jax.experimental import pallas as pl
from jax.experimental.pallas import tpu as pltpu
from jax.sharding import PartitionSpec as P

MESH = pl.DeviceIdType.MESH
BLK_MEAN = 6
OUT = 7
SEND = BLK_MEAN - 1
LANES = 128
DT = 0.12


def make_tables(slot_blocks, rows, cols, my_row, my_col):
    cap = slot_blocks.shape[1]
    levels = rows.bit_length() - 1
    half = rows // 2
    group = BLK_MEAN * rows
    ids = slot_blocks.reshape(rows, cols, cap)
    counts = jnp.sum((ids >= 0).astype(jnp.int32), axis=2)
    row_ids = jnp.arange(rows, dtype=jnp.int32)
    col_ids = jnp.arange(cols, dtype=jnp.int32)
    at_row = jnp.broadcast_to(row_ids[:, None, None], ids.shape)
    at_slot = jnp.broadcast_to(jnp.arange(cap, dtype=jnp.int32), ids.shape)
    mine = (row_ids[:, None] == my_row) & (col_ids[None, :] == my_col)
    scalars = []
    for level in range(levels):
        bit = 1 << level
        other = counts.reshape(rows // (2 * bit), 2, bit, cols)[:, ::-1].reshape(rows, cols)
        send = jnp.maximum(counts - other, 0) // 2
        take = jnp.maximum(other - counts, 0) // 2
        keep = counts - send
        scalars.append(jnp.sum(jnp.where(mine, keep, 0)))
        hit = at_row[None] == row_ids[:, None, None, None]
        keep_here = jnp.sum(jnp.where(hit, keep[:, None, :, None], 0), axis=0)
        other_here = jnp.sum(jnp.where(hit, other[:, None, :, None], 0), axis=0)
        moved = at_slot >= keep_here
        at_row = jnp.where(moved, at_row ^ bit, at_row)
        at_slot = jnp.where(moved, other_here + at_slot - keep_here, at_slot)
        counts = keep + take
    scalars.append(jnp.sum(jnp.where(mine, counts, 0)))
    place = at_row * 16 + at_slot
    origin = row_ids[:, None, None] * 16 + jnp.arange(cap, dtype=jnp.int32)
    origin = jnp.broadcast_to(origin, ids.shape).reshape(-1)
    flat_ids = ids.reshape(-1)
    flat_place = jnp.where(flat_ids >= 0, place.reshape(-1), 0)
    flat_col = jnp.broadcast_to(col_ids[None, :, None], ids.shape).reshape(-1)
    near_far = jnp.stack([my_row, my_row ^ half])
    left, right = (my_col + cols - 1) % cols, (my_col + 1) % cols
    seat_rows = jnp.concatenate([near_far[:1], near_far, near_far])
    seat_cols = jnp.stack([my_col, right, right, left, left])
    seats = (seat_rows[:, None] * 16 + jnp.arange(OUT, dtype=jnp.int32)).reshape(-1, 1)
    seat_cols = jnp.repeat(seat_cols, OUT)[:, None]
    match = (flat_place[None] == seats) & (flat_col[None] == seat_cols) & (flat_ids >= 0)[None]
    along = jnp.sum(jnp.where(match, flat_ids[None] - flat_col[None] * group, 0), axis=1)
    along = along.reshape(5, OUT)
    here, there_right, there_left = along[:1], along[1:3], along[3:5]
    down, up = (lambda a: (a + group - 1) % group), (lambda a: (a + 1) % group)
    mine = jnp.concatenate([left * group + here, left * group + down(here)])
    mine = jnp.concatenate([mine, right * group + here, right * group + up(here)])
    theirs = jnp.concatenate([there_right, down(there_right), there_left, up(there_left)])
    wanted = jnp.concatenate([mine, theirs + my_col * group]).reshape(-1)
    both = flat_place * 4096 + origin
    found = jnp.sum(jnp.where(flat_ids[None] == wanted[:, None], both[None], 0), axis=1)
    source = found ^ (my_row * 16 * 4097)
    source = jnp.concatenate([source & 4095, source >> 12])
    return jnp.concatenate([jnp.stack(scalars), source])


def cell_values(cons):
    rho, mx, my, mz, energy = cons
    inv = 1.0 / rho
    vel = (mx * inv, my * inv, mz * inv)
    p = 0.4 * (energy - 0.5 * rho * (vel[0] * vel[0] + vel[1] * vel[1] + vel[2] * vel[2]))
    theta = p * inv
    sound = jnp.sqrt(1.4 * theta)
    kappa = 0.2 * jnp.exp(0.7 * jnp.log(theta))
    return vel, p, theta, sound, kappa


def conserved(primitive):
    rho, u, v, w, p = primitive
    energy = p / 0.4 + 0.5 * rho * (u * u + v * v + w * w)
    return (rho, rho * u, rho * v, rho * w, energy)


def direction_values(cons, values, normal):
    vel, p, theta, sound, kappa = values
    un = vel[normal]
    flux = [cons[1 + normal], cons[1] * un, cons[2] * un, cons[3] * un, (cons[4] + p) * un]
    flux[1 + normal] = flux[1 + normal] + p
    return (*cons, *flux, jnp.abs(un) + sound, theta, kappa)


def face(low, high):
    half_speed = 0.5 * jnp.maximum(low[10], high[10])
    out = [0.5 * (low[5 + i] + high[5 + i]) - half_speed * (high[i] - low[i]) for i in range(5)]
    out[4] = out[4] - 0.5 * (low[12] + high[12]) * (high[11] - low[11])
    return out


def block_rate(cons, ghost_x, ghost_y):
    edge, flat = cons[0].shape
    row = lax.broadcasted_iota(jnp.int32, (edge, flat), 0)
    lane = lax.broadcasted_iota(jnp.int32, (edge, flat), 1)
    values = cell_values(cons)
    mid = direction_values(cons, values, 0)
    gx = direction_values(ghost_x, cell_values(ghost_x), 0)
    last = row == edge - 1
    up = [
        jnp.where(last, jnp.concatenate([g, g], axis=0), pltpu.roll(m, edge - 1, 0))
        for m, g in zip(mid, gx)
    ]
    upper = face(mid, up)
    bottom = face(gx, [m[:8] for m in mid])
    change = [
        u - jnp.where(row == 0, jnp.concatenate([b, b], axis=0), pltpu.roll(u, 1, 0))
        for u, b in zip(upper, bottom)
    ]
    mid = direction_values(cons, values, 1)
    gy = direction_values(ghost_y, cell_values(ghost_y), 1)
    last = lane >= flat - edge
    up = [
        jnp.where(last, jnp.concatenate([g, g], axis=1), pltpu.roll(m, flat - edge, 1))
        for m, g in zip(mid, gy)
    ]
    upper = face(mid, up)
    bottom = face(gy, [m[:, :LANES] for m in mid])
    change = [
        t + (u - jnp.where(lane < edge, jnp.concatenate([b, b], axis=1), pltpu.roll(u, edge, 1)))
        for t, u, b in zip(change, upper, bottom)
    ]
    mid = direction_values(cons, values, 2)
    up = [pltpu.roll(m, flat - 1, 1) for m in mid]
    upper = face(mid, up)
    height = lane & (edge - 1)
    zero = jnp.zeros_like(values[1])
    wall = [zero, zero, zero, values[1], zero]
    change = [
        t
        + (
            jnp.where(height == edge - 1, w, u)
            - jnp.where(height == 0, w, pltpu.roll(u, 1, 1))
        )
        for t, u, w in zip(change, upper, wall)
    ]
    return [-t for t in change]


def y_units(n):
    return 2 * ((5 * n + 7) // 8)


def units(n):
    return y_units(n) + (10 * n + 7) // 8


def y_seat(slot, f):
    at = slot * 5 + f
    return 2 * (at >> 3), 16 * (at & 7)


def x_seat(n, slot, f, part):
    at = slot * 10 + 2 * f + part
    return y_units(n) + (at >> 3), at & 7


def kernel(rows, cols, cap, *refs):
    levels = rows.bit_length() - 1
    half = rows // 2
    refs = list(refs)
    tab, cells, out = refs[:3]
    refs = refs[3:]
    send_blocks = refs[:levels]
    recv_blocks = refs[levels : 2 * levels]
    refs = refs[2 * levels :]
    start, now = refs[:2]
    sections = [refs[2 + 10 * i : 12 + 10 * i] for i in range(3)]
    bsend, brecv, hsend, hrecv = refs[32:36]
    my_row, my_col = lax.axis_index("row"), lax.axis_index("col")
    left = (my_row, lax.rem(my_col + cols - 1, cols))
    right = (my_row, lax.rem(my_col + 1, cols))

    def partner(level):
        bit = 1 << level
        return (my_row + bit - 2 * bit * (lax.rem(my_row // bit, 2)), my_col)

    barrier = pltpu.get_barrier_semaphore()
    across = partner(levels - 1)[0]
    beside = [(right, left), ((across, right[1]), (across, left[1]))]
    for device in [*beside[0], *beside[1]] + [partner(level) for level in range(levels)]:
        pl.semaphore_signal(barrier, inc=1, device_id=device, device_id_type=MESH)
    pl.semaphore_wait(barrier, 4 + levels)

    def held(slot, depth):
        value = cells[jnp.minimum(slot, cap - 1)]
        for level in range(depth):
            keep = tab[level]
            got = recv_blocks[level][jnp.clip(slot - keep, 0, SEND - 1)]
            value = jnp.where(slot >= keep, got, value)
        return value

    edge, flat = now.shape[2:]
    tile_lane = lax.broadcasted_iota(jnp.int32, (edge, LANES), 1)
    tile_group = tile_lane >> 4
    ghost_row = lax.broadcasted_iota(jnp.int32, (8, 2 * LANES), 0)

    def tile_of(ref, *seat):
        *lead, unit = seat
        return ref[(*lead, pl.ds(unit, 2))].reshape(edge, LANES)

    def put_tile(ref, unit, tile):
        ref[unit : unit + 2] = tile.reshape(2, 8, LANES)

    def move_blocks(level):
        for k in range(SEND):
            send_blocks[level][k] = held(tab[level] + k, level)
        copy = pltpu.make_async_remote_copy(
            src_ref=send_blocks[level],
            dst_ref=recv_blocks[level],
            send_sem=bsend.at[level],
            recv_sem=brecv.at[level],
            device_id=partner(level),
            device_id_type=MESH,
        )
        copy.start()
        return copy

    def remote(step, at, src, dst, device):
        copy = pltpu.make_async_remote_copy(
            src_ref=src,
            dst_ref=dst,
            send_sem=hsend.at[step, at],
            recv_sem=hrecv.at[step, at],
            device_id=device,
            device_id_type=MESH,
        )
        copy.start()
        return copy

    def pack(blocks, n, buffer, high):
        x = edge - 1 if high else 0
        side = slice(LANES, 2 * LANES) if high else slice(0, LANES)
        for first in range(0, 5 * n, 8):
            tile = None
            for at in range(first, min(first + 8, 5 * n)):
                s, f = at // 5, at % 5
                shift = (edge * (at - first) + (edge if high else 0)) % LANES
                piece = blocks[s, f, :, side]
                piece = pltpu.roll(piece, shift, 1) if shift else piece
                tile = piece if tile is None else jnp.where(tile_group == at - first, piece, tile)
            put_tile(buffer, 2 * (first // 8), tile)
        for s in range(n):
            for f in range(5):
                for part in range(2):
                    unit, row = x_seat(n, s, f, part)
                    buffer[unit, row : row + 1, :] = blocks[
                        s, f, x : x + 1, part * LANES : (part + 1) * LANES
                    ]

    base = levels + 1

    def entry(step, kind, far, slot):
        at = kind * OUT if far is None else 4 * OUT + (kind * 2 + far) * OUT
        return tab[base + (12 * OUT if step else 0) + at + slot]

    def near_seat(code):
        return jnp.minimum(code >> 4, half - 1), code & 15

    def select(step, n, known, pick, first_kind, far):
        for s in range(OUT):
            q, sigma = near_seat(entry(step, first_kind, far, s))
            for f in range(5):
                for part in range(2):
                    unit, row = x_seat(n, sigma, f, part)
                    to, at = x_seat(OUT, s, f, part)
                    pick[to, at : at + 1, :] = known[q, unit, pl.ds(row, 1), :]
        seats = [near_seat(entry(step, first_kind + 1, far, s)) for s in range(OUT)]
        for first in range(0, 5 * OUT, 8):
            tile = None
            for at in range(first, min(first + 8, 5 * OUT)):
                q, sigma = seats[at // 5]
                unit, lane = y_seat(sigma, at % 5)
                shift = (edge * (at - first) + LANES - lane) & (LANES - 1)
                piece = pltpu.roll(tile_of(known, q, unit), shift, 1)
                tile = piece if tile is None else jnp.where(tile_group == at - first, piece, tile)
            put_tile(pick, 2 * (first // 8), tile)

    def begin(step, blocks, n):
        flights = []
        for side in range(2):
            known = sections[step][side]
            pack(blocks, n, known.at[0], side == 0)
            if levels > 1:
                flights.append(remote(step, side, known.at[0], known.at[1], partner(0)))
        return flights

    def gather(step, flights):
        for level in range(1, levels - 1):
            size = 1 << level
            for side in range(2):
                known = sections[step][side]
                flights[side].wait()
                flights[side] = remote(
                    step,
                    2 * level + side,
                    known.at[pl.ds(0, size)],
                    known.at[pl.ds(size, size)],
                    partner(level),
                )
        return flights

    def trade(step, n, flights):
        sent = []
        for side in range(2):
            if flights:
                flights[side].wait()
            for far in (1, 0):
                known, pick, sel = (sections[step][at] for at in (side, 2 + 2 * side + far, 6 + 2 * side + far))
                select(step, n, known, pick, 2 * side, far)
                at = 2 * (levels - 1) + 2 * side + far
                sent.append(remote(step, at, pick, sel, beside[far][side]))
        return sent

    def open_block(slot, carry):
        value = held(slot, levels)
        for f, field in enumerate(conserved([value[f] for f in range(5)])):
            start[slot, f] = field
            now[slot, f] = field
        return carry

    def advance(step):
        lo_near, lo_far, hi_near, hi_far = sections[step][6:]

        def run(slot, carry):
            def near(kind):
                return entry(step, kind, None, slot) < 16 * half

            def x_row(close, away, kind, f):
                parts = []
                for part in range(2):
                    unit, row = x_seat(OUT, slot, f, part)
                    a = close[unit, pl.ds(row, 1), :]
                    b = away[unit, pl.ds(row, 1), :]
                    parts.append(jnp.where(near(kind), a, b))
                return jnp.concatenate(parts, axis=1)

            def y_tile(close, away, kind, f, to):
                unit, lane = y_seat(slot, f)
                tile = jnp.where(near(kind), tile_of(close, unit), tile_of(away, unit))
                return pltpu.roll(tile, (LANES + to - lane) & (LANES - 1), 1)

            ghost_x, ghost_y = [], []
            for f in range(5):
                low = x_row(lo_near, lo_far, 0, f)
                high = x_row(hi_near, hi_far, 2, f)
                ghost_x.append(jnp.where(ghost_row == 0, low, high))
                low = y_tile(lo_near, lo_far, 1, f, 0)
                high = y_tile(hi_near, hi_far, 3, f, LANES - edge)
                ghost_y.append(jnp.where(tile_lane < edge, low, high))
            if step == 0:
                ghost_x, ghost_y = conserved(ghost_x), conserved(ghost_y)
            cons = tuple(now[slot, f] for f in range(5))
            rate = block_rate(cons, tuple(ghost_x), tuple(ghost_y))
            moved = [c + DT * d for c, d in zip(cons, rate)]
            if step == 1:
                moved = [0.75 * start[slot, f] + 0.25 * moved[f] for f in range(5)]
            if step == 2:
                moved = [(1.0 / 3.0) * start[slot, f] + (2.0 / 3.0) * moved[f] for f in range(5)]
                rho = moved[0]
                vel = [m / rho for m in moved[1:4]]
                p = 0.4 * (
                    moved[4] - 0.5 * rho * (vel[0] * vel[0] + vel[1] * vel[1] + vel[2] * vel[2])
                )
                filled = slot < tab[levels]
                for f, field in enumerate((rho, *vel, p)):
                    out[slot, f] = jnp.where(filled, field, 0.0)
            else:
                for f in range(5):
                    now[slot, f] = moved[f]
            return carry

        lax.fori_loop(0, OUT, run, 0)

    moving = move_blocks(0)
    flights = begin(0, cells, cap)
    flights = gather(0, flights)
    for level in range(1, levels):
        moving.wait()
        moving = move_blocks(level)
    flights = trade(0, cap, flights)
    moving.wait()
    lax.fori_loop(0, OUT, open_block, 0)
    for step in range(3):
        if step:
            flights = trade(step, OUT, gather(step, begin(step, now, OUT)))
        for flight in flights:
            flight.wait()
        advance(step)


def body(rows, cols, block_cells, slot_blocks):
    cap = slot_blocks.shape[1]
    levels = rows.bit_length() - 1
    half = rows // 2
    edge, flat = block_cells.shape[2:]
    table = make_tables(slot_blocks, rows, cols, lax.axis_index("row"), lax.axis_index("col"))
    block = (5, edge, flat)
    scratch = [pltpu.VMEM((SEND, *block), jnp.float32) for _ in range(2 * levels)]
    scratch += [pltpu.VMEM((OUT, *block), jnp.float32) for _ in range(2)]
    for step in range(3):
        faces = (units(OUT if step else cap), 8, LANES)
        picked = (units(OUT), 8, LANES)
        scratch += [pltpu.VMEM((half, *faces), jnp.float32) for _ in range(2)]
        scratch += [pltpu.VMEM(picked, jnp.float32) for _ in range(8)]
    scratch += [pltpu.SemaphoreType.DMA((levels,)) for _ in range(2)]
    scratch += [pltpu.SemaphoreType.DMA((3, 2 * (levels + 1))) for _ in range(2)]
    return pl.pallas_call(
        functools.partial(kernel, rows, cols, cap),
        out_shape=jax.ShapeDtypeStruct((OUT, *block), jnp.float32),
        in_specs=[
            pl.BlockSpec(memory_space=pltpu.SMEM),
            pl.BlockSpec(memory_space=pltpu.VMEM),
        ],
        out_specs=pl.BlockSpec(memory_space=pltpu.VMEM),
        scratch_shapes=scratch,
        compiler_params=pltpu.CompilerParams(
            collective_id=0, has_side_effects=True, vmem_limit_bytes=32 << 20
        ),
    )(table, block_cells)


SIDES = 2
NEED = 3


def swap_lanes(a, lane, step):
    size = a.shape[1]
    return jnp.where((lane & step) == 0, pltpu.roll(a, size - step, 1), pltpu.roll(a, step, 1))


def seat_tables(slots, scratch, rows, cols, my_row, my_col):
    cap = slots.shape[1]
    group = BLK_MEAN * rows
    span = 16 * rows
    lane = lax.broadcasted_iota(jnp.int32, (cols, LANES), 1)
    col = lax.broadcasted_iota(jnp.int32, (cols, LANES), 0)
    row, slot = (lane >> 4) & (rows - 1), lane & 15
    ids = jnp.full((cols, LANES), -1, jnp.int32)
    for r in range(rows):
        part = slots[r * cols : (r + 1) * cols, :]
        part = jnp.concatenate([part, jnp.full((cols, LANES - cap), -1, jnp.int32)], axis=1)
        part = jnp.where(lane < span, part, pltpu.roll(part, span, 1))
        part = pltpu.roll(part, 16 * r, 1) if r else part
        ids = jnp.where(row == r, part, ids)
    held = ids >= 0
    counts = jnp.where(held, 1, 0)
    for step in (1, 2, 4, 8):
        counts = counts + swap_lanes(counts, lane, step)
    other = swap_lanes(counts, lane, 16)
    keep = counts - (jnp.maximum(counts - other, 0) >> 1)
    crossed = slot >= keep
    at_row = jnp.where(crossed, row ^ 1, row)
    at_slot = jnp.where(crossed, other + slot - keep, slot)
    counts = keep + (jnp.maximum(other - counts, 0) >> 1)
    other = swap_lanes(counts, lane, 32)
    keep = counts - (jnp.maximum(counts - other, 0) >> 1)
    keep = jnp.where(crossed, swap_lanes(keep, lane, 16), keep)
    other = jnp.where(crossed, swap_lanes(other, lane, 16), other)
    crossed = at_slot >= keep
    at_row = jnp.where(crossed, at_row ^ 2, at_row)
    at_slot = jnp.where(crossed, other + at_slot - keep, at_slot)
    held = held & (lane < span)
    scratch[0] = jnp.where(held, ids - col * group, -100)
    scratch[1] = jnp.where(held, at_row * 16 + at_slot, -100)

    def line(kind, c, n):
        return jnp.broadcast_to(scratch[kind, pl.ds(c, 1), :], (n, LANES))

    def total(mask, value):
        return jnp.sum(jnp.where(mask, value, 0), axis=1, keepdims=True)

    def down(j):
        return jnp.where(j <= 0, j + group - 1, j - 1)

    def up(j):
        return jnp.where(j >= group - 1, j + 1 - group, j + 1)

    left, right = lax.rem(my_col + cols - 1, cols), lax.rem(my_col + 1, cols)
    n = rows * 8
    seat = lax.broadcasted_iota(jnp.int32, (n, LANES), 0)
    lane = lax.broadcasted_iota(jnp.int32, (n, LANES), 1)
    to_row, target = seat >> 3, (seat >> 3) * 16 + (seat & 7)
    j_here, f_here = line(0, my_col, n), line(1, my_col, n)
    code = lane + 64 * f_here
    on = (f_here >> 4) == to_row
    columns = [
        total(f_here == target, lane),
        total(on & ((lane >> 5) == (to_row >> 1)), 1),
        total(on & ((lane >> 4) == to_row), 1),
        total(on, 1),
    ]
    for c, moved in ((right, down), (left, up)):
        j = total(line(1, c, n) == target, line(0, c, n) + 1) - 1
        columns.append(total(j_here == j, code))
        columns.append(total(j_here == moved(j), code))
    first = jnp.zeros((n, LANES), jnp.int32)
    for at, value in enumerate(columns):
        first = jnp.where(lane == at, value, first)
    seat = lax.broadcasted_iota(jnp.int32, (8, LANES), 0)
    lane = lax.broadcasted_iota(jnp.int32, (8, LANES), 1)
    j = total(line(1, my_col, 8) == my_row * 16 + seat, line(0, my_col, 8) + 1) - 1
    second = jnp.zeros((8, LANES), jnp.int32)
    for at, (c, key) in enumerate(((left, j), (left, down(j)), (right, j), (right, up(j)))):
        value = total(line(0, c, 8) == key, lane + 64 * line(1, c, 8))
        second = jnp.where(lane == at, value, second)
    return jnp.concatenate([first, second], axis=0)


def turned(tile, shift, axis):
    shift %= tile.shape[axis]
    return pltpu.roll(tile, shift, axis) if shift else tile


def pack_face(pieces, at, unit, axis, index):
    a, b, c, d, e = pieces
    first = jnp.where(index < 3 * unit, turned(a, -at, axis), turned(b, 3 * unit - at, axis))
    first = jnp.where(index < 6 * unit, first, turned(c, 6 * unit - at, axis))
    last = jnp.where(index < 3 * unit, turned(d, -at, axis), turned(e, 3 * unit - at, axis))
    last = jnp.where(index < 6 * unit, last, turned(c, 4 * unit - at, axis))
    return first, last


def unpack_face(first, last, at, unit, axis, index):
    third = jnp.where(
        index < at + 2 * unit,
        turned(first, at - 6 * unit, axis),
        turned(last, at - 4 * unit, axis),
    )
    return (
        turned(first, at, axis),
        turned(first, at - 3 * unit, axis),
        third,
        turned(last, at, axis),
        turned(last, at - 3 * unit, axis),
    )


def section_rate(cons, edge):
    shape = cons[0].shape
    height = lax.broadcasted_iota(jnp.int32, shape, 1) & (edge - 1)
    values = cell_values(cons)
    change = None
    for normal, axis, step in ((0, 0, 1), (1, 1, edge), (2, 1, 1)):
        mid = direction_values(cons, values, normal)
        up = [pltpu.roll(m, shape[axis] - step, axis) for m in mid]
        upper = face(mid, up)
        lower = [pltpu.roll(u, step, axis) for u in upper]
        if normal == 2:
            zero = jnp.zeros_like(values[1])
            wall = [zero, zero, zero, values[1], zero]
            upper = [jnp.where(height == edge - 1, w, u) for u, w in zip(upper, wall)]
            lower = [jnp.where(height == 0, w, u) for u, w in zip(lower, wall)]
        delta = [u - l for u, l in zip(upper, lower)]
        change = delta if change is None else [t + d for t, d in zip(change, delta)]
    return [-t for t in change]


def wide_kernel(rows, cols, cap, slots, cells_in, out, *refs):
    refs = list(refs)
    take = lambda n: [refs.pop(0) for _ in range(n)]
    (cells, lines, seats, tab) = take(4)
    packed, chosen, picks = take(4), take(4), [take(4) for _ in range(4)]
    edge_packed, edge_chosen, edge_picks = take(2), take(2), [take(4) for _ in range(2)]
    (leaving, beside) = take(2)
    far_out = [take(2) for _ in range(SEND)]
    far_in = take(SEND)
    (halo, start, now) = take(3)
    (ssem, rsem, lsem) = take(3)
    edge, flat = out.shape[2:]
    parts = flat // LANES
    my_row, my_col = lax.axis_index("row"), lax.axis_index("col")
    left, right = lax.rem(my_col + cols - 1, cols), lax.rem(my_col + 1, cols)
    pair = my_row // 2
    partner = my_row + 1 - 2 * lax.rem(my_row, 2)
    is_hub = my_row == 1 + pair
    hub = 1 + pair
    served = [my_row, partner, rows - 1 - my_row, lax.rem(my_row + 2, rows)]
    toward = [right, left]

    loading = pltpu.make_async_copy(cells_in, cells, lsem.at[0])
    loading.start()
    barrier = pltpu.get_barrier_semaphore()
    for step in range(1, rows):
        device = (lax.rem(my_row + step, rows), my_col)
        pl.semaphore_signal(barrier, inc=1, device_id=device, device_id_type=MESH)
    for step in range(rows):
        for c in toward:
            device = (lax.rem(my_row + step, rows), c)
            pl.semaphore_signal(barrier, inc=1, device_id=device, device_id_type=MESH)
    seats[...] = seat_tables(slots, lines, rows, cols, my_row, my_col)
    seating = pltpu.make_async_copy(seats, tab, lsem.at[1])
    seating.start()

    def remote(src, dst, send, recv, device):
        return pltpu.make_async_remote_copy(
            src_ref=src,
            dst_ref=dst,
            send_sem=ssem.at[send],
            recv_sem=rsem.at[recv],
            device_id=device,
            device_id_type=MESH,
        )

    tile_row = lax.broadcasted_iota(jnp.int32, (8, LANES), 0)
    tile_lane = lax.broadcasted_iota(jnp.int32, (8, LANES), 1)
    tall_lane = lax.broadcasted_iota(jnp.int32, (edge, LANES), 1)
    chunks = [(kind, side) for kind in range(2) for side in range(SIDES)]

    def pack(chunk):
        kind, side = chunks[chunk]
        for k in range(cap):
            for half in range(2):
                if kind == 0:
                    at = 0 if side else 8 - NEED
                    rows_at = pl.ds(0 if side else edge - 8, 8)
                    pieces = [
                        cells[k, f, rows_at, half * LANES : (half + 1) * LANES] for f in range(5)
                    ]
                    made = pack_face(pieces, at, 1, 0, tile_row)
                else:
                    at = 0 if side else LANES - NEED * edge
                    lanes_at = pl.ds(0 if side else flat - LANES, LANES)
                    pieces = [cells[k, f, half * 8 : (half + 1) * 8, lanes_at] for f in range(5)]
                    made = pack_face(pieces, at, edge, 1, tile_lane)
                for which in range(2):
                    packed[chunk][1, k, half * 2 + which] = made[which]

    gathers = [
        remote(packed[c].at[1], packed[c].at[0], c, c, (partner, my_col)) for c in range(4)
    ]
    sends = [
        [
            remote(
                picks[c][rel],
                chosen[c].at[rel // 2],
                4 + 4 * c + rel,
                4 + 2 * c + rel // 2,
                (served[rel], toward[chunks[c][1]]),
            )
            for rel in range(4)
        ]
        for c in range(4)
    ]
    swap = remote(leaving, beside, 20, 12, (partner, my_col))
    edge_gathers = [
        remote(edge_packed[i].at[1], edge_packed[i].at[0], 21 + i, 13 + i, (partner, my_col))
        for i in range(2)
    ]
    edge_sends = [
        [
            remote(
                edge_picks[i][rel],
                edge_chosen[i].at[rel // 2],
                23 + 4 * i + rel,
                15 + 2 * i + rel // 2,
                (served[rel], toward[i]),
            )
            for rel in range(4)
        ]
        for i in range(2)
    ]
    crossings = [
        [
            remote(far_out[i][e], far_in[i], 31 + 2 * i + e, 19 + i, (served[2 + e], my_col))
            for e in range(2)
        ]
        for i in range(SEND)
    ]

    def on_hub(do):
        pl.when(is_hub)(do)

    def on_edge(do):
        pl.when(jnp.logical_not(is_hub))(do)

    loading.wait()
    pack(0)
    pl.semaphore_wait(barrier, 3 * rows - 1)
    on_edge(gathers[0].start)
    for c in range(1, 4):
        pack(c)
        on_edge(gathers[c].start)

    seating.wait()

    def entry(row, slot, column):
        return tab[row * 8 + slot, column]

    def origin(row, slot):
        code = entry(row, slot, 0)
        return code >> 4, code & 15

    my_stay = entry(my_row, 0, 2)
    near_stay = entry(partner, 0, 2)
    my_base = entry(my_row, 0, 1)
    for i in range(SEND):
        leaving[i] = cells[jnp.minimum(my_stay + i, cap - 1)]
    swap.start()

    def seat_of(place):
        return jnp.where((place >> 4) == hub, 1, 0), jnp.minimum(place & 15, cap - 1)

    def choose(c):
        kind, side = chunks[c]
        gathers[c].wait_recv()
        for rel in (2, 3, 1, 0):
            for s in range(OUT):
                q, k = seat_of(entry(served[rel], s, 4 + 2 * side + kind) & 63)
                picks[c][rel][s] = packed[c][q, k]
            sends[c][rel].start()

    @pl.when(is_hub)
    def _():
        for c in range(4):
            choose(c)

    def whose(slot, column, shift):
        code = (tab[rows * 8 + slot, column] >> shift) & 63
        return jnp.where((code >> 5) == pair, 0, 1)

    def await_chunk(c):
        for far in range(2):
            sends[c][2 * far].wait_recv()

    await_chunk(0)
    await_chunk(1)
    corner_group = tile_lane >> 4
    for s in range(OUT):
        low, high = whose(s, 0, 0), whose(s, 2, 0)
        tiles = []
        for half in range(2):
            got = []
            for c, far, at in ((0, low, 8 - NEED), (1, high, 0)):
                first, last = chosen[c][far, s, half * 2], chosen[c][far, s, half * 2 + 1]
                got.append(unpack_face(first, last, at, 1, 0, tile_row))
            tiles.append([jnp.where(tile_row >= 4, a, b) for a, b in zip(*got)])
            for f in range(5):
                halo[s, f, half] = tiles[half][f]
        for side in range(SIDES):
            source = tiles[0] if side else tiles[parts - 1]
            made = jnp.zeros((8, LANES), jnp.float32)
            for f in range(5):
                one = 0 if side else LANES - edge
                two = edge if side else LANES - 2 * edge
                inner = (tile_row == 3) | (tile_row == 4)
                tile = jnp.where(
                    inner,
                    turned(turned(source[f], 4, 0), edge * f - two, 1),
                    turned(source[f], edge * f - one, 1),
                )
                made = jnp.where(corner_group == f, tile, made)
            edge_packed[side][1, s] = made
    for side in range(SIDES):
        on_edge(edge_gathers[side].start)

    def choose_corner(side):
        edge_gathers[side].wait_recv()
        for rel in (2, 3, 1, 0):
            for s in range(OUT):
                place = (entry(served[rel], s, 5 + 2 * side) >> 6) & 63
                q, k = seat_of(place)
                edge_picks[side][rel][s] = edge_packed[side][q, jnp.minimum(k, OUT - 1)]
            edge_sends[side][rel].start()

    @pl.when(is_hub)
    def _():
        for side in range(SIDES):
            choose_corner(side)

    swap.wait_recv()

    @pl.when(is_hub)
    def _():
        for i in range(SEND):
            for e in range(2):
                row = served[2 + e]
                slot = jnp.minimum(entry(row, 0, 1) + i, 7)
                at_row, k = origin(row, slot)
                mine = cells[jnp.minimum(k, cap - 1)]
                near = beside[jnp.clip(k - near_stay, 0, SEND - 1)]
                far_out[i][e][...] = jnp.where(at_row == my_row, mine, near)
                crossings[i][e].start()

    await_chunk(2)
    await_chunk(3)
    for side in range(SIDES):
        for far in range(2):
            edge_sends[side][2 * far].wait_recv()

    filled = entry(my_row, 0, 3)

    def run(s, carry):
        at_row, k = origin(my_row, s)
        mine = cells[jnp.minimum(k, cap - 1)]
        near = beside[jnp.clip(k - near_stay, 0, SEND - 1)]
        now[:, :edge, :flat] = jnp.where(at_row == my_row, mine, near)
        for i in range(SEND):

            @pl.when(s == i + 1)
            def _():
                crossings[i][0].wait_recv()

            @pl.when(s > i)
            def _():
                here = now[:, :edge, :flat]
                now[:, :edge, :flat] = jnp.where(s - my_base == i, far_in[i][...], here)

        for f in range(5):
            for half in range(2):
                now[f, edge:, half * LANES : (half + 1) * LANES] = halo[s, f, half]
        low, high = whose(s, 1, 0), whose(s, 3, 0)
        for half in range(2):
            got = []
            for c, far, at in ((2, low, LANES - NEED * edge), (3, high, 0)):
                first, last = chosen[c][far, s, half * 2], chosen[c][far, s, half * 2 + 1]
                got.append(unpack_face(first, last, at, edge, 1, tile_lane))
            for f in range(5):
                now[f, half * 8 : (half + 1) * 8, flat:] = jnp.where(
                    tile_lane >= LANES // 2, got[0][f], got[1][f]
                )
        low = edge_chosen[0][whose(s, 1, 6), s]
        high = edge_chosen[1][whose(s, 3, 6), s]
        for f in range(5):
            a = turned(low, LANES - edge - edge * f, 1)
            b = turned(turned(low, 4, 0), LANES - 2 * edge - edge * f, 1)
            c = turned(high, -edge * f, 1)
            d = turned(turned(high, 4, 0), edge - edge * f, 1)
            tile = jnp.where(tile_lane < edge, c, d)
            tile = jnp.where(tile_lane >= LANES // 2, b, tile)
            now[f, edge:, flat:] = jnp.where(tile_lane >= LANES - edge, a, tile)
        for f, field in enumerate(conserved([now[f] for f in range(5)])):
            start[f] = field
            now[f] = field
        for step in range(3):
            cons = tuple(now[f] for f in range(5))
            rate = section_rate(cons, edge)
            moved = [c + DT * d for c, d in zip(cons, rate)]
            if step == 1:
                moved = [0.75 * start[f] + 0.25 * moved[f] for f in range(5)]
            if step == 2:
                moved = [m[:edge, :flat] for m in moved]
                moved = [
                    (1.0 / 3.0) * start[f, :edge, :flat] + (2.0 / 3.0) * moved[f] for f in range(5)
                ]
                rho = moved[0]
                vel = [m / rho for m in moved[1:4]]
                p = 0.4 * (
                    moved[4] - 0.5 * rho * (vel[0] * vel[0] + vel[1] * vel[1] + vel[2] * vel[2])
                )
                for f, field in enumerate((rho, *vel, p)):
                    out[s, f] = jnp.where(s < filled, field, 0.0)
            else:
                for f in range(5):
                    now[f] = moved[f]
        return carry

    lax.fori_loop(0, OUT, run, 0)
    swap.wait_send()

    @pl.when(is_hub)
    def _():
        for group in (*sends, *edge_sends, *crossings):
            for flight in group:
                flight.wait_send()

    @pl.when(jnp.logical_not(is_hub))
    def _():
        for flight in (*gathers, *edge_gathers):
            flight.wait_send()


def wide_body(rows, cols, block_cells, slot_blocks):
    cap = slot_blocks.shape[1]
    edge, flat = block_cells.shape[2:]
    block = (5, edge, flat)
    f32 = lambda *shape: pltpu.VMEM(shape, jnp.float32)
    face_tiles = (4, 8, LANES)
    grown = (5, edge + 8, flat + LANES)
    scratch = [f32(cap, *block), pltpu.VMEM((2, cols, LANES), jnp.int32)]
    scratch += [space((rows * 8 + 8, LANES), jnp.int32) for space in (pltpu.VMEM, pltpu.SMEM)]
    scratch += [f32(2, cap, *face_tiles) for _ in range(4)]
    scratch += [f32(2, OUT, *face_tiles) for _ in range(4)]
    scratch += [f32(OUT, *face_tiles) for _ in range(16)]
    scratch += [f32(2, OUT, 8, LANES) for _ in range(4)]
    scratch += [f32(OUT, 8, LANES) for _ in range(8)]
    scratch += [f32(SEND, *block) for _ in range(2)]
    scratch += [f32(*block) for _ in range(3 * SEND)]
    scratch += [f32(OUT, 5, 2, 8, LANES), f32(*grown), f32(*grown)]
    scratch += [pltpu.SemaphoreType.DMA((n,)) for n in (41, 24, 2)]
    return pl.pallas_call(
        functools.partial(wide_kernel, rows, cols, cap),
        out_shape=jax.ShapeDtypeStruct((OUT, *block), jnp.float32),
        in_specs=[
            pl.BlockSpec(memory_space=pltpu.VMEM),
            pl.BlockSpec(memory_space=pl.ANY),
        ],
        out_specs=pl.BlockSpec(memory_space=pltpu.VMEM),
        scratch_shapes=scratch,
        compiler_params=pltpu.CompilerParams(
            collective_id=0, has_side_effects=True, vmem_limit_bytes=40 << 20
        ),
    )(slot_blocks, block_cells)


def solution(mesh):
    rows, cols = mesh.shape["row"], mesh.shape["col"]
    local = wide_body if (rows, cols) == (4, 8) else body
    return jax.shard_map(
        functools.partial(local, rows, cols),
        mesh=mesh,
        in_specs=(P(("row", "col"), None, None, None), P()),
        out_specs=P(("row", "col"), None, None, None),
        check_vma=False,
    )
```

```python
import functools

import jax
import jax.numpy as jnp
from jax import lax
from jax.experimental import pallas as pl
from jax.experimental.pallas import tpu as pltpu
from jax.sharding import PartitionSpec as P

MESH = pl.DeviceIdType.MESH
BLK_MEAN = 6
OUT = 7
SEND = BLK_MEAN - 1
LANES = 128
DT = 0.12


def make_tables(slot_blocks, rows, cols, my_row, my_col):
    cap = slot_blocks.shape[1]
    levels = rows.bit_length() - 1
    half = rows // 2
    group = BLK_MEAN * rows
    ids = slot_blocks.reshape(rows, cols, cap)
    counts = jnp.sum((ids >= 0).astype(jnp.int32), axis=2)
    row_ids = jnp.arange(rows, dtype=jnp.int32)
    col_ids = jnp.arange(cols, dtype=jnp.int32)
    at_row = jnp.broadcast_to(row_ids[:, None, None], ids.shape)
    at_slot = jnp.broadcast_to(jnp.arange(cap, dtype=jnp.int32), ids.shape)
    mine = (row_ids[:, None] == my_row) & (col_ids[None, :] == my_col)
    scalars = []
    for level in range(levels):
        bit = 1 << level
        other = counts.reshape(rows // (2 * bit), 2, bit, cols)[:, ::-1].reshape(rows, cols)
        send = jnp.maximum(counts - other, 0) // 2
        take = jnp.maximum(other - counts, 0) // 2
        keep = counts - send
        scalars.append(jnp.sum(jnp.where(mine, keep, 0)))
        hit = at_row[None] == row_ids[:, None, None, None]
        keep_here = jnp.sum(jnp.where(hit, keep[:, None, :, None], 0), axis=0)
        other_here = jnp.sum(jnp.where(hit, other[:, None, :, None], 0), axis=0)
        moved = at_slot >= keep_here
        at_row = jnp.where(moved, at_row ^ bit, at_row)
        at_slot = jnp.where(moved, other_here + at_slot - keep_here, at_slot)
        counts = keep + take
    scalars.append(jnp.sum(jnp.where(mine, counts, 0)))
    place = at_row * 16 + at_slot
    origin = row_ids[:, None, None] * 16 + jnp.arange(cap, dtype=jnp.int32)
    origin = jnp.broadcast_to(origin, ids.shape).reshape(-1)
    flat_ids = ids.reshape(-1)
    flat_place = jnp.where(flat_ids >= 0, place.reshape(-1), 0)
    flat_col = jnp.broadcast_to(col_ids[None, :, None], ids.shape).reshape(-1)
    near_far = jnp.stack([my_row, my_row ^ half])
    left, right = (my_col + cols - 1) % cols, (my_col + 1) % cols
    seat_rows = jnp.concatenate([near_far[:1], near_far, near_far])
    seat_cols = jnp.stack([my_col, right, right, left, left])
    seats = (seat_rows[:, None] * 16 + jnp.arange(OUT, dtype=jnp.int32)).reshape(-1, 1)
    seat_cols = jnp.repeat(seat_cols, OUT)[:, None]
    match = (flat_place[None] == seats) & (flat_col[None] == seat_cols) & (flat_ids >= 0)[None]
    along = jnp.sum(jnp.where(match, flat_ids[None] - flat_col[None] * group, 0), axis=1)
    along = along.reshape(5, OUT)
    here, there_right, there_left = along[:1], along[1:3], along[3:5]
    down, up = (lambda a: (a + group - 1) % group), (lambda a: (a + 1) % group)
    mine = jnp.concatenate([left * group + here, left * group + down(here)])
    mine = jnp.concatenate([mine, right * group + here, right * group + up(here)])
    theirs = jnp.concatenate([there_right, down(there_right), there_left, up(there_left)])
    wanted = jnp.concatenate([mine, theirs + my_col * group]).reshape(-1)
    both = flat_place * 4096 + origin
    found = jnp.sum(jnp.where(flat_ids[None] == wanted[:, None], both[None], 0), axis=1)
    source = found ^ (my_row * 16 * 4097)
    source = jnp.concatenate([source & 4095, source >> 12])
    return jnp.concatenate([jnp.stack(scalars), source])


def cell_values(cons):
    rho, mx, my, mz, energy = cons
    inv = 1.0 / rho
    vel = (mx * inv, my * inv, mz * inv)
    p = 0.4 * (energy - 0.5 * rho * (vel[0] * vel[0] + vel[1] * vel[1] + vel[2] * vel[2]))
    theta = p * inv
    sound = jnp.sqrt(1.4 * theta)
    kappa = 0.2 * jnp.exp(0.7 * jnp.log(theta))
    return vel, p, theta, sound, kappa


def conserved(primitive):
    rho, u, v, w, p = primitive
    energy = p / 0.4 + 0.5 * rho * (u * u + v * v + w * w)
    return (rho, rho * u, rho * v, rho * w, energy)


def direction_values(cons, values, normal):
    vel, p, theta, sound, kappa = values
    un = vel[normal]
    flux = [cons[1 + normal], cons[1] * un, cons[2] * un, cons[3] * un, (cons[4] + p) * un]
    flux[1 + normal] = flux[1 + normal] + p
    return (*cons, *flux, jnp.abs(un) + sound, theta, kappa)


def face(low, high):
    half_speed = 0.5 * jnp.maximum(low[10], high[10])
    out = [0.5 * (low[5 + i] + high[5 + i]) - half_speed * (high[i] - low[i]) for i in range(5)]
    out[4] = out[4] - 0.5 * (low[12] + high[12]) * (high[11] - low[11])
    return out


def block_rate(cons, ghost_x, ghost_y):
    edge, flat = cons[0].shape
    row = lax.broadcasted_iota(jnp.int32, (edge, flat), 0)
    lane = lax.broadcasted_iota(jnp.int32, (edge, flat), 1)
    values = cell_values(cons)
    mid = direction_values(cons, values, 0)
    gx = direction_values(ghost_x, cell_values(ghost_x), 0)
    last = row == edge - 1
    up = [
        jnp.where(last, jnp.concatenate([g, g], axis=0), pltpu.roll(m, edge - 1, 0))
        for m, g in zip(mid, gx)
    ]
    upper = face(mid, up)
    bottom = face(gx, [m[:8] for m in mid])
    change = [
        u - jnp.where(row == 0, jnp.concatenate([b, b], axis=0), pltpu.roll(u, 1, 0))
        for u, b in zip(upper, bottom)
    ]
    mid = direction_values(cons, values, 1)
    gy = direction_values(ghost_y, cell_values(ghost_y), 1)
    last = lane >= flat - edge
    up = [
        jnp.where(last, jnp.concatenate([g, g], axis=1), pltpu.roll(m, flat - edge, 1))
        for m, g in zip(mid, gy)
    ]
    upper = face(mid, up)
    bottom = face(gy, [m[:, :LANES] for m in mid])
    change = [
        t + (u - jnp.where(lane < edge, jnp.concatenate([b, b], axis=1), pltpu.roll(u, edge, 1)))
        for t, u, b in zip(change, upper, bottom)
    ]
    mid = direction_values(cons, values, 2)
    up = [pltpu.roll(m, flat - 1, 1) for m in mid]
    upper = face(mid, up)
    height = lane & (edge - 1)
    zero = jnp.zeros_like(values[1])
    wall = [zero, zero, zero, values[1], zero]
    change = [
        t
        + (
            jnp.where(height == edge - 1, w, u)
            - jnp.where(height == 0, w, pltpu.roll(u, 1, 1))
        )
        for t, u, w in zip(change, upper, wall)
    ]
    return [-t for t in change]


def y_units(n):
    return 2 * ((5 * n + 7) // 8)


def units(n):
    return y_units(n) + (10 * n + 7) // 8


def y_seat(slot, f):
    at = slot * 5 + f
    return 2 * (at >> 3), 16 * (at & 7)


def x_seat(n, slot, f, part):
    at = slot * 10 + 2 * f + part
    return y_units(n) + (at >> 3), at & 7


def kernel(rows, cols, cap, *refs):
    levels = rows.bit_length() - 1
    half = rows // 2
    refs = list(refs)
    tab, cells, out = refs[:3]
    refs = refs[3:]
    send_blocks = refs[:levels]
    recv_blocks = refs[levels : 2 * levels]
    refs = refs[2 * levels :]
    start, now = refs[:2]
    sections = [refs[2 + 10 * i : 12 + 10 * i] for i in range(3)]
    bsend, brecv, hsend, hrecv = refs[32:36]
    my_row, my_col = lax.axis_index("row"), lax.axis_index("col")
    left = (my_row, lax.rem(my_col + cols - 1, cols))
    right = (my_row, lax.rem(my_col + 1, cols))

    def partner(level):
        bit = 1 << level
        return (my_row + bit - 2 * bit * (lax.rem(my_row // bit, 2)), my_col)

    barrier = pltpu.get_barrier_semaphore()
    across = partner(levels - 1)[0]
    beside = [(right, left), ((across, right[1]), (across, left[1]))]
    for device in [*beside[0], *beside[1]] + [partner(level) for level in range(levels)]:
        pl.semaphore_signal(barrier, inc=1, device_id=device, device_id_type=MESH)
    pl.semaphore_wait(barrier, 4 + levels)

    def held(slot, depth):
        value = cells[jnp.minimum(slot, cap - 1)]
        for level in range(depth):
            keep = tab[level]
            got = recv_blocks[level][jnp.clip(slot - keep, 0, SEND - 1)]
            value = jnp.where(slot >= keep, got, value)
        return value

    edge, flat = now.shape[2:]
    tile_lane = lax.broadcasted_iota(jnp.int32, (edge, LANES), 1)
    tile_group = tile_lane >> 4
    ghost_row = lax.broadcasted_iota(jnp.int32, (8, 2 * LANES), 0)

    def tile_of(ref, *seat):
        *lead, unit = seat
        return ref[(*lead, pl.ds(unit, 2))].reshape(edge, LANES)

    def put_tile(ref, unit, tile):
        ref[unit : unit + 2] = tile.reshape(2, 8, LANES)

    def move_blocks(level):
        for k in range(SEND):
            send_blocks[level][k] = held(tab[level] + k, level)
        copy = pltpu.make_async_remote_copy(
            src_ref=send_blocks[level],
            dst_ref=recv_blocks[level],
            send_sem=bsend.at[level],
            recv_sem=brecv.at[level],
            device_id=partner(level),
            device_id_type=MESH,
        )
        copy.start()
        return copy

    def remote(step, at, src, dst, device):
        copy = pltpu.make_async_remote_copy(
            src_ref=src,
            dst_ref=dst,
            send_sem=hsend.at[step, at],
            recv_sem=hrecv.at[step, at],
            device_id=device,
            device_id_type=MESH,
        )
        copy.start()
        return copy

    def pack(blocks, n, buffer, high):
        x = edge - 1 if high else 0
        side = slice(LANES, 2 * LANES) if high else slice(0, LANES)
        for first in range(0, 5 * n, 8):
            tile = None
            for at in range(first, min(first + 8, 5 * n)):
                s, f = at // 5, at % 5
                shift = (edge * (at - first) + (edge if high else 0)) % LANES
                piece = blocks[s, f, :, side]
                piece = pltpu.roll(piece, shift, 1) if shift else piece
                tile = piece if tile is None else jnp.where(tile_group == at - first, piece, tile)
            put_tile(buffer, 2 * (first // 8), tile)
        for s in range(n):
            for f in range(5):
                for part in range(2):
                    unit, row = x_seat(n, s, f, part)
                    buffer[unit, row : row + 1, :] = blocks[
                        s, f, x : x + 1, part * LANES : (part + 1) * LANES
                    ]

    base = levels + 1

    def entry(step, kind, far, slot):
        at = kind * OUT if far is None else 4 * OUT + (kind * 2 + far) * OUT
        return tab[base + (12 * OUT if step else 0) + at + slot]

    def near_seat(code):
        return jnp.minimum(code >> 4, half - 1), code & 15

    def select(step, n, known, pick, first_kind, far):
        for s in range(OUT):
            q, sigma = near_seat(entry(step, first_kind, far, s))
            for f in range(5):
                for part in range(2):
                    unit, row = x_seat(n, sigma, f, part)
                    to, at = x_seat(OUT, s, f, part)
                    pick[to, at : at + 1, :] = known[q, unit, pl.ds(row, 1), :]
        seats = [near_seat(entry(step, first_kind + 1, far, s)) for s in range(OUT)]
        for first in range(0, 5 * OUT, 8):
            tile = None
            for at in range(first, min(first + 8, 5 * OUT)):
                q, sigma = seats[at // 5]
                unit, lane = y_seat(sigma, at % 5)
                shift = (edge * (at - first) + LANES - lane) & (LANES - 1)
                piece = pltpu.roll(tile_of(known, q, unit), shift, 1)
                tile = piece if tile is None else jnp.where(tile_group == at - first, piece, tile)
            put_tile(pick, 2 * (first // 8), tile)

    def begin(step, blocks, n):
        flights = []
        for side in range(2):
            known = sections[step][side]
            pack(blocks, n, known.at[0], side == 0)
            if levels > 1:
                flights.append(remote(step, side, known.at[0], known.at[1], partner(0)))
        return flights

    def gather(step, flights):
        for level in range(1, levels - 1):
            size = 1 << level
            for side in range(2):
                known = sections[step][side]
                flights[side].wait()
                flights[side] = remote(
                    step,
                    2 * level + side,
                    known.at[pl.ds(0, size)],
                    known.at[pl.ds(size, size)],
                    partner(level),
                )
        return flights

    def trade(step, n, flights):
        sent = []
        for side in range(2):
            if flights:
                flights[side].wait()
            for far in (1, 0):
                known, pick, sel = (sections[step][at] for at in (side, 2 + 2 * side + far, 6 + 2 * side + far))
                select(step, n, known, pick, 2 * side, far)
                at = 2 * (levels - 1) + 2 * side + far
                sent.append(remote(step, at, pick, sel, beside[far][side]))
        return sent

    def open_block(slot, carry):
        value = held(slot, levels)
        for f, field in enumerate(conserved([value[f] for f in range(5)])):
            start[slot, f] = field
            now[slot, f] = field
        return carry

    def advance(step):
        lo_near, lo_far, hi_near, hi_far = sections[step][6:]

        def run(slot, carry):
            def near(kind):
                return entry(step, kind, None, slot) < 16 * half

            def x_row(close, away, kind, f):
                parts = []
                for part in range(2):
                    unit, row = x_seat(OUT, slot, f, part)
                    a = close[unit, pl.ds(row, 1), :]
                    b = away[unit, pl.ds(row, 1), :]
                    parts.append(jnp.where(near(kind), a, b))
                return jnp.concatenate(parts, axis=1)

            def y_tile(close, away, kind, f, to):
                unit, lane = y_seat(slot, f)
                tile = jnp.where(near(kind), tile_of(close, unit), tile_of(away, unit))
                return pltpu.roll(tile, (LANES + to - lane) & (LANES - 1), 1)

            ghost_x, ghost_y = [], []
            for f in range(5):
                low = x_row(lo_near, lo_far, 0, f)
                high = x_row(hi_near, hi_far, 2, f)
                ghost_x.append(jnp.where(ghost_row == 0, low, high))
                low = y_tile(lo_near, lo_far, 1, f, 0)
                high = y_tile(hi_near, hi_far, 3, f, LANES - edge)
                ghost_y.append(jnp.where(tile_lane < edge, low, high))
            if step == 0:
                ghost_x, ghost_y = conserved(ghost_x), conserved(ghost_y)
            cons = tuple(now[slot, f] for f in range(5))
            rate = block_rate(cons, tuple(ghost_x), tuple(ghost_y))
            moved = [c + DT * d for c, d in zip(cons, rate)]
            if step == 1:
                moved = [0.75 * start[slot, f] + 0.25 * moved[f] for f in range(5)]
            if step == 2:
                moved = [(1.0 / 3.0) * start[slot, f] + (2.0 / 3.0) * moved[f] for f in range(5)]
                rho = moved[0]
                vel = [m / rho for m in moved[1:4]]
                p = 0.4 * (
                    moved[4] - 0.5 * rho * (vel[0] * vel[0] + vel[1] * vel[1] + vel[2] * vel[2])
                )
                filled = slot < tab[levels]
                for f, field in enumerate((rho, *vel, p)):
                    out[slot, f] = jnp.where(filled, field, 0.0)
            else:
                for f in range(5):
                    now[slot, f] = moved[f]
            return carry

        lax.fori_loop(0, OUT, run, 0)

    moving = move_blocks(0)
    flights = begin(0, cells, cap)
    flights = gather(0, flights)
    for level in range(1, levels):
        moving.wait()
        moving = move_blocks(level)
    flights = trade(0, cap, flights)
    moving.wait()
    lax.fori_loop(0, OUT, open_block, 0)
    for step in range(3):
        if step:
            flights = trade(step, OUT, gather(step, begin(step, now, OUT)))
        for flight in flights:
            flight.wait()
        advance(step)


def body(rows, cols, block_cells, slot_blocks):
    cap = slot_blocks.shape[1]
    levels = rows.bit_length() - 1
    half = rows // 2
    edge, flat = block_cells.shape[2:]
    table = make_tables(slot_blocks, rows, cols, lax.axis_index("row"), lax.axis_index("col"))
    block = (5, edge, flat)
    scratch = [pltpu.VMEM((SEND, *block), jnp.float32) for _ in range(2 * levels)]
    scratch += [pltpu.VMEM((OUT, *block), jnp.float32) for _ in range(2)]
    for step in range(3):
        faces = (units(OUT if step else cap), 8, LANES)
        picked = (units(OUT), 8, LANES)
        scratch += [pltpu.VMEM((half, *faces), jnp.float32) for _ in range(2)]
        scratch += [pltpu.VMEM(picked, jnp.float32) for _ in range(8)]
    scratch += [pltpu.SemaphoreType.DMA((levels,)) for _ in range(2)]
    scratch += [pltpu.SemaphoreType.DMA((3, 2 * (levels + 1))) for _ in range(2)]
    return pl.pallas_call(
        functools.partial(kernel, rows, cols, cap),
        out_shape=jax.ShapeDtypeStruct((OUT, *block), jnp.float32),
        in_specs=[
            pl.BlockSpec(memory_space=pltpu.SMEM),
            pl.BlockSpec(memory_space=pltpu.VMEM),
        ],
        out_specs=pl.BlockSpec(memory_space=pltpu.VMEM),
        scratch_shapes=scratch,
        compiler_params=pltpu.CompilerParams(
            collective_id=0, has_side_effects=True, vmem_limit_bytes=32 << 20
        ),
    )(table, block_cells)


SIDES = 2
NEED = 3
PARTS = 8
LAG = 4
FORWARD = 2
LATE = 3
RELAY = 4


def swap_lanes(a, lane, step):
    size = a.shape[1]
    return jnp.where((lane & step) == 0, pltpu.roll(a, size - step, 1), pltpu.roll(a, step, 1))


def seat_tables(slots, scratch, rows, cols, my_row, my_col):
    cap, devices = slots.shape
    slots = jnp.concatenate([slots, jnp.zeros((16 - cap, devices), jnp.int32)], axis=0)
    slots = jnp.concatenate([slots, jnp.zeros((16, LANES - devices), jnp.int32)], axis=1)
    slots = jnp.transpose(slots)[:devices, :cap]
    group = BLK_MEAN * rows
    span = 16 * rows
    lane = lax.broadcasted_iota(jnp.int32, (cols, LANES), 1)
    col = lax.broadcasted_iota(jnp.int32, (cols, LANES), 0)
    row, slot = (lane >> 4) & (rows - 1), lane & 15
    ids = jnp.full((cols, LANES), -1, jnp.int32)
    for r in range(rows):
        part = slots[r * cols : (r + 1) * cols, :]
        part = jnp.concatenate([part, jnp.full((cols, LANES - cap), -1, jnp.int32)], axis=1)
        part = jnp.where(lane < span, part, pltpu.roll(part, span, 1))
        part = pltpu.roll(part, 16 * r, 1) if r else part
        ids = jnp.where(row == r, part, ids)
    held = ids >= 0
    counts = jnp.where(held, 1, 0)
    for step in (1, 2, 4, 8):
        counts = counts + swap_lanes(counts, lane, step)
    other = swap_lanes(counts, lane, 16)
    keep = counts - (jnp.maximum(counts - other, 0) >> 1)
    crossed = slot >= keep
    at_row = jnp.where(crossed, row ^ 1, row)
    at_slot = jnp.where(crossed, other + slot - keep, slot)
    counts = keep + (jnp.maximum(other - counts, 0) >> 1)
    other = swap_lanes(counts, lane, 32)
    keep = counts - (jnp.maximum(counts - other, 0) >> 1)
    keep = jnp.where(crossed, swap_lanes(keep, lane, 16), keep)
    other = jnp.where(crossed, swap_lanes(other, lane, 16), other)
    crossed = at_slot >= keep
    at_row = jnp.where(crossed, at_row ^ 2, at_row)
    at_slot = jnp.where(crossed, other + at_slot - keep, at_slot)
    held = held & (lane < span)
    scratch[0] = jnp.where(held, ids - col * group, -100)
    scratch[1] = jnp.where(held, at_row * 16 + at_slot, -100)

    def line(kind, c, n):
        return jnp.broadcast_to(scratch[kind, pl.ds(c, 1), :], (n, LANES))

    def total(mask, value):
        return jnp.sum(jnp.where(mask, value, 0), axis=1, keepdims=True)

    def down(j):
        return jnp.where(j <= 0, j + group - 1, j - 1)

    def up(j):
        return jnp.where(j >= group - 1, j + 1 - group, j + 1)

    left, right = lax.rem(my_col + cols - 1, cols), lax.rem(my_col + 1, cols)
    n = rows * 8
    seat = lax.broadcasted_iota(jnp.int32, (n, LANES), 0)
    lane = lax.broadcasted_iota(jnp.int32, (n, LANES), 1)
    to_row, target = seat >> 3, (seat >> 3) * 16 + (seat & 7)
    j_here, f_here = line(0, my_col, n), line(1, my_col, n)
    code = lane + 64 * f_here
    on = (f_here >> 4) == to_row
    columns = [
        total(f_here == target, lane),
        total(on & ((lane >> 5) == (to_row >> 1)), 1),
        total(on & ((lane >> 4) == to_row), 1),
        total(on, 1),
    ]
    for c, moved in ((right, down), (left, up)):
        j = total(line(1, c, n) == target, line(0, c, n) + 1) - 1
        columns.append(total(j_here == j, code))
        columns.append(total(j_here == moved(j), code))
    columns.append(total(on & ((lane >> 4) == rows - 1 - to_row), 1))
    first = jnp.zeros((n, LANES), jnp.int32)
    for at, value in enumerate(columns):
        first = jnp.where(lane == at, value, first)
    seat = lax.broadcasted_iota(jnp.int32, (8, LANES), 0)
    lane = lax.broadcasted_iota(jnp.int32, (8, LANES), 1)
    j = total(line(1, my_col, 8) == my_row * 16 + seat, line(0, my_col, 8) + 1) - 1
    second = jnp.zeros((8, LANES), jnp.int32)
    for at, (c, key) in enumerate(((left, j), (left, down(j)), (right, j), (right, up(j)))):
        value = total(line(0, c, 8) == key, lane + 64 * line(1, c, 8))
        second = jnp.where(lane == at, value, second)
    return jnp.concatenate([first, second], axis=0)


def turned(tile, shift, axis):
    shift %= tile.shape[axis]
    return pltpu.roll(tile, shift, axis) if shift else tile


def pack_face(pieces, at, unit, axis, index):
    a, b, c, d, e = pieces
    first = jnp.where(index < 3 * unit, turned(a, -at, axis), turned(b, 3 * unit - at, axis))
    first = jnp.where(index < 6 * unit, first, turned(c, 6 * unit - at, axis))
    last = jnp.where(index < 3 * unit, turned(d, -at, axis), turned(e, 3 * unit - at, axis))
    last = jnp.where(index < 6 * unit, last, turned(c, 4 * unit - at, axis))
    return first, last


def unpack_face(first, last, at, unit, axis, index):
    third = jnp.where(
        index < at + 2 * unit,
        turned(first, at - 6 * unit, axis),
        turned(last, at - 4 * unit, axis),
    )
    return (
        turned(first, at, axis),
        turned(first, at - 3 * unit, axis),
        third,
        turned(last, at, axis),
        turned(last, at - 3 * unit, axis),
    )


def section_rate(cons, edge):
    shape = cons[0].shape
    height = lax.broadcasted_iota(jnp.int32, shape, 1) & (edge - 1)
    values = cell_values(cons)
    change = None
    for normal, axis, step in ((0, 0, 1), (1, 1, edge), (2, 1, 1)):
        mid = direction_values(cons, values, normal)
        up = [pltpu.roll(m, shape[axis] - step, axis) for m in mid]
        upper = face(mid, up)
        lower = [pltpu.roll(u, step, axis) for u in upper]
        if normal == 2:
            zero = jnp.zeros_like(values[1])
            wall = [zero, zero, zero, values[1], zero]
            upper = [jnp.where(height == edge - 1, w, u) for u, w in zip(upper, wall)]
            lower = [jnp.where(height == 0, w, u) for u, w in zip(lower, wall)]
        delta = [u - l for u, l in zip(upper, lower)]
        change = delta if change is None else [t + d for t, d in zip(change, delta)]
    return [-t for t in change]


def wide_kernel(rows, cols, cap, slots, cells, out, *refs):
    refs = list(refs)
    take = lambda n: [refs.pop(0) for _ in range(n)]
    (lines, seats, tab) = take(3)
    packed, chosen, picks = take(PARTS), take(PARTS), [take(4) for _ in range(PARTS)]
    merged = take(PARTS)
    edge_packed, edge_chosen, edge_picks = take(2), take(2), [take(4) for _ in range(2)]
    (leaving, beside, across) = take(3)
    far_out, far_in = take(SEND), take(SEND)
    (halo, start, now) = take(3)
    (ssem, rsem, lsem) = take(3)
    edge, flat = out.shape[2:]
    parts = flat // LANES
    my_row, my_col = lax.axis_index("row"), lax.axis_index("col")
    left, right = lax.rem(my_col + cols - 1, cols), lax.rem(my_col + 1, cols)
    pair = my_row // 2
    partner = my_row + 1 - 2 * lax.rem(my_row, 2)
    is_hub = my_row == 1 + pair
    hub = 1 + pair
    served = [my_row, partner, rows - 1 - my_row, lax.rem(my_row + 2, rows)]
    toward = [right, left]

    barrier = pltpu.get_barrier_semaphore()
    for step in range(1, rows):
        device = (lax.rem(my_row + step, rows), my_col)
        pl.semaphore_signal(barrier, inc=1, device_id=device, device_id_type=MESH)
    for step in range(rows):
        for c in toward:
            device = (lax.rem(my_row + step, rows), c)
            pl.semaphore_signal(barrier, inc=1, device_id=device, device_id_type=MESH)
    seats[...] = seat_tables(slots[...], lines, rows, cols, my_row, my_col)
    seating = pltpu.make_async_copy(seats, tab, lsem.at[0])
    seating.start()

    def remote(src, dst, send, recv, device):
        return pltpu.make_async_remote_copy(
            src_ref=src,
            dst_ref=dst,
            send_sem=ssem.at[send],
            recv_sem=rsem.at[recv],
            device_id=device,
            device_id_type=MESH,
        )

    tile_row = lax.broadcasted_iota(jnp.int32, (8, LANES), 0)
    tile_lane = lax.broadcasted_iota(jnp.int32, (8, LANES), 1)
    tall_lane = lax.broadcasted_iota(jnp.int32, (edge, LANES), 1)
    chunks = [(k, side, half) for k in range(2) for half in range(2) for side in range(SIDES)]

    def pack(chunk):
        kind, side, half = chunks[chunk]
        for k in range(cap):
            if kind == 0:
                at = 0 if side else 8 - NEED
                rows_at = pl.ds(0 if side else edge - 8, 8)
                pieces = [cells[k, f, rows_at, half * LANES : (half + 1) * LANES] for f in range(5)]
                made = pack_face(pieces, at, 1, 0, tile_row)
            else:
                at = 0 if side else LANES - NEED * edge
                lanes_at = pl.ds(0 if side else flat - LANES, LANES)
                pieces = [cells[k, f, half * 8 : (half + 1) * 8, lanes_at] for f in range(5)]
                made = pack_face(pieces, at, edge, 1, tile_lane)
            for which in range(2):
                packed[chunk][1, k, which] = made[which]

    used = [0, 0]

    def number(send):
        used[send] += 1
        return used[send] - 1

    def to_rows(source, into, column, through=None):
        recv = [number(0) for _ in range(3)]
        flights = []
        for rel in range(4):
            far, device = rel // 2, (served[rel], column)
            target = into.at[far]
            if rel == 3 and through is not None:
                far, device, target = 2, (served[2], my_col), through
            flights.append(remote(source[rel], target, number(1), recv[far], device))
        return flights

    gathers = [
        remote(p.at[1], p.at[0], number(1), number(0), (partner, my_col))
        for p in (*packed, *edge_packed)
    ]
    gathers, edge_gathers = gathers[:PARTS], gathers[PARTS:]
    sends = [
        to_rows(picks[c], chosen[c], toward[chunks[c][1]], merged[c]) for c in range(PARTS)
    ]
    edge_sends = [
        to_rows(edge_picks[i], edge_chosen[i], toward[i]) for i in range(SIDES)
    ]
    swap = remote(leaving, beside, number(1), number(0), (partner, my_col))
    other_hub = (rows - 1 - my_row, my_col)
    recv = number(0)
    reach = remote(leaving, across, number(1), recv, other_hub)
    relay = remote(across, across, number(1), recv, (partner, my_col))
    crossings, relays = [], []
    for i in range(SEND):
        recv = number(0)
        crossings.append(remote(far_out[i], far_in[i], number(1), recv, other_hub))
        if i < FORWARD:
            relays.append(remote(far_in[i], far_in[i], number(1), recv, (partner, my_col)))

    def on_hub(do):
        pl.when(is_hub)(do)

    def on_edge(do):
        pl.when(jnp.logical_not(is_hub))(do)

    pack(0)
    pl.semaphore_wait(barrier, 3 * rows - 1)
    on_edge(gathers[0].start)
    seating.wait()

    def entry(row, slot, column):
        return tab[row * 8 + slot, column]

    def origin(row, slot):
        code = entry(row, slot, 0)
        return code >> 4, code & 15

    my_stay = entry(my_row, 0, 2)
    near_stay = entry(partner, 0, 2)
    my_base = entry(my_row, 0, 1)

    def fill_leaving():
        for i in range(SEND):
            leaving[i] = cells[jnp.minimum(my_stay + i, cap - 1)]

    @pl.when(is_hub)
    def _():
        fill_leaving()
        reach.start()
        swap.start()

    for c in range(1, PARTS):
        pack(c)
        on_edge(gathers[c].start)

    @pl.when(jnp.logical_not(is_hub))
    def _():
        fill_leaving()
        for flight in gathers:
            flight.wait_send()
        swap.start()

    def seat_of(place):
        return jnp.where((place >> 4) == hub, 1, 0), jnp.minimum(place & 15, cap - 1)

    def choose(c):
        kind, side, half = chunks[c]
        gathers[c].wait_recv()
        for rel in (3, 2, 0):
            for s in range(OUT):
                q, k = seat_of(entry(served[rel], s, 4 + 2 * side + kind) & 63)
                picks[c][rel][s] = packed[c][q, k]
            sends[c][rel].start()

    def merge(c):
        kind, side, half = chunks[c]
        sends[c][3].wait_recv()
        for s in range(OUT):
            place = entry(partner, s, 4 + 2 * side + kind) & 63
            q, k = seat_of(place)
            picks[c][1][s] = jnp.where((place >> 5) == pair, packed[c][q, k], merged[c][s])
        sends[c][1].start()

    @pl.when(is_hub)
    def _():
        for c in range(PARTS + LAG):
            if c == RELAY:
                reach.wait_recv()
                relay.start()
            if c < PARTS:
                choose(c)
            if c >= LAG:
                merge(c - LAG)

    hub_flag = jnp.where(is_hub, 1, 0)

    def whose(slot, column, shift):
        code = (tab[rows * 8 + slot, column] >> shift) & 63
        return jnp.where((code >> 5) == pair, 0, 1)

    def await_chunk(c):
        sends[c][0].wait_recv()
        on_hub(sends[c][2].wait_recv)

    for c in range(4):
        await_chunk(c)
    corner_group = tile_lane >> 4
    for s in range(OUT):
        low, high = whose(s, 0, 0) * hub_flag, whose(s, 2, 0) * hub_flag
        tiles = []
        for half in range(2):
            got = []
            for side, far, at in ((0, low, 8 - NEED), (1, high, 0)):
                c = 2 * half + side
                first, last = chosen[c][far, s, 0], chosen[c][far, s, 1]
                got.append(unpack_face(first, last, at, 1, 0, tile_row))
            tiles.append([jnp.where(tile_row >= 4, a, b) for a, b in zip(*got)])
            for f in range(5):
                halo[s, f, half] = tiles[half][f]
        for side in range(SIDES):
            source = tiles[0] if side else tiles[parts - 1]
            made = jnp.zeros((8, LANES), jnp.float32)
            for f in range(5):
                one = 0 if side else LANES - edge
                two = edge if side else LANES - 2 * edge
                inner = (tile_row == 3) | (tile_row == 4)
                tile = jnp.where(
                    inner,
                    turned(turned(source[f], 4, 0), edge * f - two, 1),
                    turned(source[f], edge * f - one, 1),
                )
                made = jnp.where(corner_group == f, tile, made)
            edge_packed[side][1, s] = made
    for side in range(SIDES):
        on_edge(edge_gathers[side].start)

    def choose_corner(side):
        edge_gathers[side].wait_recv()
        for rel in (2, 3, 1, 0):
            for s in range(OUT):
                place = (entry(served[rel], s, 5 + 2 * side) >> 6) & 63
                q, k = seat_of(place)
                edge_picks[side][rel][s] = edge_packed[side][q, jnp.minimum(k, OUT - 1)]
            edge_sends[side][rel].start()

    @pl.when(is_hub)
    def _():
        for side in range(SIDES):
            choose_corner(side)

    swap.wait_recv()

    @pl.when(is_hub)
    def _():
        hub_row, edge_row = served[2], served[3]
        onward = entry(edge_row, 0, 8)
        last = entry(edge_row, 0, 3) - onward
        hub_base = entry(hub_row, 0, 1)
        for i in range(SEND):
            k = jnp.where(
                i < onward,
                entry(edge_row, jnp.clip(last + i, 0, 7), 0),
                entry(hub_row, jnp.clip(hub_base + i - onward, 0, 7), 0),
            )
            far_out[i][...] = beside[jnp.clip((k & 15) - near_stay, 0, SEND - 1)]
            crossings[i].start()

    for c in range(4, PARTS):
        await_chunk(c)
    for side in range(SIDES):
        for far in range(2):
            edge_sends[side][2 * far].wait_recv()

    filled = entry(my_row, 0, 3)
    onward = entry(pair * (rows - 1), 0, 8)
    far_stay = entry(rows - 1 - hub, 0, 2)
    first_far = jnp.where(is_hub, my_base - onward, filled - onward)
    on_edge(reach.wait_recv)

    def run(s, carry):
        at_row, k = origin(my_row, s)
        mine = cells[jnp.minimum(k, cap - 1)]
        near = beside[jnp.clip(k - near_stay, 0, SEND - 1)]
        far = across[jnp.clip(k - far_stay, 0, SEND - 1)]
        far_hub = at_row == rows - 1 - hub
        home = jnp.where(at_row == my_row, mine, jnp.where(far_hub, far, near))
        now[:, :edge, :flat] = home
        far_edge = at_row == (1 - pair) * (rows - 1)
        for i in range(SEND):

            @pl.when((s == i + 1) & is_hub)
            def _():
                crossings[i].wait_recv()
                if i < FORWARD:
                    relays[i].start()

            if i < FORWARD:

                @pl.when((s == i + LATE) & jnp.logical_not(is_hub))
                def _():
                    crossings[i].wait_recv()

            ready = jnp.where(is_hub, i + 1, i + LATE if i < FORWARD else OUT)

            @pl.when(s >= ready)
            def _():
                here = now[:, :edge, :flat]
                chosen_far = far_edge & (s - first_far == i)
                now[:, :edge, :flat] = jnp.where(chosen_far, far_in[i][...], here)

        for f in range(5):
            for half in range(2):
                now[f, edge:, half * LANES : (half + 1) * LANES] = halo[s, f, half]
        low, high = whose(s, 1, 0) * hub_flag, whose(s, 3, 0) * hub_flag
        for half in range(2):
            got = []
            for side, far, at in ((0, low, LANES - NEED * edge), (1, high, 0)):
                c = 4 + 2 * half + side
                first, last = chosen[c][far, s, 0], chosen[c][far, s, 1]
                got.append(unpack_face(first, last, at, edge, 1, tile_lane))
            for f in range(5):
                now[f, half * 8 : (half + 1) * 8, flat:] = jnp.where(
                    tile_lane >= LANES // 2, got[0][f], got[1][f]
                )
        low = edge_chosen[0][whose(s, 1, 6), s]
        high = edge_chosen[1][whose(s, 3, 6), s]
        for f in range(5):
            a = turned(low, LANES - edge - edge * f, 1)
            b = turned(turned(low, 4, 0), LANES - 2 * edge - edge * f, 1)
            c = turned(high, -edge * f, 1)
            d = turned(turned(high, 4, 0), edge - edge * f, 1)
            tile = jnp.where(tile_lane < edge, c, d)
            tile = jnp.where(tile_lane >= LANES // 2, b, tile)
            now[f, edge:, flat:] = jnp.where(tile_lane >= LANES - edge, a, tile)
        for f, field in enumerate(conserved([now[f] for f in range(5)])):
            start[f] = field
            now[f] = field
        for step in range(3):
            cons = tuple(now[f] for f in range(5))
            rate = section_rate(cons, edge)
            moved = [c + DT * d for c, d in zip(cons, rate)]
            if step == 1:
                moved = [0.75 * start[f] + 0.25 * moved[f] for f in range(5)]
            if step == 2:
                moved = [m[:edge, :flat] for m in moved]
                moved = [
                    (1.0 / 3.0) * start[f, :edge, :flat] + (2.0 / 3.0) * moved[f] for f in range(5)
                ]
                rho = moved[0]
                vel = [m / rho for m in moved[1:4]]
                p = 0.4 * (
                    moved[4] - 0.5 * rho * (vel[0] * vel[0] + vel[1] * vel[1] + vel[2] * vel[2])
                )
                for f, field in enumerate((rho, *vel, p)):
                    out[s, f] = jnp.where(s < filled, field, 0.0)
            else:
                for f in range(5):
                    now[f] = moved[f]
        return carry

    lax.fori_loop(0, OUT, run, 0)
    swap.wait_send()

    @pl.when(is_hub)
    def _():
        for group in (*sends, *edge_sends, crossings, relays, (reach, relay)):
            for flight in group:
                flight.wait_send()

    @pl.when(jnp.logical_not(is_hub))
    def _():
        for flight in edge_gathers:
            flight.wait_send()


def wide_body(rows, cols, block_cells, slot_blocks):
    cap = slot_blocks.shape[1]
    edge, flat = block_cells.shape[2:]
    block = (5, edge, flat)
    f32 = lambda *shape: pltpu.VMEM(shape, jnp.float32)
    face_tiles = (2, 8, LANES)
    grown = (5, edge + 8, flat + LANES)
    scratch = [pltpu.VMEM((2, cols, LANES), jnp.int32)]
    scratch += [space((rows * 8 + 8, LANES), jnp.int32) for space in (pltpu.VMEM, pltpu.SMEM)]
    scratch += [f32(2, cap, *face_tiles) for _ in range(PARTS)]
    scratch += [f32(2, OUT, *face_tiles) for _ in range(PARTS)]
    scratch += [f32(OUT, *face_tiles) for _ in range(4 * PARTS)]
    scratch += [f32(OUT, *face_tiles) for _ in range(PARTS)]
    scratch += [f32(2, OUT, 8, LANES) for _ in range(4)]
    scratch += [f32(OUT, 8, LANES) for _ in range(8)]
    scratch += [f32(SEND, *block) for _ in range(3)]
    scratch += [f32(*block) for _ in range(2 * SEND)]
    scratch += [f32(OUT, 5, 2, 8, LANES), f32(*grown), f32(*grown)]
    scratch += [pltpu.SemaphoreType.DMA((n,)) for n in (6 * PARTS + 32, 4 * PARTS + 16, 1)]
    return pl.pallas_call(
        functools.partial(wide_kernel, rows, cols, cap),
        out_shape=jax.ShapeDtypeStruct((OUT, *block), jnp.float32),
        in_specs=[
            pl.BlockSpec(memory_space=pltpu.VMEM),
            pl.BlockSpec(memory_space=pltpu.VMEM),
        ],
        out_specs=pl.BlockSpec(memory_space=pltpu.VMEM),
        scratch_shapes=scratch,
        compiler_params=pltpu.CompilerParams(
            collective_id=0, has_side_effects=True, vmem_limit_bytes=40 << 20
        ),
    )(slot_blocks.T, block_cells)


def solution(mesh):
    rows, cols = mesh.shape["row"], mesh.shape["col"]
    local = wide_body if (rows, cols) == (4, 8) else body
    return jax.shard_map(
        functools.partial(local, rows, cols),
        mesh=mesh,
        in_specs=(P(("row", "col"), None, None, None), P()),
        out_specs=P(("row", "col"), None, None, None),
        check_vma=False,
    )
```

```python
import functools

import jax
import jax.numpy as jnp
from jax import lax
from jax.experimental import pallas as pl
from jax.experimental.pallas import tpu as pltpu
from jax.sharding import PartitionSpec as P

MESH = pl.DeviceIdType.MESH
BLK_MEAN = 6
OUT = 7
SEND = BLK_MEAN - 1
LANES = 128
DT = 0.12


def make_tables(slot_blocks, rows, cols, my_row, my_col):
    cap = slot_blocks.shape[1]
    levels = rows.bit_length() - 1
    half = rows // 2
    group = BLK_MEAN * rows
    ids = slot_blocks.reshape(rows, cols, cap)
    counts = jnp.sum((ids >= 0).astype(jnp.int32), axis=2)
    row_ids = jnp.arange(rows, dtype=jnp.int32)
    col_ids = jnp.arange(cols, dtype=jnp.int32)
    at_row = jnp.broadcast_to(row_ids[:, None, None], ids.shape)
    at_slot = jnp.broadcast_to(jnp.arange(cap, dtype=jnp.int32), ids.shape)
    mine = (row_ids[:, None] == my_row) & (col_ids[None, :] == my_col)
    scalars = []
    for level in range(levels):
        bit = 1 << level
        other = counts.reshape(rows // (2 * bit), 2, bit, cols)[:, ::-1].reshape(rows, cols)
        send = jnp.maximum(counts - other, 0) // 2
        take = jnp.maximum(other - counts, 0) // 2
        keep = counts - send
        scalars.append(jnp.sum(jnp.where(mine, keep, 0)))
        hit = at_row[None] == row_ids[:, None, None, None]
        keep_here = jnp.sum(jnp.where(hit, keep[:, None, :, None], 0), axis=0)
        other_here = jnp.sum(jnp.where(hit, other[:, None, :, None], 0), axis=0)
        moved = at_slot >= keep_here
        at_row = jnp.where(moved, at_row ^ bit, at_row)
        at_slot = jnp.where(moved, other_here + at_slot - keep_here, at_slot)
        counts = keep + take
    scalars.append(jnp.sum(jnp.where(mine, counts, 0)))
    place = at_row * 16 + at_slot
    origin = row_ids[:, None, None] * 16 + jnp.arange(cap, dtype=jnp.int32)
    origin = jnp.broadcast_to(origin, ids.shape).reshape(-1)
    flat_ids = ids.reshape(-1)
    flat_place = jnp.where(flat_ids >= 0, place.reshape(-1), 0)
    flat_col = jnp.broadcast_to(col_ids[None, :, None], ids.shape).reshape(-1)
    near_far = jnp.stack([my_row, my_row ^ half])
    left, right = (my_col + cols - 1) % cols, (my_col + 1) % cols
    seat_rows = jnp.concatenate([near_far[:1], near_far, near_far])
    seat_cols = jnp.stack([my_col, right, right, left, left])
    seats = (seat_rows[:, None] * 16 + jnp.arange(OUT, dtype=jnp.int32)).reshape(-1, 1)
    seat_cols = jnp.repeat(seat_cols, OUT)[:, None]
    match = (flat_place[None] == seats) & (flat_col[None] == seat_cols) & (flat_ids >= 0)[None]
    along = jnp.sum(jnp.where(match, flat_ids[None] - flat_col[None] * group, 0), axis=1)
    along = along.reshape(5, OUT)
    here, there_right, there_left = along[:1], along[1:3], along[3:5]
    down, up = (lambda a: (a + group - 1) % group), (lambda a: (a + 1) % group)
    mine = jnp.concatenate([left * group + here, left * group + down(here)])
    mine = jnp.concatenate([mine, right * group + here, right * group + up(here)])
    theirs = jnp.concatenate([there_right, down(there_right), there_left, up(there_left)])
    wanted = jnp.concatenate([mine, theirs + my_col * group]).reshape(-1)
    both = flat_place * 4096 + origin
    found = jnp.sum(jnp.where(flat_ids[None] == wanted[:, None], both[None], 0), axis=1)
    source = found ^ (my_row * 16 * 4097)
    source = jnp.concatenate([source & 4095, source >> 12])
    return jnp.concatenate([jnp.stack(scalars), source])


def cell_values(cons):
    rho, mx, my, mz, energy = cons
    inv = 1.0 / rho
    vel = (mx * inv, my * inv, mz * inv)
    p = 0.4 * (energy - 0.5 * rho * (vel[0] * vel[0] + vel[1] * vel[1] + vel[2] * vel[2]))
    theta = p * inv
    sound = jnp.sqrt(1.4 * theta)
    kappa = 0.2 * jnp.exp(0.7 * jnp.log(theta))
    return vel, p, theta, sound, kappa


def conserved(primitive):
    rho, u, v, w, p = primitive
    energy = p / 0.4 + 0.5 * rho * (u * u + v * v + w * w)
    return (rho, rho * u, rho * v, rho * w, energy)


def direction_values(cons, values, normal):
    vel, p, theta, sound, kappa = values
    un = vel[normal]
    flux = [cons[1 + normal], cons[1] * un, cons[2] * un, cons[3] * un, (cons[4] + p) * un]
    flux[1 + normal] = flux[1 + normal] + p
    return (*cons, *flux, jnp.abs(un) + sound, theta, kappa)


def face(low, high):
    half_speed = 0.5 * jnp.maximum(low[10], high[10])
    out = [0.5 * (low[5 + i] + high[5 + i]) - half_speed * (high[i] - low[i]) for i in range(5)]
    out[4] = out[4] - 0.5 * (low[12] + high[12]) * (high[11] - low[11])
    return out


def block_rate(cons, ghost_x, ghost_y):
    edge, flat = cons[0].shape
    row = lax.broadcasted_iota(jnp.int32, (edge, flat), 0)
    lane = lax.broadcasted_iota(jnp.int32, (edge, flat), 1)
    values = cell_values(cons)
    mid = direction_values(cons, values, 0)
    gx = direction_values(ghost_x, cell_values(ghost_x), 0)
    last = row == edge - 1
    up = [
        jnp.where(last, jnp.concatenate([g, g], axis=0), pltpu.roll(m, edge - 1, 0))
        for m, g in zip(mid, gx)
    ]
    upper = face(mid, up)
    bottom = face(gx, [m[:8] for m in mid])
    change = [
        u - jnp.where(row == 0, jnp.concatenate([b, b], axis=0), pltpu.roll(u, 1, 0))
        for u, b in zip(upper, bottom)
    ]
    mid = direction_values(cons, values, 1)
    gy = direction_values(ghost_y, cell_values(ghost_y), 1)
    last = lane >= flat - edge
    up = [
        jnp.where(last, jnp.concatenate([g, g], axis=1), pltpu.roll(m, flat - edge, 1))
        for m, g in zip(mid, gy)
    ]
    upper = face(mid, up)
    bottom = face(gy, [m[:, :LANES] for m in mid])
    change = [
        t + (u - jnp.where(lane < edge, jnp.concatenate([b, b], axis=1), pltpu.roll(u, edge, 1)))
        for t, u, b in zip(change, upper, bottom)
    ]
    mid = direction_values(cons, values, 2)
    up = [pltpu.roll(m, flat - 1, 1) for m in mid]
    upper = face(mid, up)
    height = lane & (edge - 1)
    zero = jnp.zeros_like(values[1])
    wall = [zero, zero, zero, values[1], zero]
    change = [
        t
        + (
            jnp.where(height == edge - 1, w, u)
            - jnp.where(height == 0, w, pltpu.roll(u, 1, 1))
        )
        for t, u, w in zip(change, upper, wall)
    ]
    return [-t for t in change]


def y_units(n):
    return 2 * ((5 * n + 7) // 8)


def units(n):
    return y_units(n) + (10 * n + 7) // 8


def y_seat(slot, f):
    at = slot * 5 + f
    return 2 * (at >> 3), 16 * (at & 7)


def x_seat(n, slot, f, part):
    at = slot * 10 + 2 * f + part
    return y_units(n) + (at >> 3), at & 7


def kernel(rows, cols, cap, *refs):
    levels = rows.bit_length() - 1
    half = rows // 2
    refs = list(refs)
    tab, cells, out = refs[:3]
    refs = refs[3:]
    send_blocks = refs[:levels]
    recv_blocks = refs[levels : 2 * levels]
    refs = refs[2 * levels :]
    start, now = refs[:2]
    sections = [refs[2 + 10 * i : 12 + 10 * i] for i in range(3)]
    bsend, brecv, hsend, hrecv = refs[32:36]
    my_row, my_col = lax.axis_index("row"), lax.axis_index("col")
    left = (my_row, lax.rem(my_col + cols - 1, cols))
    right = (my_row, lax.rem(my_col + 1, cols))

    def partner(level):
        bit = 1 << level
        return (my_row + bit - 2 * bit * (lax.rem(my_row // bit, 2)), my_col)

    barrier = pltpu.get_barrier_semaphore()
    across = partner(levels - 1)[0]
    beside = [(right, left), ((across, right[1]), (across, left[1]))]
    for device in [*beside[0], *beside[1]] + [partner(level) for level in range(levels)]:
        pl.semaphore_signal(barrier, inc=1, device_id=device, device_id_type=MESH)
    pl.semaphore_wait(barrier, 4 + levels)

    def held(slot, depth):
        value = cells[jnp.minimum(slot, cap - 1)]
        for level in range(depth):
            keep = tab[level]
            got = recv_blocks[level][jnp.clip(slot - keep, 0, SEND - 1)]
            value = jnp.where(slot >= keep, got, value)
        return value

    edge, flat = now.shape[2:]
    tile_lane = lax.broadcasted_iota(jnp.int32, (edge, LANES), 1)
    tile_group = tile_lane >> 4
    ghost_row = lax.broadcasted_iota(jnp.int32, (8, 2 * LANES), 0)

    def tile_of(ref, *seat):
        *lead, unit = seat
        return ref[(*lead, pl.ds(unit, 2))].reshape(edge, LANES)

    def put_tile(ref, unit, tile):
        ref[unit : unit + 2] = tile.reshape(2, 8, LANES)

    def move_blocks(level):
        for k in range(SEND):
            send_blocks[level][k] = held(tab[level] + k, level)
        copy = pltpu.make_async_remote_copy(
            src_ref=send_blocks[level],
            dst_ref=recv_blocks[level],
            send_sem=bsend.at[level],
            recv_sem=brecv.at[level],
            device_id=partner(level),
            device_id_type=MESH,
        )
        copy.start()
        return copy

    def remote(step, at, src, dst, device):
        copy = pltpu.make_async_remote_copy(
            src_ref=src,
            dst_ref=dst,
            send_sem=hsend.at[step, at],
            recv_sem=hrecv.at[step, at],
            device_id=device,
            device_id_type=MESH,
        )
        copy.start()
        return copy

    def pack(blocks, n, buffer, high):
        x = edge - 1 if high else 0
        side = slice(LANES, 2 * LANES) if high else slice(0, LANES)
        for first in range(0, 5 * n, 8):
            tile = None
            for at in range(first, min(first + 8, 5 * n)):
                s, f = at // 5, at % 5
                shift = (edge * (at - first) + (edge if high else 0)) % LANES
                piece = blocks[s, f, :, side]
                piece = pltpu.roll(piece, shift, 1) if shift else piece
                tile = piece if tile is None else jnp.where(tile_group == at - first, piece, tile)
            put_tile(buffer, 2 * (first // 8), tile)
        for s in range(n):
            for f in range(5):
                for part in range(2):
                    unit, row = x_seat(n, s, f, part)
                    buffer[unit, row : row + 1, :] = blocks[
                        s, f, x : x + 1, part * LANES : (part + 1) * LANES
                    ]

    base = levels + 1

    def entry(step, kind, far, slot):
        at = kind * OUT if far is None else 4 * OUT + (kind * 2 + far) * OUT
        return tab[base + (12 * OUT if step else 0) + at + slot]

    def near_seat(code):
        return jnp.minimum(code >> 4, half - 1), code & 15

    def select(step, n, known, pick, first_kind, far):
        for s in range(OUT):
            q, sigma = near_seat(entry(step, first_kind, far, s))
            for f in range(5):
                for part in range(2):
                    unit, row = x_seat(n, sigma, f, part)
                    to, at = x_seat(OUT, s, f, part)
                    pick[to, at : at + 1, :] = known[q, unit, pl.ds(row, 1), :]
        seats = [near_seat(entry(step, first_kind + 1, far, s)) for s in range(OUT)]
        for first in range(0, 5 * OUT, 8):
            tile = None
            for at in range(first, min(first + 8, 5 * OUT)):
                q, sigma = seats[at // 5]
                unit, lane = y_seat(sigma, at % 5)
                shift = (edge * (at - first) + LANES - lane) & (LANES - 1)
                piece = pltpu.roll(tile_of(known, q, unit), shift, 1)
                tile = piece if tile is None else jnp.where(tile_group == at - first, piece, tile)
            put_tile(pick, 2 * (first // 8), tile)

    def begin(step, blocks, n):
        flights = []
        for side in range(2):
            known = sections[step][side]
            pack(blocks, n, known.at[0], side == 0)
            if levels > 1:
                flights.append(remote(step, side, known.at[0], known.at[1], partner(0)))
        return flights

    def gather(step, flights):
        for level in range(1, levels - 1):
            size = 1 << level
            for side in range(2):
                known = sections[step][side]
                flights[side].wait()
                flights[side] = remote(
                    step,
                    2 * level + side,
                    known.at[pl.ds(0, size)],
                    known.at[pl.ds(size, size)],
                    partner(level),
                )
        return flights

    def trade(step, n, flights):
        sent = []
        for side in range(2):
            if flights:
                flights[side].wait()
            for far in (1, 0):
                known, pick, sel = (sections[step][at] for at in (side, 2 + 2 * side + far, 6 + 2 * side + far))
                select(step, n, known, pick, 2 * side, far)
                at = 2 * (levels - 1) + 2 * side + far
                sent.append(remote(step, at, pick, sel, beside[far][side]))
        return sent

    def open_block(slot, carry):
        value = held(slot, levels)
        for f, field in enumerate(conserved([value[f] for f in range(5)])):
            start[slot, f] = field
            now[slot, f] = field
        return carry

    def advance(step):
        lo_near, lo_far, hi_near, hi_far = sections[step][6:]

        def run(slot, carry):
            def near(kind):
                return entry(step, kind, None, slot) < 16 * half

            def x_row(close, away, kind, f):
                parts = []
                for part in range(2):
                    unit, row = x_seat(OUT, slot, f, part)
                    a = close[unit, pl.ds(row, 1), :]
                    b = away[unit, pl.ds(row, 1), :]
                    parts.append(jnp.where(near(kind), a, b))
                return jnp.concatenate(parts, axis=1)

            def y_tile(close, away, kind, f, to):
                unit, lane = y_seat(slot, f)
                tile = jnp.where(near(kind), tile_of(close, unit), tile_of(away, unit))
                return pltpu.roll(tile, (LANES + to - lane) & (LANES - 1), 1)

            ghost_x, ghost_y = [], []
            for f in range(5):
                low = x_row(lo_near, lo_far, 0, f)
                high = x_row(hi_near, hi_far, 2, f)
                ghost_x.append(jnp.where(ghost_row == 0, low, high))
                low = y_tile(lo_near, lo_far, 1, f, 0)
                high = y_tile(hi_near, hi_far, 3, f, LANES - edge)
                ghost_y.append(jnp.where(tile_lane < edge, low, high))
            if step == 0:
                ghost_x, ghost_y = conserved(ghost_x), conserved(ghost_y)
            cons = tuple(now[slot, f] for f in range(5))
            rate = block_rate(cons, tuple(ghost_x), tuple(ghost_y))
            moved = [c + DT * d for c, d in zip(cons, rate)]
            if step == 1:
                moved = [0.75 * start[slot, f] + 0.25 * moved[f] for f in range(5)]
            if step == 2:
                moved = [(1.0 / 3.0) * start[slot, f] + (2.0 / 3.0) * moved[f] for f in range(5)]
                rho = moved[0]
                vel = [m / rho for m in moved[1:4]]
                p = 0.4 * (
                    moved[4] - 0.5 * rho * (vel[0] * vel[0] + vel[1] * vel[1] + vel[2] * vel[2])
                )
                filled = slot < tab[levels]
                for f, field in enumerate((rho, *vel, p)):
                    out[slot, f] = jnp.where(filled, field, 0.0)
            else:
                for f in range(5):
                    now[slot, f] = moved[f]
            return carry

        lax.fori_loop(0, OUT, run, 0)

    moving = move_blocks(0)
    flights = begin(0, cells, cap)
    flights = gather(0, flights)
    for level in range(1, levels):
        moving.wait()
        moving = move_blocks(level)
    flights = trade(0, cap, flights)
    moving.wait()
    lax.fori_loop(0, OUT, open_block, 0)
    for step in range(3):
        if step:
            flights = trade(step, OUT, gather(step, begin(step, now, OUT)))
        for flight in flights:
            flight.wait()
        advance(step)


def body(rows, cols, block_cells, slot_blocks):
    cap = slot_blocks.shape[1]
    levels = rows.bit_length() - 1
    half = rows // 2
    edge, flat = block_cells.shape[2:]
    table = make_tables(slot_blocks, rows, cols, lax.axis_index("row"), lax.axis_index("col"))
    block = (5, edge, flat)
    scratch = [pltpu.VMEM((SEND, *block), jnp.float32) for _ in range(2 * levels)]
    scratch += [pltpu.VMEM((OUT, *block), jnp.float32) for _ in range(2)]
    for step in range(3):
        faces = (units(OUT if step else cap), 8, LANES)
        picked = (units(OUT), 8, LANES)
        scratch += [pltpu.VMEM((half, *faces), jnp.float32) for _ in range(2)]
        scratch += [pltpu.VMEM(picked, jnp.float32) for _ in range(8)]
    scratch += [pltpu.SemaphoreType.DMA((levels,)) for _ in range(2)]
    scratch += [pltpu.SemaphoreType.DMA((3, 2 * (levels + 1))) for _ in range(2)]
    return pl.pallas_call(
        functools.partial(kernel, rows, cols, cap),
        out_shape=jax.ShapeDtypeStruct((OUT, *block), jnp.float32),
        in_specs=[
            pl.BlockSpec(memory_space=pltpu.SMEM),
            pl.BlockSpec(memory_space=pltpu.VMEM),
        ],
        out_specs=pl.BlockSpec(memory_space=pltpu.VMEM),
        scratch_shapes=scratch,
        compiler_params=pltpu.CompilerParams(
            collective_id=0, has_side_effects=True, vmem_limit_bytes=32 << 20
        ),
    )(table, block_cells)


SIDES = 2
NEED = 3
PARTS = 8
LAG = 4
FORWARD = 2
LATE = 3
RELAY = 4


def swap_lanes(a, lane, step):
    size = a.shape[1]
    return jnp.where((lane & step) == 0, pltpu.roll(a, size - step, 1), pltpu.roll(a, step, 1))


def seat_tables(slots, scratch, rows, cols, my_row, my_col):
    cap, devices = slots.shape
    slots = jnp.concatenate([slots, jnp.zeros((16 - cap, devices), jnp.int32)], axis=0)
    slots = jnp.concatenate([slots, jnp.zeros((16, LANES - devices), jnp.int32)], axis=1)
    slots = jnp.transpose(slots)[:devices, :cap]
    group = BLK_MEAN * rows
    span = 16 * rows
    lane = lax.broadcasted_iota(jnp.int32, (cols, LANES), 1)
    col = lax.broadcasted_iota(jnp.int32, (cols, LANES), 0)
    row, slot = (lane >> 4) & (rows - 1), lane & 15
    ids = jnp.full((cols, LANES), -1, jnp.int32)
    for r in range(rows):
        part = slots[r * cols : (r + 1) * cols, :]
        part = jnp.concatenate([part, jnp.full((cols, LANES - cap), -1, jnp.int32)], axis=1)
        part = jnp.where(lane < span, part, pltpu.roll(part, span, 1))
        part = pltpu.roll(part, 16 * r, 1) if r else part
        ids = jnp.where(row == r, part, ids)
    held = ids >= 0
    counts = jnp.where(held, 1, 0)
    for step in (1, 2, 4, 8):
        counts = counts + swap_lanes(counts, lane, step)
    other = swap_lanes(counts, lane, 16)
    keep = counts - (jnp.maximum(counts - other, 0) >> 1)
    crossed = slot >= keep
    at_row = jnp.where(crossed, row ^ 1, row)
    at_slot = jnp.where(crossed, other + slot - keep, slot)
    counts = keep + (jnp.maximum(other - counts, 0) >> 1)
    other = swap_lanes(counts, lane, 32)
    keep = counts - (jnp.maximum(counts - other, 0) >> 1)
    keep = jnp.where(crossed, swap_lanes(keep, lane, 16), keep)
    other = jnp.where(crossed, swap_lanes(other, lane, 16), other)
    crossed = at_slot >= keep
    at_row = jnp.where(crossed, at_row ^ 2, at_row)
    at_slot = jnp.where(crossed, other + at_slot - keep, at_slot)
    held = held & (lane < span)
    scratch[0] = jnp.where(held, ids - col * group, -100)
    scratch[1] = jnp.where(held, at_row * 16 + at_slot, -100)

    def line(kind, c, n):
        return jnp.broadcast_to(scratch[kind, pl.ds(c, 1), :], (n, LANES))

    def total(mask, value):
        return jnp.sum(jnp.where(mask, value, 0), axis=1, keepdims=True)

    def down(j):
        return jnp.where(j <= 0, j + group - 1, j - 1)

    def up(j):
        return jnp.where(j >= group - 1, j + 1 - group, j + 1)

    left, right = lax.rem(my_col + cols - 1, cols), lax.rem(my_col + 1, cols)
    n = rows * 8
    seat = lax.broadcasted_iota(jnp.int32, (n, LANES), 0)
    lane = lax.broadcasted_iota(jnp.int32, (n, LANES), 1)
    to_row, target = seat >> 3, (seat >> 3) * 16 + (seat & 7)
    j_here, f_here = line(0, my_col, n), line(1, my_col, n)
    code = lane + 64 * f_here
    on = (f_here >> 4) == to_row
    columns = [
        total(f_here == target, lane),
        total(on & ((lane >> 5) == (to_row >> 1)), 1),
        total(on & ((lane >> 4) == to_row), 1),
        total(on, 1),
    ]
    for c, moved in ((right, down), (left, up)):
        j = total(line(1, c, n) == target, line(0, c, n) + 1) - 1
        columns.append(total(j_here == j, code))
        columns.append(total(j_here == moved(j), code))
    columns.append(total(on & ((lane >> 4) == rows - 1 - to_row), 1))
    first = jnp.zeros((n, LANES), jnp.int32)
    for at, value in enumerate(columns):
        first = jnp.where(lane == at, value, first)
    seat = lax.broadcasted_iota(jnp.int32, (8, LANES), 0)
    lane = lax.broadcasted_iota(jnp.int32, (8, LANES), 1)
    j = total(line(1, my_col, 8) == my_row * 16 + seat, line(0, my_col, 8) + 1) - 1
    second = jnp.zeros((8, LANES), jnp.int32)
    for at, (c, key) in enumerate(((left, j), (left, down(j)), (right, j), (right, up(j)))):
        value = total(line(0, c, 8) == key, lane + 64 * line(1, c, 8))
        second = jnp.where(lane == at, value, second)
    return jnp.concatenate([first, second], axis=0)


def turned(tile, shift, axis):
    shift %= tile.shape[axis]
    return pltpu.roll(tile, shift, axis) if shift else tile


def pack_face(pieces, at, unit, axis, index):
    a, b, c, d, e = pieces
    first = jnp.where(index < 3 * unit, turned(a, -at, axis), turned(b, 3 * unit - at, axis))
    first = jnp.where(index < 6 * unit, first, turned(c, 6 * unit - at, axis))
    last = jnp.where(index < 3 * unit, turned(d, -at, axis), turned(e, 3 * unit - at, axis))
    last = jnp.where(index < 6 * unit, last, turned(c, 4 * unit - at, axis))
    return first, last


def unpack_face(first, last, at, unit, axis, index):
    third = jnp.where(
        index < at + 2 * unit,
        turned(first, at - 6 * unit, axis),
        turned(last, at - 4 * unit, axis),
    )
    return (
        turned(first, at, axis),
        turned(first, at - 3 * unit, axis),
        third,
        turned(last, at, axis),
        turned(last, at - 3 * unit, axis),
    )


def section_rate(cons, edge):
    shape = cons[0].shape
    height = lax.broadcasted_iota(jnp.int32, shape, 1) & (edge - 1)
    values = cell_values(cons)
    change = None
    for normal, axis, step in ((0, 0, 1), (1, 1, edge), (2, 1, 1)):
        mid = direction_values(cons, values, normal)
        up = [pltpu.roll(m, shape[axis] - step, axis) for m in mid]
        upper = face(mid, up)
        lower = [pltpu.roll(u, step, axis) for u in upper]
        if normal == 2:
            zero = jnp.zeros_like(values[1])
            wall = [zero, zero, zero, values[1], zero]
            upper = [jnp.where(height == edge - 1, w, u) for u, w in zip(upper, wall)]
            lower = [jnp.where(height == 0, w, u) for u, w in zip(lower, wall)]
        delta = [u - l for u, l in zip(upper, lower)]
        change = delta if change is None else [t + d for t, d in zip(change, delta)]
    return [-t for t in change]


def wide_kernel(rows, cols, cap, slots, cells, out, *refs):
    refs = list(refs)
    take = lambda n: [refs.pop(0) for _ in range(n)]
    (lines, seats, tab) = take(3)
    packed, chosen, picks = take(PARTS), take(PARTS), [take(4) for _ in range(PARTS)]
    merged = take(PARTS)
    edge_packed, edge_chosen, edge_picks = take(2), take(2), [take(4) for _ in range(2)]
    (leaving, beside, across) = take(3)
    far_out, far_in = take(SEND), take(SEND)
    (halo, start, now) = take(3)
    (ssem, rsem, lsem) = take(3)
    edge, flat = out.shape[2:]
    parts = flat // LANES
    my_row, my_col = lax.axis_index("row"), lax.axis_index("col")
    left, right = lax.rem(my_col + cols - 1, cols), lax.rem(my_col + 1, cols)
    pair = my_row // 2
    partner = my_row + 1 - 2 * lax.rem(my_row, 2)
    is_hub = my_row == 1 + pair
    hub = 1 + pair
    served = [my_row, partner, rows - 1 - my_row, lax.rem(my_row + 2, rows)]
    toward = [right, left]

    barrier = pltpu.get_barrier_semaphore()
    for step in range(1, rows):
        device = (lax.rem(my_row + step, rows), my_col)
        pl.semaphore_signal(barrier, inc=1, device_id=device, device_id_type=MESH)
    for step in range(rows):
        for c in toward:
            device = (lax.rem(my_row + step, rows), c)
            pl.semaphore_signal(barrier, inc=1, device_id=device, device_id_type=MESH)
    seats[...] = seat_tables(slots[...], lines, rows, cols, my_row, my_col)
    seating = pltpu.make_async_copy(seats, tab, lsem.at[0])
    seating.start()

    def remote(src, dst, send, recv, device):
        return pltpu.make_async_remote_copy(
            src_ref=src,
            dst_ref=dst,
            send_sem=ssem.at[send],
            recv_sem=rsem.at[recv],
            device_id=device,
            device_id_type=MESH,
        )

    tile_row = lax.broadcasted_iota(jnp.int32, (8, LANES), 0)
    tile_lane = lax.broadcasted_iota(jnp.int32, (8, LANES), 1)
    tall_lane = lax.broadcasted_iota(jnp.int32, (edge, LANES), 1)
    chunks = [(k, side, half) for k in range(2) for half in range(2) for side in range(SIDES)]

    def pack(chunk):
        kind, side, half = chunks[chunk]
        for k in range(cap):
            if kind == 0:
                at = 0 if side else 8 - NEED
                rows_at = pl.ds(0 if side else edge - 8, 8)
                pieces = [cells[k, f, rows_at, half * LANES : (half + 1) * LANES] for f in range(5)]
                made = pack_face(pieces, at, 1, 0, tile_row)
            else:
                at = 0 if side else LANES - NEED * edge
                lanes_at = pl.ds(0 if side else flat - LANES, LANES)
                pieces = [cells[k, f, half * 8 : (half + 1) * 8, lanes_at] for f in range(5)]
                made = pack_face(pieces, at, edge, 1, tile_lane)
            for which in range(2):
                packed[chunk][1, k, which] = made[which]

    used = [0, 0]

    def number(send):
        used[send] += 1
        return used[send] - 1

    def to_rows(source, into, column, through=None):
        recv = [number(0) for _ in range(3)]
        flights = []
        for rel in range(4):
            far, device = rel // 2, (served[rel], column)
            target = into.at[far]
            if rel == 3 and through is not None:
                far, device, target = 2, (served[2], my_col), through
            flights.append(remote(source[rel], target, number(1), recv[far], device))
        return flights

    gathers = [
        remote(p.at[1], p.at[0], number(1), number(0), (partner, my_col))
        for p in (*packed, *edge_packed)
    ]
    gathers, edge_gathers = gathers[:PARTS], gathers[PARTS:]
    sends = [
        to_rows(picks[c], chosen[c], toward[chunks[c][1]], merged[c]) for c in range(PARTS)
    ]
    edge_sends = [
        to_rows(edge_picks[i], edge_chosen[i], toward[i]) for i in range(SIDES)
    ]
    swap = remote(leaving, beside, number(1), number(0), (partner, my_col))
    other_hub = (rows - 1 - my_row, my_col)
    recv = number(0)
    reach = remote(leaving, across, number(1), recv, other_hub)
    relay = remote(across, across, number(1), recv, (partner, my_col))
    crossings, relays = [], []
    for i in range(SEND):
        recv = number(0)
        crossings.append(remote(far_out[i], far_in[i], number(1), recv, other_hub))
        if i < FORWARD:
            relays.append(remote(far_in[i], far_in[i], number(1), recv, (partner, my_col)))

    def on_hub(do):
        pl.when(is_hub)(do)

    def on_edge(do):
        pl.when(jnp.logical_not(is_hub))(do)

    pack(0)
    pl.semaphore_wait(barrier, 3 * rows - 1)
    on_edge(gathers[0].start)
    seating.wait()

    def entry(row, slot, column):
        return tab[row * 8 + slot, column]

    def origin(row, slot):
        code = entry(row, slot, 0)
        return code >> 4, code & 15

    my_stay = entry(my_row, 0, 2)
    near_stay = entry(partner, 0, 2)
    my_base = entry(my_row, 0, 1)

    def fill_leaving():
        for i in range(SEND):
            leaving[i] = cells[jnp.minimum(my_stay + i, cap - 1)]

    @pl.when(is_hub)
    def _():
        fill_leaving()
        reach.start()
        swap.start()

    for c in range(1, PARTS):
        pack(c)
        on_edge(gathers[c].start)

    @pl.when(jnp.logical_not(is_hub))
    def _():
        fill_leaving()
        for flight in gathers:
            flight.wait_send()
        swap.start()

    def seat_of(place):
        return jnp.where((place >> 4) == hub, 1, 0), jnp.minimum(place & 15, cap - 1)

    def choose(c):
        kind, side, half = chunks[c]
        gathers[c].wait_recv()
        for rel in (3, 2, 0):
            for s in range(OUT):
                q, k = seat_of(entry(served[rel], s, 4 + 2 * side + kind) & 63)
                picks[c][rel][s] = packed[c][q, k]
            sends[c][rel].start()

    def merge(c):
        kind, side, half = chunks[c]
        sends[c][3].wait_recv()
        for s in range(OUT):
            place = entry(partner, s, 4 + 2 * side + kind) & 63
            q, k = seat_of(place)
            picks[c][1][s] = jnp.where((place >> 5) == pair, packed[c][q, k], merged[c][s])
        sends[c][1].start()

    @pl.when(is_hub)
    def _():
        for c in range(PARTS + LAG):
            if c == RELAY:
                reach.wait_recv()
                relay.start()
            if c < PARTS:
                choose(c)
            if c >= LAG:
                merge(c - LAG)

    hub_flag = jnp.where(is_hub, 1, 0)

    def whose(slot, column, shift):
        code = (tab[rows * 8 + slot, column] >> shift) & 63
        return jnp.where((code >> 5) == pair, 0, 1)

    def await_chunk(c):
        sends[c][0].wait_recv()
        on_hub(sends[c][2].wait_recv)

    for c in range(4):
        await_chunk(c)
    corner_group = tile_lane >> 4
    for s in range(OUT):
        low, high = whose(s, 0, 0) * hub_flag, whose(s, 2, 0) * hub_flag
        tiles = []
        for half in range(2):
            got = []
            for side, far, at in ((0, low, 8 - NEED), (1, high, 0)):
                c = 2 * half + side
                first, last = chosen[c][far, s, 0], chosen[c][far, s, 1]
                got.append(unpack_face(first, last, at, 1, 0, tile_row))
            tiles.append([jnp.where(tile_row >= 4, a, b) for a, b in zip(*got)])
            for f in range(5):
                halo[s, f, half] = tiles[half][f]
        for side in range(SIDES):
            source = tiles[0] if side else tiles[parts - 1]
            made = jnp.zeros((8, LANES), jnp.float32)
            for f in range(5):
                one = 0 if side else LANES - edge
                two = edge if side else LANES - 2 * edge
                inner = (tile_row == 3) | (tile_row == 4)
                tile = jnp.where(
                    inner,
                    turned(turned(source[f], 4, 0), edge * f - two, 1),
                    turned(source[f], edge * f - one, 1),
                )
                made = jnp.where(corner_group == f, tile, made)
            edge_packed[side][1, s] = made
    for side in range(SIDES):
        on_edge(edge_gathers[side].start)

    def choose_corner(side):
        edge_gathers[side].wait_recv()
        for rel in (2, 3, 1, 0):
            for s in range(OUT):
                place = (entry(served[rel], s, 5 + 2 * side) >> 6) & 63
                q, k = seat_of(place)
                edge_picks[side][rel][s] = edge_packed[side][q, jnp.minimum(k, OUT - 1)]
            edge_sends[side][rel].start()

    @pl.when(is_hub)
    def _():
        for side in range(SIDES):
            choose_corner(side)

    swap.wait_recv()

    @pl.when(is_hub)
    def _():
        hub_row, edge_row = served[2], served[3]
        onward = entry(edge_row, 0, 8)
        last = entry(edge_row, 0, 3) - onward
        hub_base = entry(hub_row, 0, 1)
        for i in range(SEND):
            k = jnp.where(
                i < onward,
                entry(edge_row, jnp.clip(last + i, 0, 7), 0),
                entry(hub_row, jnp.clip(hub_base + i - onward, 0, 7), 0),
            )
            far_out[i][...] = beside[jnp.clip((k & 15) - near_stay, 0, SEND - 1)]
            crossings[i].start()

    for c in range(4, PARTS):
        await_chunk(c)
    for side in range(SIDES):
        for far in range(2):
            edge_sends[side][2 * far].wait_recv()

    filled = entry(my_row, 0, 3)
    onward = entry(pair * (rows - 1), 0, 8)
    far_stay = entry(rows - 1 - hub, 0, 2)
    first_far = jnp.where(is_hub, my_base - onward, filled - onward)
    on_edge(reach.wait_recv)

    def run(turn, carry):
        s = lax.rem(turn + OUT - 1, OUT)
        at_row, k = origin(my_row, s)
        mine = cells[jnp.minimum(k, cap - 1)]
        near = beside[jnp.clip(k - near_stay, 0, SEND - 1)]
        far = across[jnp.clip(k - far_stay, 0, SEND - 1)]
        far_hub = at_row == rows - 1 - hub
        home = jnp.where(at_row == my_row, mine, jnp.where(far_hub, far, near))
        now[:, :edge, :flat] = home
        far_edge = at_row == (1 - pair) * (rows - 1)
        for i in range(SEND):

            @pl.when((s == i + 1) & is_hub)
            def _():
                crossings[i].wait_recv()
                if i < FORWARD:
                    relays[i].start()

            if i < FORWARD:

                @pl.when((s == i + LATE) & jnp.logical_not(is_hub))
                def _():
                    crossings[i].wait_recv()

            ready = jnp.where(is_hub, i + 1, i + LATE if i < FORWARD else OUT)

            @pl.when((s >= ready) & (s < OUT - 1))
            def _():
                here = now[:, :edge, :flat]
                chosen_far = far_edge & (s - first_far == i)
                now[:, :edge, :flat] = jnp.where(chosen_far, far_in[i][...], here)

        for f in range(5):
            for half in range(2):
                now[f, edge:, half * LANES : (half + 1) * LANES] = halo[s, f, half]
        low, high = whose(s, 1, 0) * hub_flag, whose(s, 3, 0) * hub_flag
        for half in range(2):
            got = []
            for side, far, at in ((0, low, LANES - NEED * edge), (1, high, 0)):
                c = 4 + 2 * half + side
                first, last = chosen[c][far, s, 0], chosen[c][far, s, 1]
                got.append(unpack_face(first, last, at, edge, 1, tile_lane))
            for f in range(5):
                now[f, half * 8 : (half + 1) * 8, flat:] = jnp.where(
                    tile_lane >= LANES // 2, got[0][f], got[1][f]
                )
        low = edge_chosen[0][whose(s, 1, 6), s]
        high = edge_chosen[1][whose(s, 3, 6), s]
        for f in range(5):
            a = turned(low, LANES - edge - edge * f, 1)
            b = turned(turned(low, 4, 0), LANES - 2 * edge - edge * f, 1)
            c = turned(high, -edge * f, 1)
            d = turned(turned(high, 4, 0), edge - edge * f, 1)
            tile = jnp.where(tile_lane < edge, c, d)
            tile = jnp.where(tile_lane >= LANES // 2, b, tile)
            now[f, edge:, flat:] = jnp.where(tile_lane >= LANES - edge, a, tile)
        for f, field in enumerate(conserved([now[f] for f in range(5)])):
            start[f] = field
            now[f] = field
        for step in range(3):
            cons = tuple(now[f] for f in range(5))
            rate = section_rate(cons, edge)
            moved = [c + DT * d for c, d in zip(cons, rate)]
            if step == 1:
                moved = [0.75 * start[f] + 0.25 * moved[f] for f in range(5)]
            if step == 2:
                moved = [m[:edge, :flat] for m in moved]
                moved = [
                    (1.0 / 3.0) * start[f, :edge, :flat] + (2.0 / 3.0) * moved[f] for f in range(5)
                ]
                rho = moved[0]
                vel = [m / rho for m in moved[1:4]]
                p = 0.4 * (
                    moved[4] - 0.5 * rho * (vel[0] * vel[0] + vel[1] * vel[1] + vel[2] * vel[2])
                )
                for f, field in enumerate((rho, *vel, p)):
                    out[s, f] = jnp.where(s < filled, field, 0.0)
            else:
                for f in range(5):
                    now[f] = moved[f]
        return carry

    lax.fori_loop(0, OUT, run, 0)
    swap.wait_send()

    @pl.when(is_hub)
    def _():
        for group in (*sends, *edge_sends, crossings, relays, (reach, relay)):
            for flight in group:
                flight.wait_send()

    @pl.when(jnp.logical_not(is_hub))
    def _():
        for flight in edge_gathers:
            flight.wait_send()


def wide_body(rows, cols, block_cells, slot_blocks):
    cap = slot_blocks.shape[1]
    edge, flat = block_cells.shape[2:]
    block = (5, edge, flat)
    f32 = lambda *shape: pltpu.VMEM(shape, jnp.float32)
    face_tiles = (2, 8, LANES)
    grown = (5, edge + 8, flat + LANES)
    scratch = [pltpu.VMEM((2, cols, LANES), jnp.int32)]
    scratch += [space((rows * 8 + 8, LANES), jnp.int32) for space in (pltpu.VMEM, pltpu.SMEM)]
    scratch += [f32(2, cap, *face_tiles) for _ in range(PARTS)]
    scratch += [f32(2, OUT, *face_tiles) for _ in range(PARTS)]
    scratch += [f32(OUT, *face_tiles) for _ in range(4 * PARTS)]
    scratch += [f32(OUT, *face_tiles) for _ in range(PARTS)]
    scratch += [f32(2, OUT, 8, LANES) for _ in range(4)]
    scratch += [f32(OUT, 8, LANES) for _ in range(8)]
    scratch += [f32(SEND, *block) for _ in range(3)]
    scratch += [f32(*block) for _ in range(2 * SEND)]
    scratch += [f32(OUT, 5, 2, 8, LANES), f32(*grown), f32(*grown)]
    scratch += [pltpu.SemaphoreType.DMA((n,)) for n in (6 * PARTS + 32, 4 * PARTS + 16, 1)]
    return pl.pallas_call(
        functools.partial(wide_kernel, rows, cols, cap),
        out_shape=jax.ShapeDtypeStruct((OUT, *block), jnp.float32),
        in_specs=[
            pl.BlockSpec(memory_space=pltpu.VMEM),
            pl.BlockSpec(memory_space=pltpu.VMEM),
        ],
        out_specs=pl.BlockSpec(memory_space=pltpu.VMEM),
        scratch_shapes=scratch,
        compiler_params=pltpu.CompilerParams(
            collective_id=0, has_side_effects=True, vmem_limit_bytes=40 << 20
        ),
    )(slot_blocks.T, block_cells)


def solution(mesh):
    rows, cols = mesh.shape["row"], mesh.shape["col"]
    local = wide_body if (rows, cols) == (4, 8) else body
    return jax.shard_map(
        functools.partial(local, rows, cols),
        mesh=mesh,
        in_specs=(P(("row", "col"), None, None, None), P()),
        out_specs=P(("row", "col"), None, None, None),
        check_vma=False,
    )
```

```python
import functools

import jax
import jax.numpy as jnp
from jax import lax
from jax.experimental import pallas as pl
from jax.experimental.pallas import tpu as pltpu
from jax.sharding import PartitionSpec as P

MESH = pl.DeviceIdType.MESH
BLK_MEAN = 6
OUT = 7
SEND = BLK_MEAN - 1
LANES = 128
DT = 0.12


def make_tables(slot_blocks, rows, cols, my_row, my_col):
    cap = slot_blocks.shape[1]
    levels = rows.bit_length() - 1
    half = rows // 2
    group = BLK_MEAN * rows
    ids = slot_blocks.reshape(rows, cols, cap)
    counts = jnp.sum((ids >= 0).astype(jnp.int32), axis=2)
    row_ids = jnp.arange(rows, dtype=jnp.int32)
    col_ids = jnp.arange(cols, dtype=jnp.int32)
    at_row = jnp.broadcast_to(row_ids[:, None, None], ids.shape)
    at_slot = jnp.broadcast_to(jnp.arange(cap, dtype=jnp.int32), ids.shape)
    mine = (row_ids[:, None] == my_row) & (col_ids[None, :] == my_col)
    scalars = []
    for level in range(levels):
        bit = 1 << level
        other = counts.reshape(rows // (2 * bit), 2, bit, cols)[:, ::-1].reshape(rows, cols)
        send = jnp.maximum(counts - other, 0) // 2
        take = jnp.maximum(other - counts, 0) // 2
        keep = counts - send
        scalars.append(jnp.sum(jnp.where(mine, keep, 0)))
        hit = at_row[None] == row_ids[:, None, None, None]
        keep_here = jnp.sum(jnp.where(hit, keep[:, None, :, None], 0), axis=0)
        other_here = jnp.sum(jnp.where(hit, other[:, None, :, None], 0), axis=0)
        moved = at_slot >= keep_here
        at_row = jnp.where(moved, at_row ^ bit, at_row)
        at_slot = jnp.where(moved, other_here + at_slot - keep_here, at_slot)
        counts = keep + take
    scalars.append(jnp.sum(jnp.where(mine, counts, 0)))
    place = at_row * 16 + at_slot
    origin = row_ids[:, None, None] * 16 + jnp.arange(cap, dtype=jnp.int32)
    origin = jnp.broadcast_to(origin, ids.shape).reshape(-1)
    flat_ids = ids.reshape(-1)
    flat_place = jnp.where(flat_ids >= 0, place.reshape(-1), 0)
    flat_col = jnp.broadcast_to(col_ids[None, :, None], ids.shape).reshape(-1)
    near_far = jnp.stack([my_row, my_row ^ half])
    left, right = (my_col + cols - 1) % cols, (my_col + 1) % cols
    seat_rows = jnp.concatenate([near_far[:1], near_far, near_far])
    seat_cols = jnp.stack([my_col, right, right, left, left])
    seats = (seat_rows[:, None] * 16 + jnp.arange(OUT, dtype=jnp.int32)).reshape(-1, 1)
    seat_cols = jnp.repeat(seat_cols, OUT)[:, None]
    match = (flat_place[None] == seats) & (flat_col[None] == seat_cols) & (flat_ids >= 0)[None]
    along = jnp.sum(jnp.where(match, flat_ids[None] - flat_col[None] * group, 0), axis=1)
    along = along.reshape(5, OUT)
    here, there_right, there_left = along[:1], along[1:3], along[3:5]
    down, up = (lambda a: (a + group - 1) % group), (lambda a: (a + 1) % group)
    mine = jnp.concatenate([left * group + here, left * group + down(here)])
    mine = jnp.concatenate([mine, right * group + here, right * group + up(here)])
    theirs = jnp.concatenate([there_right, down(there_right), there_left, up(there_left)])
    wanted = jnp.concatenate([mine, theirs + my_col * group]).reshape(-1)
    both = flat_place * 4096 + origin
    found = jnp.sum(jnp.where(flat_ids[None] == wanted[:, None], both[None], 0), axis=1)
    source = found ^ (my_row * 16 * 4097)
    source = jnp.concatenate([source & 4095, source >> 12])
    return jnp.concatenate([jnp.stack(scalars), source])


def cell_values(cons):
    rho, mx, my, mz, energy = cons
    inv = 1.0 / rho
    vel = (mx * inv, my * inv, mz * inv)
    p = 0.4 * (energy - 0.5 * rho * (vel[0] * vel[0] + vel[1] * vel[1] + vel[2] * vel[2]))
    theta = p * inv
    sound = jnp.sqrt(1.4 * theta)
    kappa = 0.2 * jnp.exp(0.7 * jnp.log(theta))
    return vel, p, theta, sound, kappa


def conserved(primitive):
    rho, u, v, w, p = primitive
    energy = p / 0.4 + 0.5 * rho * (u * u + v * v + w * w)
    return (rho, rho * u, rho * v, rho * w, energy)


def direction_values(cons, values, normal):
    vel, p, theta, sound, kappa = values
    un = vel[normal]
    flux = [cons[1 + normal], cons[1] * un, cons[2] * un, cons[3] * un, (cons[4] + p) * un]
    flux[1 + normal] = flux[1 + normal] + p
    return (*cons, *flux, jnp.abs(un) + sound, theta, kappa)


def face(low, high):
    half_speed = 0.5 * jnp.maximum(low[10], high[10])
    out = [0.5 * (low[5 + i] + high[5 + i]) - half_speed * (high[i] - low[i]) for i in range(5)]
    out[4] = out[4] - 0.5 * (low[12] + high[12]) * (high[11] - low[11])
    return out


def block_rate(cons, ghost_x, ghost_y):
    edge, flat = cons[0].shape
    row = lax.broadcasted_iota(jnp.int32, (edge, flat), 0)
    lane = lax.broadcasted_iota(jnp.int32, (edge, flat), 1)
    values = cell_values(cons)
    mid = direction_values(cons, values, 0)
    gx = direction_values(ghost_x, cell_values(ghost_x), 0)
    last = row == edge - 1
    up = [
        jnp.where(last, jnp.concatenate([g, g], axis=0), pltpu.roll(m, edge - 1, 0))
        for m, g in zip(mid, gx)
    ]
    upper = face(mid, up)
    bottom = face(gx, [m[:8] for m in mid])
    change = [
        u - jnp.where(row == 0, jnp.concatenate([b, b], axis=0), pltpu.roll(u, 1, 0))
        for u, b in zip(upper, bottom)
    ]
    mid = direction_values(cons, values, 1)
    gy = direction_values(ghost_y, cell_values(ghost_y), 1)
    last = lane >= flat - edge
    up = [
        jnp.where(last, jnp.concatenate([g, g], axis=1), pltpu.roll(m, flat - edge, 1))
        for m, g in zip(mid, gy)
    ]
    upper = face(mid, up)
    bottom = face(gy, [m[:, :LANES] for m in mid])
    change = [
        t + (u - jnp.where(lane < edge, jnp.concatenate([b, b], axis=1), pltpu.roll(u, edge, 1)))
        for t, u, b in zip(change, upper, bottom)
    ]
    mid = direction_values(cons, values, 2)
    up = [pltpu.roll(m, flat - 1, 1) for m in mid]
    upper = face(mid, up)
    height = lane & (edge - 1)
    zero = jnp.zeros_like(values[1])
    wall = [zero, zero, zero, values[1], zero]
    change = [
        t
        + (
            jnp.where(height == edge - 1, w, u)
            - jnp.where(height == 0, w, pltpu.roll(u, 1, 1))
        )
        for t, u, w in zip(change, upper, wall)
    ]
    return [-t for t in change]


def y_units(n):
    return 2 * ((5 * n + 7) // 8)


def units(n):
    return y_units(n) + (10 * n + 7) // 8


def y_seat(slot, f):
    at = slot * 5 + f
    return 2 * (at >> 3), 16 * (at & 7)


def x_seat(n, slot, f, part):
    at = slot * 10 + 2 * f + part
    return y_units(n) + (at >> 3), at & 7


def kernel(rows, cols, cap, *refs):
    levels = rows.bit_length() - 1
    half = rows // 2
    refs = list(refs)
    tab, cells, out = refs[:3]
    refs = refs[3:]
    send_blocks = refs[:levels]
    recv_blocks = refs[levels : 2 * levels]
    refs = refs[2 * levels :]
    start, now = refs[:2]
    sections = [refs[2 + 10 * i : 12 + 10 * i] for i in range(3)]
    bsend, brecv, hsend, hrecv = refs[32:36]
    my_row, my_col = lax.axis_index("row"), lax.axis_index("col")
    left = (my_row, lax.rem(my_col + cols - 1, cols))
    right = (my_row, lax.rem(my_col + 1, cols))

    def partner(level):
        bit = 1 << level
        return (my_row + bit - 2 * bit * (lax.rem(my_row // bit, 2)), my_col)

    barrier = pltpu.get_barrier_semaphore()
    across = partner(levels - 1)[0]
    beside = [(right, left), ((across, right[1]), (across, left[1]))]
    for device in [*beside[0], *beside[1]] + [partner(level) for level in range(levels)]:
        pl.semaphore_signal(barrier, inc=1, device_id=device, device_id_type=MESH)
    pl.semaphore_wait(barrier, 4 + levels)

    def held(slot, depth):
        value = cells[jnp.minimum(slot, cap - 1)]
        for level in range(depth):
            keep = tab[level]
            got = recv_blocks[level][jnp.clip(slot - keep, 0, SEND - 1)]
            value = jnp.where(slot >= keep, got, value)
        return value

    edge, flat = now.shape[2:]
    tile_lane = lax.broadcasted_iota(jnp.int32, (edge, LANES), 1)
    tile_group = tile_lane >> 4
    ghost_row = lax.broadcasted_iota(jnp.int32, (8, 2 * LANES), 0)

    def tile_of(ref, *seat):
        *lead, unit = seat
        return ref[(*lead, pl.ds(unit, 2))].reshape(edge, LANES)

    def put_tile(ref, unit, tile):
        ref[unit : unit + 2] = tile.reshape(2, 8, LANES)

    def move_blocks(level):
        for k in range(SEND):
            send_blocks[level][k] = held(tab[level] + k, level)
        copy = pltpu.make_async_remote_copy(
            src_ref=send_blocks[level],
            dst_ref=recv_blocks[level],
            send_sem=bsend.at[level],
            recv_sem=brecv.at[level],
            device_id=partner(level),
            device_id_type=MESH,
        )
        copy.start()
        return copy

    def remote(step, at, src, dst, device):
        copy = pltpu.make_async_remote_copy(
            src_ref=src,
            dst_ref=dst,
            send_sem=hsend.at[step, at],
            recv_sem=hrecv.at[step, at],
            device_id=device,
            device_id_type=MESH,
        )
        copy.start()
        return copy

    def pack(blocks, n, buffer, high):
        x = edge - 1 if high else 0
        side = slice(LANES, 2 * LANES) if high else slice(0, LANES)
        for first in range(0, 5 * n, 8):
            tile = None
            for at in range(first, min(first + 8, 5 * n)):
                s, f = at // 5, at % 5
                shift = (edge * (at - first) + (edge if high else 0)) % LANES
                piece = blocks[s, f, :, side]
                piece = pltpu.roll(piece, shift, 1) if shift else piece
                tile = piece if tile is None else jnp.where(tile_group == at - first, piece, tile)
            put_tile(buffer, 2 * (first // 8), tile)
        for s in range(n):
            for f in range(5):
                for part in range(2):
                    unit, row = x_seat(n, s, f, part)
                    buffer[unit, row : row + 1, :] = blocks[
                        s, f, x : x + 1, part * LANES : (part + 1) * LANES
                    ]

    base = levels + 1

    def entry(step, kind, far, slot):
        at = kind * OUT if far is None else 4 * OUT + (kind * 2 + far) * OUT
        return tab[base + (12 * OUT if step else 0) + at + slot]

    def near_seat(code):
        return jnp.minimum(code >> 4, half - 1), code & 15

    def select(step, n, known, pick, first_kind, far):
        for s in range(OUT):
            q, sigma = near_seat(entry(step, first_kind, far, s))
            for f in range(5):
                for part in range(2):
                    unit, row = x_seat(n, sigma, f, part)
                    to, at = x_seat(OUT, s, f, part)
                    pick[to, at : at + 1, :] = known[q, unit, pl.ds(row, 1), :]
        seats = [near_seat(entry(step, first_kind + 1, far, s)) for s in range(OUT)]
        for first in range(0, 5 * OUT, 8):
            tile = None
            for at in range(first, min(first + 8, 5 * OUT)):
                q, sigma = seats[at // 5]
                unit, lane = y_seat(sigma, at % 5)
                shift = (edge * (at - first) + LANES - lane) & (LANES - 1)
                piece = pltpu.roll(tile_of(known, q, unit), shift, 1)
                tile = piece if tile is None else jnp.where(tile_group == at - first, piece, tile)
            put_tile(pick, 2 * (first // 8), tile)

    def begin(step, blocks, n):
        flights = []
        for side in range(2):
            known = sections[step][side]
            pack(blocks, n, known.at[0], side == 0)
            if levels > 1:
                flights.append(remote(step, side, known.at[0], known.at[1], partner(0)))
        return flights

    def gather(step, flights):
        for level in range(1, levels - 1):
            size = 1 << level
            for side in range(2):
                known = sections[step][side]
                flights[side].wait()
                flights[side] = remote(
                    step,
                    2 * level + side,
                    known.at[pl.ds(0, size)],
                    known.at[pl.ds(size, size)],
                    partner(level),
                )
        return flights

    def trade(step, n, flights):
        sent = []
        for side in range(2):
            if flights:
                flights[side].wait()
            for far in (1, 0):
                known, pick, sel = (sections[step][at] for at in (side, 2 + 2 * side + far, 6 + 2 * side + far))
                select(step, n, known, pick, 2 * side, far)
                at = 2 * (levels - 1) + 2 * side + far
                sent.append(remote(step, at, pick, sel, beside[far][side]))
        return sent

    def open_block(slot, carry):
        value = held(slot, levels)
        for f, field in enumerate(conserved([value[f] for f in range(5)])):
            start[slot, f] = field
            now[slot, f] = field
        return carry

    def advance(step):
        lo_near, lo_far, hi_near, hi_far = sections[step][6:]

        def run(slot, carry):
            def near(kind):
                return entry(step, kind, None, slot) < 16 * half

            def x_row(close, away, kind, f):
                parts = []
                for part in range(2):
                    unit, row = x_seat(OUT, slot, f, part)
                    a = close[unit, pl.ds(row, 1), :]
                    b = away[unit, pl.ds(row, 1), :]
                    parts.append(jnp.where(near(kind), a, b))
                return jnp.concatenate(parts, axis=1)

            def y_tile(close, away, kind, f, to):
                unit, lane = y_seat(slot, f)
                tile = jnp.where(near(kind), tile_of(close, unit), tile_of(away, unit))
                return pltpu.roll(tile, (LANES + to - lane) & (LANES - 1), 1)

            ghost_x, ghost_y = [], []
            for f in range(5):
                low = x_row(lo_near, lo_far, 0, f)
                high = x_row(hi_near, hi_far, 2, f)
                ghost_x.append(jnp.where(ghost_row == 0, low, high))
                low = y_tile(lo_near, lo_far, 1, f, 0)
                high = y_tile(hi_near, hi_far, 3, f, LANES - edge)
                ghost_y.append(jnp.where(tile_lane < edge, low, high))
            if step == 0:
                ghost_x, ghost_y = conserved(ghost_x), conserved(ghost_y)
            cons = tuple(now[slot, f] for f in range(5))
            rate = block_rate(cons, tuple(ghost_x), tuple(ghost_y))
            moved = [c + DT * d for c, d in zip(cons, rate)]
            if step == 1:
                moved = [0.75 * start[slot, f] + 0.25 * moved[f] for f in range(5)]
            if step == 2:
                moved = [(1.0 / 3.0) * start[slot, f] + (2.0 / 3.0) * moved[f] for f in range(5)]
                rho = moved[0]
                vel = [m / rho for m in moved[1:4]]
                p = 0.4 * (
                    moved[4] - 0.5 * rho * (vel[0] * vel[0] + vel[1] * vel[1] + vel[2] * vel[2])
                )
                filled = slot < tab[levels]
                for f, field in enumerate((rho, *vel, p)):
                    out[slot, f] = jnp.where(filled, field, 0.0)
            else:
                for f in range(5):
                    now[slot, f] = moved[f]
            return carry

        lax.fori_loop(0, OUT, run, 0)

    moving = move_blocks(0)
    flights = begin(0, cells, cap)
    flights = gather(0, flights)
    for level in range(1, levels):
        moving.wait()
        moving = move_blocks(level)
    flights = trade(0, cap, flights)
    moving.wait()
    lax.fori_loop(0, OUT, open_block, 0)
    for step in range(3):
        if step:
            flights = trade(step, OUT, gather(step, begin(step, now, OUT)))
        for flight in flights:
            flight.wait()
        advance(step)


def body(rows, cols, block_cells, slot_blocks):
    cap = slot_blocks.shape[1]
    levels = rows.bit_length() - 1
    half = rows // 2
    edge, flat = block_cells.shape[2:]
    table = make_tables(slot_blocks, rows, cols, lax.axis_index("row"), lax.axis_index("col"))
    block = (5, edge, flat)
    scratch = [pltpu.VMEM((SEND, *block), jnp.float32) for _ in range(2 * levels)]
    scratch += [pltpu.VMEM((OUT, *block), jnp.float32) for _ in range(2)]
    for step in range(3):
        faces = (units(OUT if step else cap), 8, LANES)
        picked = (units(OUT), 8, LANES)
        scratch += [pltpu.VMEM((half, *faces), jnp.float32) for _ in range(2)]
        scratch += [pltpu.VMEM(picked, jnp.float32) for _ in range(8)]
    scratch += [pltpu.SemaphoreType.DMA((levels,)) for _ in range(2)]
    scratch += [pltpu.SemaphoreType.DMA((3, 2 * (levels + 1))) for _ in range(2)]
    return pl.pallas_call(
        functools.partial(kernel, rows, cols, cap),
        out_shape=jax.ShapeDtypeStruct((OUT, *block), jnp.float32),
        in_specs=[
            pl.BlockSpec(memory_space=pltpu.SMEM),
            pl.BlockSpec(memory_space=pltpu.VMEM),
        ],
        out_specs=pl.BlockSpec(memory_space=pltpu.VMEM),
        scratch_shapes=scratch,
        compiler_params=pltpu.CompilerParams(
            collective_id=0, has_side_effects=True, vmem_limit_bytes=32 << 20
        ),
    )(table, block_cells)


SIDES = 2
NEED = 3
PARTS = 8
LAG = 4
EARLY = 4
AHEAD = 2
FORWARD = 2
LATE = 3
RELAY = 4


def swap_lanes(a, lane, step):
    size = a.shape[1]
    return jnp.where((lane & step) == 0, pltpu.roll(a, size - step, 1), pltpu.roll(a, step, 1))


def seat_tables(slots, scratch, rows, cols, my_row, my_col):
    cap, devices = slots.shape
    slots = jnp.concatenate([slots, jnp.zeros((16 - cap, devices), jnp.int32)], axis=0)
    slots = jnp.concatenate([slots, jnp.zeros((16, LANES - devices), jnp.int32)], axis=1)
    slots = jnp.transpose(slots)[:devices, :cap]
    group = BLK_MEAN * rows
    span = 16 * rows
    lane = lax.broadcasted_iota(jnp.int32, (cols, LANES), 1)
    col = lax.broadcasted_iota(jnp.int32, (cols, LANES), 0)
    row, slot = (lane >> 4) & (rows - 1), lane & 15
    ids = jnp.full((cols, LANES), -1, jnp.int32)
    for r in range(rows):
        part = slots[r * cols : (r + 1) * cols, :]
        part = jnp.concatenate([part, jnp.full((cols, LANES - cap), -1, jnp.int32)], axis=1)
        part = jnp.where(lane < span, part, pltpu.roll(part, span, 1))
        part = pltpu.roll(part, 16 * r, 1) if r else part
        ids = jnp.where(row == r, part, ids)
    held = ids >= 0
    counts = jnp.where(held, 1, 0)
    for step in (1, 2, 4, 8):
        counts = counts + swap_lanes(counts, lane, step)
    other = swap_lanes(counts, lane, 16)
    keep = counts - (jnp.maximum(counts - other, 0) >> 1)
    crossed = slot >= keep
    at_row = jnp.where(crossed, row ^ 1, row)
    at_slot = jnp.where(crossed, other + slot - keep, slot)
    counts = keep + (jnp.maximum(other - counts, 0) >> 1)
    other = swap_lanes(counts, lane, 32)
    keep = counts - (jnp.maximum(counts - other, 0) >> 1)
    keep = jnp.where(crossed, swap_lanes(keep, lane, 16), keep)
    other = jnp.where(crossed, swap_lanes(other, lane, 16), other)
    crossed = at_slot >= keep
    at_row = jnp.where(crossed, at_row ^ 2, at_row)
    at_slot = jnp.where(crossed, other + at_slot - keep, at_slot)
    held = held & (lane < span)
    scratch[0] = jnp.where(held, ids - col * group, -100)
    scratch[1] = jnp.where(held, at_row * 16 + at_slot, -100)

    def line(kind, c, n):
        return jnp.broadcast_to(scratch[kind, pl.ds(c, 1), :], (n, LANES))

    def total(mask, value):
        return jnp.sum(jnp.where(mask, value, 0), axis=1, keepdims=True)

    def down(j):
        return jnp.where(j <= 0, j + group - 1, j - 1)

    def up(j):
        return jnp.where(j >= group - 1, j + 1 - group, j + 1)

    left, right = lax.rem(my_col + cols - 1, cols), lax.rem(my_col + 1, cols)
    n = rows * 8
    seat = lax.broadcasted_iota(jnp.int32, (n, LANES), 0)
    lane = lax.broadcasted_iota(jnp.int32, (n, LANES), 1)
    to_row, target = seat >> 3, (seat >> 3) * 16 + (seat & 7)
    j_here, f_here = line(0, my_col, n), line(1, my_col, n)
    code = lane + 64 * f_here
    on = (f_here >> 4) == to_row
    columns = [
        total(f_here == target, lane),
        total(on & ((lane >> 5) == (to_row >> 1)), 1),
        total(on & ((lane >> 4) == to_row), 1),
        total(on, 1),
    ]
    for c, moved in ((right, down), (left, up)):
        j = total(line(1, c, n) == target, line(0, c, n) + 1) - 1
        columns.append(total(j_here == j, code))
        columns.append(total(j_here == moved(j), code))
    columns.append(total(on & ((lane >> 4) == rows - 1 - to_row), 1))
    first = jnp.zeros((n, LANES), jnp.int32)
    for at, value in enumerate(columns):
        first = jnp.where(lane == at, value, first)
    seat = lax.broadcasted_iota(jnp.int32, (8, LANES), 0)
    lane = lax.broadcasted_iota(jnp.int32, (8, LANES), 1)
    j = total(line(1, my_col, 8) == my_row * 16 + seat, line(0, my_col, 8) + 1) - 1
    second = jnp.zeros((8, LANES), jnp.int32)
    for at, (c, key) in enumerate(((left, j), (left, down(j)), (right, j), (right, up(j)))):
        value = total(line(0, c, 8) == key, lane + 64 * line(1, c, 8))
        second = jnp.where(lane == at, value, second)
    return jnp.concatenate([first, second], axis=0)


def turned(tile, shift, axis):
    shift %= tile.shape[axis]
    return pltpu.roll(tile, shift, axis) if shift else tile


def pack_face(pieces, at, unit, axis, index):
    a, b, c, d, e = pieces
    first = jnp.where(index < 3 * unit, turned(a, -at, axis), turned(b, 3 * unit - at, axis))
    first = jnp.where(index < 6 * unit, first, turned(c, 6 * unit - at, axis))
    last = jnp.where(index < 3 * unit, turned(d, -at, axis), turned(e, 3 * unit - at, axis))
    last = jnp.where(index < 6 * unit, last, turned(c, 4 * unit - at, axis))
    return first, last


def unpack_face(first, last, at, unit, axis, index):
    third = jnp.where(
        index < at + 2 * unit,
        turned(first, at - 6 * unit, axis),
        turned(last, at - 4 * unit, axis),
    )
    return (
        turned(first, at, axis),
        turned(first, at - 3 * unit, axis),
        third,
        turned(last, at, axis),
        turned(last, at - 3 * unit, axis),
    )


def twice_face(low, high):
    speed = jnp.maximum(low[10], high[10])
    out = [(low[5 + i] + high[5 + i]) - speed * (high[i] - low[i]) for i in range(5)]
    out[4] = out[4] - (low[12] + high[12]) * (high[11] - low[11])
    return out


def rolled_side(mid, un, normal, roll):
    cons, un = [roll(m) for m in mid[:5]], roll(un)
    speed, theta, kappa = (roll(m) for m in mid[10:])
    p = theta * cons[0]
    flux = [cons[1 + normal], cons[1] * un, cons[2] * un, cons[3] * un, (cons[4] + p) * un]
    flux[1 + normal] = flux[1 + normal] + p
    return (*cons, *flux, speed, theta, kappa)


def cut(values, height, width):
    if isinstance(values, (tuple, list)):
        return tuple(cut(v, height, width) for v in values)
    return values[:height, :width]


def twice_change(cons, edge, flat, last):
    rows, lanes = cons[0].shape
    values = cell_values(cons)
    change = None
    for normal, axis, step in ((0, 0, 1), (1, 1, edge), (2, 1, 1)):
        tall = edge if last and normal else rows
        wide = flat if last and normal != 1 else lanes
        here = cut(values, tall, wide)
        mid = direction_values(cut(cons, tall, wide), here, normal)
        size = (tall, wide)[axis]
        roll = functools.partial(pltpu.roll, shift=size - step, axis=axis)
        upper = twice_face(mid, rolled_side(mid, here[0][normal], normal, roll))
        if normal == 2:
            height = lax.broadcasted_iota(jnp.int32, (tall, wide), 1) & (edge - 1)
            wall = 2.0 * here[1]
            walls = [0.0, 0.0, 0.0, wall, 0.0]
            upper = [jnp.where(height == edge - 1, w, u) for u, w in zip(upper, walls)]
        lower = [pltpu.roll(u, step, axis) for u in upper]
        if normal == 2:
            lower[3] = jnp.where(height == 0, wall, lower[3])
        delta = [u - l for u, l in zip(upper, lower)]
        delta = cut(delta, edge, flat) if last else delta
        change = delta if change is None else [t + d for t, d in zip(change, delta)]
    return change


def wide_kernel(rows, cols, cap, slots, cells, out, *refs):
    refs = list(refs)
    take = lambda n: [refs.pop(0) for _ in range(n)]
    (lines, seats, tab) = take(3)
    packed, chosen, picks = take(PARTS), take(PARTS), [take(4) for _ in range(PARTS)]
    merged = take(PARTS)
    edge_packed, edge_chosen, edge_picks = take(2), take(2), [take(4) for _ in range(2)]
    (leaving, beside) = take(2)
    across, far_out, far_in = take(SEND), take(SEND), take(SEND)
    (halo, start, now) = take(3)
    (ssem, rsem, lsem) = take(3)
    edge, flat = out.shape[2:]
    parts = flat // LANES
    my_row, my_col = lax.axis_index("row"), lax.axis_index("col")
    left, right = lax.rem(my_col + cols - 1, cols), lax.rem(my_col + 1, cols)
    pair = my_row // 2
    partner = my_row + 1 - 2 * lax.rem(my_row, 2)
    is_hub = my_row == 1 + pair
    hub = 1 + pair
    served = [my_row, partner, rows - 1 - my_row, lax.rem(my_row + 2, rows)]
    toward = [right, left]

    barrier = pltpu.get_barrier_semaphore()
    for step in range(1, rows):
        device = (lax.rem(my_row + step, rows), my_col)
        pl.semaphore_signal(barrier, inc=1, device_id=device, device_id_type=MESH)
    for step in range(rows):
        for c in toward:
            device = (lax.rem(my_row + step, rows), c)
            pl.semaphore_signal(barrier, inc=1, device_id=device, device_id_type=MESH)
    seats[...] = seat_tables(slots[...], lines, rows, cols, my_row, my_col)
    seating = pltpu.make_async_copy(seats, tab, lsem.at[0])
    seating.start()

    def remote(src, dst, send, recv, device):
        return pltpu.make_async_remote_copy(
            src_ref=src,
            dst_ref=dst,
            send_sem=ssem.at[send],
            recv_sem=rsem.at[recv],
            device_id=device,
            device_id_type=MESH,
        )

    tile_row = lax.broadcasted_iota(jnp.int32, (8, LANES), 0)
    tile_lane = lax.broadcasted_iota(jnp.int32, (8, LANES), 1)
    tall_lane = lax.broadcasted_iota(jnp.int32, (edge, LANES), 1)
    chunks = [(k, side, half) for k in range(2) for half in range(2) for side in range(SIDES)]

    def pack(chunk):
        kind, side, half = chunks[chunk]
        for k in range(cap):
            if kind == 0:
                at = 0 if side else 8 - NEED
                rows_at = pl.ds(0 if side else edge - 8, 8)
                pieces = [cells[k, f, rows_at, half * LANES : (half + 1) * LANES] for f in range(5)]
                made = pack_face(pieces, at, 1, 0, tile_row)
            else:
                at = 0 if side else LANES - NEED * edge
                lanes_at = pl.ds(0 if side else flat - LANES, LANES)
                pieces = [cells[k, f, half * 8 : (half + 1) * 8, lanes_at] for f in range(5)]
                made = pack_face(pieces, at, edge, 1, tile_lane)
            for which in range(2):
                packed[chunk][1, k, which] = made[which]

    used = [0, 0]

    def number(send):
        used[send] += 1
        return used[send] - 1

    def to_rows(source, into, column, through=None):
        recv = [number(0) for _ in range(3)]
        flights = []
        for rel in range(4):
            far, device = rel // 2, (served[rel], column)
            target = into.at[far]
            if rel == 3 and through is not None:
                far, device, target = 2, (served[2], my_col), through
            flights.append(remote(source[rel], target, number(1), recv[far], device))
        return flights

    gathers = [
        remote(p.at[1], p.at[0], number(1), number(0), (partner, my_col))
        for p in (*packed, *edge_packed)
    ]
    gathers, edge_gathers = gathers[:PARTS], gathers[PARTS:]
    sends = [
        to_rows(picks[c], chosen[c], toward[chunks[c][1]], merged[c]) for c in range(PARTS)
    ]
    edge_sends = [
        to_rows(edge_picks[i], edge_chosen[i], toward[i]) for i in range(SIDES)
    ]
    swap = remote(leaving, beside, number(1), number(0), (partner, my_col))
    other_hub = (rows - 1 - my_row, my_col)
    reaches, passes, crossings, relays = [], [], [], []
    for i in range(SEND):
        recv = number(0)
        reaches.append(remote(leaving.at[i], across[i], number(1), recv, other_hub))
        passes.append(remote(across[i], across[i], number(1), recv, (partner, my_col)))
    for i in range(SEND):
        recv = number(0)
        crossings.append(remote(far_out[i], far_in[i], number(1), recv, other_hub))
        if i < FORWARD:
            relays.append(remote(far_in[i], far_in[i], number(1), recv, (partner, my_col)))

    def on_hub(do):
        pl.when(is_hub)(do)

    def on_edge(do):
        pl.when(jnp.logical_not(is_hub))(do)

    pack(0)
    pl.semaphore_wait(barrier, 3 * rows - 1)
    on_edge(gathers[0].start)
    seating.wait()

    def entry(row, slot, column):
        return tab[row * 8 + slot, column]

    def origin(row, slot):
        code = entry(row, slot, 0)
        return code >> 4, code & 15

    my_stay = entry(my_row, 0, 2)
    near_stay = entry(partner, 0, 2)
    my_base = entry(my_row, 0, 1)

    def fill_leaving():
        for i in range(SEND):
            leaving[i] = cells[jnp.minimum(my_stay + i, cap - 1)]

    @pl.when(is_hub)
    def _():
        fill_leaving()
        for flight in reaches[:EARLY]:
            flight.start()
        swap.start()

    for c in range(1, PARTS):
        pack(c)
        on_edge(gathers[c].start)

    @pl.when(jnp.logical_not(is_hub))
    def _():
        fill_leaving()
        for flight in gathers:
            flight.wait_send()
        swap.start()

    def seat_of(place):
        return jnp.where((place >> 4) == hub, 1, 0), jnp.minimum(place & 15, cap - 1)

    def choose(c):
        kind, side, half = chunks[c]
        gathers[c].wait_recv()
        for rel in (3, 2, 0):
            for s in range(OUT):
                q, k = seat_of(entry(served[rel], s, 4 + 2 * side + kind) & 63)
                picks[c][rel][s] = packed[c][q, k]
            sends[c][rel].start()

    def merge(c):
        kind, side, half = chunks[c]
        sends[c][3].wait_recv()
        for s in range(OUT):
            place = entry(partner, s, 4 + 2 * side + kind) & 63
            q, k = seat_of(place)
            picks[c][1][s] = jnp.where((place >> 5) == pair, packed[c][q, k], merged[c][s])
        sends[c][1].start()

    @pl.when(is_hub)
    def _():
        for c in range(PARTS + LAG):
            if c == RELAY:
                for i in range(EARLY):
                    reaches[i].wait_recv()
                    passes[i].start()
            if c < PARTS:
                choose(c)
            if c >= LAG:
                merge(c - LAG)

    hub_flag = jnp.where(is_hub, 1, 0)

    def whose(slot, column, shift):
        code = (tab[rows * 8 + slot, column] >> shift) & 63
        return jnp.where((code >> 5) == pair, 0, 1)

    def await_chunk(c):
        sends[c][0].wait_recv()
        on_hub(sends[c][2].wait_recv)

    for c in range(4):
        await_chunk(c)
    corner_group = tile_lane >> 4
    for s in range(OUT):
        low, high = whose(s, 0, 0) * hub_flag, whose(s, 2, 0) * hub_flag
        tiles = []
        for half in range(2):
            got = []
            for side, far, at in ((0, low, 8 - NEED), (1, high, 0)):
                c = 2 * half + side
                first, last = chosen[c][far, s, 0], chosen[c][far, s, 1]
                got.append(unpack_face(first, last, at, 1, 0, tile_row))
            tiles.append([jnp.where(tile_row >= 4, a, b) for a, b in zip(*got)])
            for f in range(5):
                halo[s, f, half] = tiles[half][f]
        for side in range(SIDES):
            source = tiles[0] if side else tiles[parts - 1]
            made = jnp.zeros((8, LANES), jnp.float32)
            for f in range(5):
                one = 0 if side else LANES - edge
                two = edge if side else LANES - 2 * edge
                inner = (tile_row == 3) | (tile_row == 4)
                tile = jnp.where(
                    inner,
                    turned(turned(source[f], 4, 0), edge * f - two, 1),
                    turned(source[f], edge * f - one, 1),
                )
                made = jnp.where(corner_group == f, tile, made)
            edge_packed[side][1, s] = made
    for side in range(SIDES):
        on_edge(edge_gathers[side].start)

    def choose_corner(side):
        edge_gathers[side].wait_recv()
        for rel in (2, 3, 1, 0):
            for s in range(OUT):
                place = (entry(served[rel], s, 5 + 2 * side) >> 6) & 63
                q, k = seat_of(place)
                edge_picks[side][rel][s] = edge_packed[side][q, jnp.minimum(k, OUT - 1)]
            edge_sends[side][rel].start()

    @pl.when(is_hub)
    def _():
        for side in range(SIDES):
            choose_corner(side)

    swap.wait_recv()

    @pl.when(is_hub)
    def _():
        hub_row, edge_row = served[2], served[3]
        onward = entry(edge_row, 0, 8)
        last = entry(edge_row, 0, 3) - onward
        hub_base = entry(hub_row, 0, 1)
        for i in range(SEND):
            k = jnp.where(
                i < onward,
                entry(edge_row, jnp.clip(last + i, 0, 7), 0),
                entry(hub_row, jnp.clip(hub_base + i - onward, 0, 7), 0),
            )
            far_out[i][...] = beside[jnp.clip((k & 15) - near_stay, 0, SEND - 1)]
            crossings[i].start()
            if EARLY <= i + AHEAD < SEND:
                reaches[i + AHEAD].start()

    for c in range(4, PARTS):
        await_chunk(c)
    for side in range(SIDES):
        for far in range(2):
            edge_sends[side][2 * far].wait_recv()

    filled = entry(my_row, 0, 3)
    onward = entry(pair * (rows - 1), 0, 8)
    far_stay = entry(rows - 1 - hub, 0, 2)
    first_far = jnp.where(is_hub, my_base - onward, filled - onward)

    def run(turn, carry):
        s = lax.rem(turn + OUT - 1, OUT)
        at_row, k = origin(my_row, s)
        mine = cells[jnp.minimum(k, cap - 1)]
        near = beside[jnp.clip(k - near_stay, 0, SEND - 1)]
        far_hub = at_row == rows - 1 - hub
        now[:, :edge, :flat] = jnp.where(at_row == my_row, mine, near)
        far_edge = at_row == (1 - pair) * (rows - 1)
        for i in range(SEND):

            @pl.when((s == i + 1) & is_hub)
            def _():
                crossings[i].wait_recv()
                if i < FORWARD:
                    relays[i].start()

            if i < FORWARD:

                @pl.when((s == i + LATE) & jnp.logical_not(is_hub))
                def _():
                    crossings[i].wait_recv()

            if i >= EARLY:

                @pl.when((s == i) & is_hub)
                def _():
                    reaches[i].wait_recv()
                    passes[i].start()

            @pl.when((s == i + 1) & jnp.logical_not(is_hub))
            def _():
                reaches[i].wait_recv()

            @pl.when((s > i) & (s < OUT - 1))
            def _():
                here = now[:, :edge, :flat]
                chosen_far = far_hub & (k - far_stay == i)
                now[:, :edge, :flat] = jnp.where(chosen_far, across[i][...], here)

            ready = jnp.where(is_hub, i + 1, i + LATE if i < FORWARD else OUT)

            @pl.when((s >= ready) & (s < OUT - 1))
            def _():
                here = now[:, :edge, :flat]
                chosen_far = far_edge & (s - first_far == i)
                now[:, :edge, :flat] = jnp.where(chosen_far, far_in[i][...], here)

        for f in range(5):
            for half in range(2):
                now[f, edge:, half * LANES : (half + 1) * LANES] = halo[s, f, half]
        low, high = whose(s, 1, 0) * hub_flag, whose(s, 3, 0) * hub_flag
        for half in range(2):
            got = []
            for side, far, at in ((0, low, LANES - NEED * edge), (1, high, 0)):
                c = 4 + 2 * half + side
                first, last = chosen[c][far, s, 0], chosen[c][far, s, 1]
                got.append(unpack_face(first, last, at, edge, 1, tile_lane))
            for f in range(5):
                now[f, half * 8 : (half + 1) * 8, flat:] = jnp.where(
                    tile_lane >= LANES // 2, got[0][f], got[1][f]
                )
        low = edge_chosen[0][whose(s, 1, 6), s]
        high = edge_chosen[1][whose(s, 3, 6), s]
        for f in range(5):
            a = turned(low, LANES - edge - edge * f, 1)
            b = turned(turned(low, 4, 0), LANES - 2 * edge - edge * f, 1)
            c = turned(high, -edge * f, 1)
            d = turned(turned(high, 4, 0), edge - edge * f, 1)
            tile = jnp.where(tile_lane < edge, c, d)
            tile = jnp.where(tile_lane >= LANES // 2, b, tile)
            now[f, edge:, flat:] = jnp.where(tile_lane >= LANES - edge, a, tile)
        for f, field in enumerate(conserved([now[f] for f in range(5)])):
            start[f] = field
            now[f] = field
        for step in range(3):
            cons = tuple(now[f] for f in range(5))
            change = twice_change(cons, edge, flat, step == 2)
            if step == 2:
                cons = cut(cons, edge, flat)
            moved = [c - (0.5 * DT) * d for c, d in zip(cons, change)]
            if step == 1:
                moved = [0.75 * start[f] + 0.25 * moved[f] for f in range(5)]
            if step == 2:
                moved = [
                    (1.0 / 3.0) * start[f, :edge, :flat] + (2.0 / 3.0) * moved[f] for f in range(5)
                ]
                rho = moved[0]
                vel = [m / rho for m in moved[1:4]]
                p = 0.4 * (
                    moved[4] - 0.5 * rho * (vel[0] * vel[0] + vel[1] * vel[1] + vel[2] * vel[2])
                )
                for f, field in enumerate((rho, *vel, p)):
                    out[s, f] = jnp.where(s < filled, field, 0.0)
            else:
                for f in range(5):
                    now[f] = moved[f]
        return carry

    lax.fori_loop(0, OUT, run, 0)
    swap.wait_send()

    @pl.when(is_hub)
    def _():
        for group in (*sends, *edge_sends, crossings, relays, reaches, passes):
            for flight in group:
                flight.wait_send()

    @pl.when(jnp.logical_not(is_hub))
    def _():
        for flight in edge_gathers:
            flight.wait_send()


def wide_body(rows, cols, block_cells, slot_blocks):
    cap = slot_blocks.shape[1]
    edge, flat = block_cells.shape[2:]
    block = (5, edge, flat)
    f32 = lambda *shape: pltpu.VMEM(shape, jnp.float32)
    face_tiles = (2, 8, LANES)
    grown = (5, edge + 8, flat + LANES)
    scratch = [pltpu.VMEM((2, cols, LANES), jnp.int32)]
    scratch += [space((rows * 8 + 8, LANES), jnp.int32) for space in (pltpu.VMEM, pltpu.SMEM)]
    scratch += [f32(2, cap, *face_tiles) for _ in range(PARTS)]
    scratch += [f32(2, OUT, *face_tiles) for _ in range(PARTS)]
    scratch += [f32(OUT, *face_tiles) for _ in range(4 * PARTS)]
    scratch += [f32(OUT, *face_tiles) for _ in range(PARTS)]
    scratch += [f32(2, OUT, 8, LANES) for _ in range(4)]
    scratch += [f32(OUT, 8, LANES) for _ in range(8)]
    scratch += [f32(SEND, *block) for _ in range(2)]
    scratch += [f32(*block) for _ in range(3 * SEND)]
    scratch += [f32(OUT, 5, 2, 8, LANES), f32(*grown), f32(*grown)]
    scratch += [pltpu.SemaphoreType.DMA((n,)) for n in (6 * PARTS + 32, 4 * PARTS + 32, 1)]
    return pl.pallas_call(
        functools.partial(wide_kernel, rows, cols, cap),
        out_shape=jax.ShapeDtypeStruct((OUT, *block), jnp.float32),
        in_specs=[
            pl.BlockSpec(memory_space=pltpu.VMEM),
            pl.BlockSpec(memory_space=pltpu.VMEM),
        ],
        out_specs=pl.BlockSpec(memory_space=pltpu.VMEM),
        scratch_shapes=scratch,
        compiler_params=pltpu.CompilerParams(
            collective_id=0, has_side_effects=True, vmem_limit_bytes=40 << 20
        ),
    )(slot_blocks.T, block_cells)


def solution(mesh):
    rows, cols = mesh.shape["row"], mesh.shape["col"]
    local = wide_body if (rows, cols) == (4, 8) else body
    return jax.shard_map(
        functools.partial(local, rows, cols),
        mesh=mesh,
        in_specs=(P(("row", "col"), None, None, None), P()),
        out_specs=P(("row", "col"), None, None, None),
        check_vma=False,
    )
```

```python
import functools

import jax
import jax.numpy as jnp
from jax import lax
from jax.experimental import pallas as pl
from jax.experimental.pallas import tpu as pltpu
from jax.sharding import PartitionSpec as P

MESH = pl.DeviceIdType.MESH
BLK_MEAN = 6
OUT = 7
SEND = BLK_MEAN - 1
LANES = 128
DT = 0.12


def make_tables(slot_blocks, rows, cols, my_row, my_col):
    cap = slot_blocks.shape[1]
    levels = rows.bit_length() - 1
    half = rows // 2
    group = BLK_MEAN * rows
    ids = slot_blocks.reshape(rows, cols, cap)
    counts = jnp.sum((ids >= 0).astype(jnp.int32), axis=2)
    row_ids = jnp.arange(rows, dtype=jnp.int32)
    col_ids = jnp.arange(cols, dtype=jnp.int32)
    at_row = jnp.broadcast_to(row_ids[:, None, None], ids.shape)
    at_slot = jnp.broadcast_to(jnp.arange(cap, dtype=jnp.int32), ids.shape)
    mine = (row_ids[:, None] == my_row) & (col_ids[None, :] == my_col)
    scalars = []
    for level in range(levels):
        bit = 1 << level
        other = counts.reshape(rows // (2 * bit), 2, bit, cols)[:, ::-1].reshape(rows, cols)
        send = jnp.maximum(counts - other, 0) // 2
        take = jnp.maximum(other - counts, 0) // 2
        keep = counts - send
        scalars.append(jnp.sum(jnp.where(mine, keep, 0)))
        hit = at_row[None] == row_ids[:, None, None, None]
        keep_here = jnp.sum(jnp.where(hit, keep[:, None, :, None], 0), axis=0)
        other_here = jnp.sum(jnp.where(hit, other[:, None, :, None], 0), axis=0)
        moved = at_slot >= keep_here
        at_row = jnp.where(moved, at_row ^ bit, at_row)
        at_slot = jnp.where(moved, other_here + at_slot - keep_here, at_slot)
        counts = keep + take
    scalars.append(jnp.sum(jnp.where(mine, counts, 0)))
    place = at_row * 16 + at_slot
    origin = row_ids[:, None, None] * 16 + jnp.arange(cap, dtype=jnp.int32)
    origin = jnp.broadcast_to(origin, ids.shape).reshape(-1)
    flat_ids = ids.reshape(-1)
    flat_place = jnp.where(flat_ids >= 0, place.reshape(-1), 0)
    flat_col = jnp.broadcast_to(col_ids[None, :, None], ids.shape).reshape(-1)
    near_far = jnp.stack([my_row, my_row ^ half])
    left, right = (my_col + cols - 1) % cols, (my_col + 1) % cols
    seat_rows = jnp.concatenate([near_far[:1], near_far, near_far])
    seat_cols = jnp.stack([my_col, right, right, left, left])
    seats = (seat_rows[:, None] * 16 + jnp.arange(OUT, dtype=jnp.int32)).reshape(-1, 1)
    seat_cols = jnp.repeat(seat_cols, OUT)[:, None]
    match = (flat_place[None] == seats) & (flat_col[None] == seat_cols) & (flat_ids >= 0)[None]
    along = jnp.sum(jnp.where(match, flat_ids[None] - flat_col[None] * group, 0), axis=1)
    along = along.reshape(5, OUT)
    here, there_right, there_left = along[:1], along[1:3], along[3:5]
    down, up = (lambda a: (a + group - 1) % group), (lambda a: (a + 1) % group)
    mine = jnp.concatenate([left * group + here, left * group + down(here)])
    mine = jnp.concatenate([mine, right * group + here, right * group + up(here)])
    theirs = jnp.concatenate([there_right, down(there_right), there_left, up(there_left)])
    wanted = jnp.concatenate([mine, theirs + my_col * group]).reshape(-1)
    both = flat_place * 4096 + origin
    found = jnp.sum(jnp.where(flat_ids[None] == wanted[:, None], both[None], 0), axis=1)
    source = found ^ (my_row * 16 * 4097)
    source = jnp.concatenate([source & 4095, source >> 12])
    return jnp.concatenate([jnp.stack(scalars), source])


def cell_values(cons):
    rho, mx, my, mz, energy = cons
    inv = 1.0 / rho
    vel = (mx * inv, my * inv, mz * inv)
    p = 0.4 * (energy - 0.5 * rho * (vel[0] * vel[0] + vel[1] * vel[1] + vel[2] * vel[2]))
    theta = p * inv
    sound = jnp.sqrt(1.4 * theta)
    kappa = 0.2 * jnp.exp(0.7 * jnp.log(theta))
    return vel, p, theta, sound, kappa


def conserved(primitive):
    rho, u, v, w, p = primitive
    energy = p / 0.4 + 0.5 * rho * (u * u + v * v + w * w)
    return (rho, rho * u, rho * v, rho * w, energy)


def direction_values(cons, values, normal):
    vel, p, theta, sound, kappa = values
    un = vel[normal]
    flux = [cons[1 + normal], cons[1] * un, cons[2] * un, cons[3] * un, (cons[4] + p) * un]
    flux[1 + normal] = flux[1 + normal] + p
    return (*cons, *flux, jnp.abs(un) + sound, theta, kappa)


def face(low, high):
    half_speed = 0.5 * jnp.maximum(low[10], high[10])
    out = [0.5 * (low[5 + i] + high[5 + i]) - half_speed * (high[i] - low[i]) for i in range(5)]
    out[4] = out[4] - 0.5 * (low[12] + high[12]) * (high[11] - low[11])
    return out


def block_rate(cons, ghost_x, ghost_y):
    edge, flat = cons[0].shape
    row = lax.broadcasted_iota(jnp.int32, (edge, flat), 0)
    lane = lax.broadcasted_iota(jnp.int32, (edge, flat), 1)
    values = cell_values(cons)
    mid = direction_values(cons, values, 0)
    gx = direction_values(ghost_x, cell_values(ghost_x), 0)
    last = row == edge - 1
    up = [
        jnp.where(last, jnp.concatenate([g, g], axis=0), pltpu.roll(m, edge - 1, 0))
        for m, g in zip(mid, gx)
    ]
    upper = face(mid, up)
    bottom = face(gx, [m[:8] for m in mid])
    change = [
        u - jnp.where(row == 0, jnp.concatenate([b, b], axis=0), pltpu.roll(u, 1, 0))
        for u, b in zip(upper, bottom)
    ]
    mid = direction_values(cons, values, 1)
    gy = direction_values(ghost_y, cell_values(ghost_y), 1)
    last = lane >= flat - edge
    up = [
        jnp.where(last, jnp.concatenate([g, g], axis=1), pltpu.roll(m, flat - edge, 1))
        for m, g in zip(mid, gy)
    ]
    upper = face(mid, up)
    bottom = face(gy, [m[:, :LANES] for m in mid])
    change = [
        t + (u - jnp.where(lane < edge, jnp.concatenate([b, b], axis=1), pltpu.roll(u, edge, 1)))
        for t, u, b in zip(change, upper, bottom)
    ]
    mid = direction_values(cons, values, 2)
    up = [pltpu.roll(m, flat - 1, 1) for m in mid]
    upper = face(mid, up)
    height = lane & (edge - 1)
    zero = jnp.zeros_like(values[1])
    wall = [zero, zero, zero, values[1], zero]
    change = [
        t
        + (
            jnp.where(height == edge - 1, w, u)
            - jnp.where(height == 0, w, pltpu.roll(u, 1, 1))
        )
        for t, u, w in zip(change, upper, wall)
    ]
    return [-t for t in change]


def y_units(n):
    return 2 * ((5 * n + 7) // 8)


def units(n):
    return y_units(n) + (10 * n + 7) // 8


def y_seat(slot, f):
    at = slot * 5 + f
    return 2 * (at >> 3), 16 * (at & 7)


def x_seat(n, slot, f, part):
    at = slot * 10 + 2 * f + part
    return y_units(n) + (at >> 3), at & 7


def kernel(rows, cols, cap, *refs):
    levels = rows.bit_length() - 1
    half = rows // 2
    refs = list(refs)
    tab, cells, out = refs[:3]
    refs = refs[3:]
    send_blocks = refs[:levels]
    recv_blocks = refs[levels : 2 * levels]
    refs = refs[2 * levels :]
    start, now = refs[:2]
    sections = [refs[2 + 10 * i : 12 + 10 * i] for i in range(3)]
    bsend, brecv, hsend, hrecv = refs[32:36]
    my_row, my_col = lax.axis_index("row"), lax.axis_index("col")
    left = (my_row, lax.rem(my_col + cols - 1, cols))
    right = (my_row, lax.rem(my_col + 1, cols))

    def partner(level):
        bit = 1 << level
        return (my_row + bit - 2 * bit * (lax.rem(my_row // bit, 2)), my_col)

    barrier = pltpu.get_barrier_semaphore()
    across = partner(levels - 1)[0]
    beside = [(right, left), ((across, right[1]), (across, left[1]))]
    for device in [*beside[0], *beside[1]] + [partner(level) for level in range(levels)]:
        pl.semaphore_signal(barrier, inc=1, device_id=device, device_id_type=MESH)
    pl.semaphore_wait(barrier, 4 + levels)

    def held(slot, depth):
        value = cells[jnp.minimum(slot, cap - 1)]
        for level in range(depth):
            keep = tab[level]
            got = recv_blocks[level][jnp.clip(slot - keep, 0, SEND - 1)]
            value = jnp.where(slot >= keep, got, value)
        return value

    edge, flat = now.shape[2:]
    tile_lane = lax.broadcasted_iota(jnp.int32, (edge, LANES), 1)
    tile_group = tile_lane >> 4
    ghost_row = lax.broadcasted_iota(jnp.int32, (8, 2 * LANES), 0)

    def tile_of(ref, *seat):
        *lead, unit = seat
        return ref[(*lead, pl.ds(unit, 2))].reshape(edge, LANES)

    def put_tile(ref, unit, tile):
        ref[unit : unit + 2] = tile.reshape(2, 8, LANES)

    def move_blocks(level):
        for k in range(SEND):
            send_blocks[level][k] = held(tab[level] + k, level)
        copy = pltpu.make_async_remote_copy(
            src_ref=send_blocks[level],
            dst_ref=recv_blocks[level],
            send_sem=bsend.at[level],
            recv_sem=brecv.at[level],
            device_id=partner(level),
            device_id_type=MESH,
        )
        copy.start()
        return copy

    def remote(step, at, src, dst, device):
        copy = pltpu.make_async_remote_copy(
            src_ref=src,
            dst_ref=dst,
            send_sem=hsend.at[step, at],
            recv_sem=hrecv.at[step, at],
            device_id=device,
            device_id_type=MESH,
        )
        copy.start()
        return copy

    def pack(blocks, n, buffer, high):
        x = edge - 1 if high else 0
        side = slice(LANES, 2 * LANES) if high else slice(0, LANES)
        for first in range(0, 5 * n, 8):
            tile = None
            for at in range(first, min(first + 8, 5 * n)):
                s, f = at // 5, at % 5
                shift = (edge * (at - first) + (edge if high else 0)) % LANES
                piece = blocks[s, f, :, side]
                piece = pltpu.roll(piece, shift, 1) if shift else piece
                tile = piece if tile is None else jnp.where(tile_group == at - first, piece, tile)
            put_tile(buffer, 2 * (first // 8), tile)
        for s in range(n):
            for f in range(5):
                for part in range(2):
                    unit, row = x_seat(n, s, f, part)
                    buffer[unit, row : row + 1, :] = blocks[
                        s, f, x : x + 1, part * LANES : (part + 1) * LANES
                    ]

    base = levels + 1

    def entry(step, kind, far, slot):
        at = kind * OUT if far is None else 4 * OUT + (kind * 2 + far) * OUT
        return tab[base + (12 * OUT if step else 0) + at + slot]

    def near_seat(code):
        return jnp.minimum(code >> 4, half - 1), code & 15

    def select(step, n, known, pick, first_kind, far):
        for s in range(OUT):
            q, sigma = near_seat(entry(step, first_kind, far, s))
            for f in range(5):
                for part in range(2):
                    unit, row = x_seat(n, sigma, f, part)
                    to, at = x_seat(OUT, s, f, part)
                    pick[to, at : at + 1, :] = known[q, unit, pl.ds(row, 1), :]
        seats = [near_seat(entry(step, first_kind + 1, far, s)) for s in range(OUT)]
        for first in range(0, 5 * OUT, 8):
            tile = None
            for at in range(first, min(first + 8, 5 * OUT)):
                q, sigma = seats[at // 5]
                unit, lane = y_seat(sigma, at % 5)
                shift = (edge * (at - first) + LANES - lane) & (LANES - 1)
                piece = pltpu.roll(tile_of(known, q, unit), shift, 1)
                tile = piece if tile is None else jnp.where(tile_group == at - first, piece, tile)
            put_tile(pick, 2 * (first // 8), tile)

    def begin(step, blocks, n):
        flights = []
        for side in range(2):
            known = sections[step][side]
            pack(blocks, n, known.at[0], side == 0)
            if levels > 1:
                flights.append(remote(step, side, known.at[0], known.at[1], partner(0)))
        return flights

    def gather(step, flights):
        for level in range(1, levels - 1):
            size = 1 << level
            for side in range(2):
                known = sections[step][side]
                flights[side].wait()
                flights[side] = remote(
                    step,
                    2 * level + side,
                    known.at[pl.ds(0, size)],
                    known.at[pl.ds(size, size)],
                    partner(level),
                )
        return flights

    def trade(step, n, flights):
        sent = []
        for side in range(2):
            if flights:
                flights[side].wait()
            for far in (1, 0):
                known, pick, sel = (sections[step][at] for at in (side, 2 + 2 * side + far, 6 + 2 * side + far))
                select(step, n, known, pick, 2 * side, far)
                at = 2 * (levels - 1) + 2 * side + far
                sent.append(remote(step, at, pick, sel, beside[far][side]))
        return sent

    def open_block(slot, carry):
        value = held(slot, levels)
        for f, field in enumerate(conserved([value[f] for f in range(5)])):
            start[slot, f] = field
            now[slot, f] = field
        return carry

    def advance(step):
        lo_near, lo_far, hi_near, hi_far = sections[step][6:]

        def run(slot, carry):
            def near(kind):
                return entry(step, kind, None, slot) < 16 * half

            def x_row(close, away, kind, f):
                parts = []
                for part in range(2):
                    unit, row = x_seat(OUT, slot, f, part)
                    a = close[unit, pl.ds(row, 1), :]
                    b = away[unit, pl.ds(row, 1), :]
                    parts.append(jnp.where(near(kind), a, b))
                return jnp.concatenate(parts, axis=1)

            def y_tile(close, away, kind, f, to):
                unit, lane = y_seat(slot, f)
                tile = jnp.where(near(kind), tile_of(close, unit), tile_of(away, unit))
                return pltpu.roll(tile, (LANES + to - lane) & (LANES - 1), 1)

            ghost_x, ghost_y = [], []
            for f in range(5):
                low = x_row(lo_near, lo_far, 0, f)
                high = x_row(hi_near, hi_far, 2, f)
                ghost_x.append(jnp.where(ghost_row == 0, low, high))
                low = y_tile(lo_near, lo_far, 1, f, 0)
                high = y_tile(hi_near, hi_far, 3, f, LANES - edge)
                ghost_y.append(jnp.where(tile_lane < edge, low, high))
            if step == 0:
                ghost_x, ghost_y = conserved(ghost_x), conserved(ghost_y)
            cons = tuple(now[slot, f] for f in range(5))
            rate = block_rate(cons, tuple(ghost_x), tuple(ghost_y))
            moved = [c + DT * d for c, d in zip(cons, rate)]
            if step == 1:
                moved = [0.75 * start[slot, f] + 0.25 * moved[f] for f in range(5)]
            if step == 2:
                moved = [(1.0 / 3.0) * start[slot, f] + (2.0 / 3.0) * moved[f] for f in range(5)]
                rho = moved[0]
                vel = [m / rho for m in moved[1:4]]
                p = 0.4 * (
                    moved[4] - 0.5 * rho * (vel[0] * vel[0] + vel[1] * vel[1] + vel[2] * vel[2])
                )
                filled = slot < tab[levels]
                for f, field in enumerate((rho, *vel, p)):
                    out[slot, f] = jnp.where(filled, field, 0.0)
            else:
                for f in range(5):
                    now[slot, f] = moved[f]
            return carry

        lax.fori_loop(0, OUT, run, 0)

    moving = move_blocks(0)
    flights = begin(0, cells, cap)
    flights = gather(0, flights)
    for level in range(1, levels):
        moving.wait()
        moving = move_blocks(level)
    flights = trade(0, cap, flights)
    moving.wait()
    lax.fori_loop(0, OUT, open_block, 0)
    for step in range(3):
        if step:
            flights = trade(step, OUT, gather(step, begin(step, now, OUT)))
        for flight in flights:
            flight.wait()
        advance(step)


def body(rows, cols, block_cells, slot_blocks):
    cap = slot_blocks.shape[1]
    levels = rows.bit_length() - 1
    half = rows // 2
    edge, flat = block_cells.shape[2:]
    table = make_tables(slot_blocks, rows, cols, lax.axis_index("row"), lax.axis_index("col"))
    block = (5, edge, flat)
    scratch = [pltpu.VMEM((SEND, *block), jnp.float32) for _ in range(2 * levels)]
    scratch += [pltpu.VMEM((OUT, *block), jnp.float32) for _ in range(2)]
    for step in range(3):
        faces = (units(OUT if step else cap), 8, LANES)
        picked = (units(OUT), 8, LANES)
        scratch += [pltpu.VMEM((half, *faces), jnp.float32) for _ in range(2)]
        scratch += [pltpu.VMEM(picked, jnp.float32) for _ in range(8)]
    scratch += [pltpu.SemaphoreType.DMA((levels,)) for _ in range(2)]
    scratch += [pltpu.SemaphoreType.DMA((3, 2 * (levels + 1))) for _ in range(2)]
    return pl.pallas_call(
        functools.partial(kernel, rows, cols, cap),
        out_shape=jax.ShapeDtypeStruct((OUT, *block), jnp.float32),
        in_specs=[
            pl.BlockSpec(memory_space=pltpu.SMEM),
            pl.BlockSpec(memory_space=pltpu.VMEM),
        ],
        out_specs=pl.BlockSpec(memory_space=pltpu.VMEM),
        scratch_shapes=scratch,
        compiler_params=pltpu.CompilerParams(
            collective_id=0, has_side_effects=True, vmem_limit_bytes=32 << 20
        ),
    )(table, block_cells)


SIDES = 2
NEED = 3
PARTS = 8
LAG = 4
EARLY = 4
AHEAD = 2
FORWARD = 2
LATE = 3
RELAY = 4


def swap_lanes(a, lane, step):
    size = a.shape[1]
    return jnp.where((lane & step) == 0, pltpu.roll(a, size - step, 1), pltpu.roll(a, step, 1))


def seat_tables(slots, scratch, rows, cols, my_row, my_col):
    cap, devices = slots.shape
    slots = jnp.concatenate([slots, jnp.zeros((16 - cap, devices), jnp.int32)], axis=0)
    slots = jnp.concatenate([slots, jnp.zeros((16, LANES - devices), jnp.int32)], axis=1)
    slots = jnp.transpose(slots)[:devices, :cap]
    group = BLK_MEAN * rows
    span = 16 * rows
    lane = lax.broadcasted_iota(jnp.int32, (cols, LANES), 1)
    col = lax.broadcasted_iota(jnp.int32, (cols, LANES), 0)
    row, slot = (lane >> 4) & (rows - 1), lane & 15
    ids = jnp.full((cols, LANES), -1, jnp.int32)
    for r in range(rows):
        part = slots[r * cols : (r + 1) * cols, :]
        part = jnp.concatenate([part, jnp.full((cols, LANES - cap), -1, jnp.int32)], axis=1)
        part = jnp.where(lane < span, part, pltpu.roll(part, span, 1))
        part = pltpu.roll(part, 16 * r, 1) if r else part
        ids = jnp.where(row == r, part, ids)
    held = ids >= 0
    counts = jnp.where(held, 1, 0)
    for step in (1, 2, 4, 8):
        counts = counts + swap_lanes(counts, lane, step)
    other = swap_lanes(counts, lane, 16)
    keep = counts - (jnp.maximum(counts - other, 0) >> 1)
    crossed = slot >= keep
    at_row = jnp.where(crossed, row ^ 1, row)
    at_slot = jnp.where(crossed, other + slot - keep, slot)
    counts = keep + (jnp.maximum(other - counts, 0) >> 1)
    other = swap_lanes(counts, lane, 32)
    keep = counts - (jnp.maximum(counts - other, 0) >> 1)
    keep = jnp.where(crossed, swap_lanes(keep, lane, 16), keep)
    other = jnp.where(crossed, swap_lanes(other, lane, 16), other)
    crossed = at_slot >= keep
    at_row = jnp.where(crossed, at_row ^ 2, at_row)
    at_slot = jnp.where(crossed, other + at_slot - keep, at_slot)
    held = held & (lane < span)
    scratch[0] = jnp.where(held, ids - col * group, -100)
    scratch[1] = jnp.where(held, at_row * 16 + at_slot, -100)

    def line(kind, c, n):
        return jnp.broadcast_to(scratch[kind, pl.ds(c, 1), :], (n, LANES))

    def total(mask, value):
        return jnp.sum(jnp.where(mask, value, 0), axis=1, keepdims=True)

    def down(j):
        return jnp.where(j <= 0, j + group - 1, j - 1)

    def up(j):
        return jnp.where(j >= group - 1, j + 1 - group, j + 1)

    left, right = lax.rem(my_col + cols - 1, cols), lax.rem(my_col + 1, cols)
    n = rows * 8
    seat = lax.broadcasted_iota(jnp.int32, (n, LANES), 0)
    lane = lax.broadcasted_iota(jnp.int32, (n, LANES), 1)
    to_row, target = seat >> 3, (seat >> 3) * 16 + (seat & 7)
    j_here, f_here = line(0, my_col, n), line(1, my_col, n)
    code = lane + 64 * f_here
    on = (f_here >> 4) == to_row
    columns = [
        total(f_here == target, lane),
        total(on & ((lane >> 5) == (to_row >> 1)), 1),
        total(on & ((lane >> 4) == to_row), 1),
        total(on, 1),
    ]
    for c, moved in ((right, down), (left, up)):
        j = total(line(1, c, n) == target, line(0, c, n) + 1) - 1
        columns.append(total(j_here == j, code))
        columns.append(total(j_here == moved(j), code))
    columns.append(total(on & ((lane >> 4) == rows - 1 - to_row), 1))
    first = jnp.zeros((n, LANES), jnp.int32)
    for at, value in enumerate(columns):
        first = jnp.where(lane == at, value, first)
    seat = lax.broadcasted_iota(jnp.int32, (8, LANES), 0)
    lane = lax.broadcasted_iota(jnp.int32, (8, LANES), 1)
    j = total(line(1, my_col, 8) == my_row * 16 + seat, line(0, my_col, 8) + 1) - 1
    second = jnp.zeros((8, LANES), jnp.int32)
    for at, (c, key) in enumerate(((left, j), (left, down(j)), (right, j), (right, up(j)))):
        value = total(line(0, c, 8) == key, lane + 64 * line(1, c, 8))
        second = jnp.where(lane == at, value, second)
    return jnp.concatenate([first, second], axis=0)


def turned(tile, shift, axis):
    shift %= tile.shape[axis]
    return pltpu.roll(tile, shift, axis) if shift else tile


def pack_face(pieces, at, unit, axis, index):
    a, b, c, d, e = pieces
    first = jnp.where(index < 3 * unit, turned(a, -at, axis), turned(b, 3 * unit - at, axis))
    first = jnp.where(index < 6 * unit, first, turned(c, 6 * unit - at, axis))
    last = jnp.where(index < 3 * unit, turned(d, -at, axis), turned(e, 3 * unit - at, axis))
    last = jnp.where(index < 6 * unit, last, turned(c, 4 * unit - at, axis))
    return first, last


def unpack_face(first, last, at, unit, axis, index):
    third = jnp.where(
        index < at + 2 * unit,
        turned(first, at - 6 * unit, axis),
        turned(last, at - 4 * unit, axis),
    )
    return (
        turned(first, at, axis),
        turned(first, at - 3 * unit, axis),
        third,
        turned(last, at, axis),
        turned(last, at - 3 * unit, axis),
    )


def twice_face(low, high):
    speed = jnp.maximum(low[10], high[10])
    out = [(low[5 + i] + high[5 + i]) - speed * (high[i] - low[i]) for i in range(5)]
    out[4] = out[4] - (low[12] + high[12]) * (high[11] - low[11])
    return out


def rolled_side(mid, un, normal, roll):
    cons, un = [roll(m) for m in mid[:5]], roll(un)
    speed, theta, kappa = (roll(m) for m in mid[10:])
    p = theta * cons[0]
    flux = [cons[1 + normal], cons[1] * un, cons[2] * un, cons[3] * un, (cons[4] + p) * un]
    flux[1 + normal] = flux[1 + normal] + p
    return (*cons, *flux, speed, theta, kappa)


def cut(values, height, width):
    if isinstance(values, (tuple, list)):
        return tuple(cut(v, height, width) for v in values)
    return values[:height, :width]


def twice_change(cons, edge, flat, last):
    rows, lanes = cons[0].shape
    values = cell_values(cons)
    change = None
    for normal, axis, step in ((0, 0, 1), (1, 1, edge), (2, 1, 1)):
        tall = edge if last and normal else rows
        wide = flat if last and normal != 1 else lanes
        here = cut(values, tall, wide)
        mid = direction_values(cut(cons, tall, wide), here, normal)
        size = (tall, wide)[axis]
        roll = functools.partial(pltpu.roll, shift=size - step, axis=axis)
        upper = twice_face(mid, rolled_side(mid, here[0][normal], normal, roll))
        if normal == 2:
            height = lax.broadcasted_iota(jnp.int32, (tall, wide), 1) & (edge - 1)
            wall = 2.0 * here[1]
            walls = [0.0, 0.0, 0.0, wall, 0.0]
            upper = [jnp.where(height == edge - 1, w, u) for u, w in zip(upper, walls)]
        lower = [pltpu.roll(u, step, axis) for u in upper]
        if normal == 2:
            lower[3] = jnp.where(height == 0, wall, lower[3])
        delta = [u - l for u, l in zip(upper, lower)]
        delta = cut(delta, edge, flat) if last else delta
        change = delta if change is None else [t + d for t, d in zip(change, delta)]
    return change


def wide_kernel(rows, cols, cap, slots, cells, out, *refs):
    refs = list(refs)
    take = lambda n: [refs.pop(0) for _ in range(n)]
    (lines, seats, tab) = take(3)
    packed, chosen, picks = take(PARTS), take(PARTS), [take(4) for _ in range(PARTS)]
    merged = take(PARTS)
    edge_packed, edge_chosen, edge_picks = take(2), take(2), [take(4) for _ in range(2)]
    (leaving, beside) = take(2)
    across, far_out, far_in = take(SEND), take(SEND), take(SEND)
    (halo, start, now) = take(3)
    (ssem, rsem, lsem) = take(3)
    edge, flat = out.shape[2:]
    parts = flat // LANES
    my_row, my_col = lax.axis_index("row"), lax.axis_index("col")
    left, right = lax.rem(my_col + cols - 1, cols), lax.rem(my_col + 1, cols)
    pair = my_row // 2
    partner = my_row + 1 - 2 * lax.rem(my_row, 2)
    is_hub = my_row == 1 + pair
    hub = 1 + pair
    served = [my_row, partner, rows - 1 - my_row, lax.rem(my_row + 2, rows)]
    toward = [right, left]

    barrier = pltpu.get_barrier_semaphore()
    for step in range(1, rows):
        device = (lax.rem(my_row + step, rows), my_col)
        pl.semaphore_signal(barrier, inc=1, device_id=device, device_id_type=MESH)
    for step in range(rows):
        for c in toward:
            device = (lax.rem(my_row + step, rows), c)
            pl.semaphore_signal(barrier, inc=1, device_id=device, device_id_type=MESH)
    seats[...] = seat_tables(slots[...], lines, rows, cols, my_row, my_col)
    seating = pltpu.make_async_copy(seats, tab, lsem.at[0])
    seating.start()

    def remote(src, dst, send, recv, device):
        return pltpu.make_async_remote_copy(
            src_ref=src,
            dst_ref=dst,
            send_sem=ssem.at[send],
            recv_sem=rsem.at[recv],
            device_id=device,
            device_id_type=MESH,
        )

    tile_row = lax.broadcasted_iota(jnp.int32, (8, LANES), 0)
    tile_lane = lax.broadcasted_iota(jnp.int32, (8, LANES), 1)
    tall_lane = lax.broadcasted_iota(jnp.int32, (edge, LANES), 1)
    chunks = [(k, side, half) for k in range(2) for half in range(2) for side in range(SIDES)]

    def pack(chunk):
        kind, side, half = chunks[chunk]
        for k in range(cap):
            if kind == 0:
                at = 0 if side else 8 - NEED
                rows_at = pl.ds(0 if side else edge - 8, 8)
                pieces = [cells[k, f, rows_at, half * LANES : (half + 1) * LANES] for f in range(5)]
                made = pack_face(pieces, at, 1, 0, tile_row)
            else:
                at = 0 if side else LANES - NEED * edge
                lanes_at = pl.ds(0 if side else flat - LANES, LANES)
                pieces = [cells[k, f, half * 8 : (half + 1) * 8, lanes_at] for f in range(5)]
                made = pack_face(pieces, at, edge, 1, tile_lane)
            for which in range(2):
                packed[chunk][1, k, which] = made[which]

    used = [0, 0]

    def number(send):
        used[send] += 1
        return used[send] - 1

    def to_rows(source, into, column, through=None):
        recv = [number(0) for _ in range(3)]
        flights = []
        for rel in range(4):
            far, device = rel // 2, (served[rel], column)
            target = into.at[far]
            if rel == 3 and through is not None:
                far, device, target = 2, (served[2], my_col), through
            flights.append(remote(source[rel], target, number(1), recv[far], device))
        return flights

    gathers = [
        remote(p.at[1], p.at[0], number(1), number(0), (partner, my_col))
        for p in (*packed, *edge_packed)
    ]
    gathers, edge_gathers = gathers[:PARTS], gathers[PARTS:]
    sends = [
        to_rows(picks[c], chosen[c], toward[chunks[c][1]], merged[c]) for c in range(PARTS)
    ]
    edge_sends = [
        to_rows(edge_picks[i], edge_chosen[i], toward[i]) for i in range(SIDES)
    ]
    swap = remote(leaving, beside, number(1), number(0), (partner, my_col))
    other_hub = (rows - 1 - my_row, my_col)
    reaches, passes, crossings, relays = [], [], [], []
    for i in range(SEND):
        recv = number(0)
        reaches.append(remote(leaving.at[i], across[i], number(1), recv, other_hub))
        passes.append(remote(across[i], across[i], number(1), recv, (partner, my_col)))
    for i in range(SEND):
        recv = number(0)
        crossings.append(remote(far_out[i], far_in[i], number(1), recv, other_hub))
        if i < FORWARD:
            relays.append(remote(far_in[i], far_in[i], number(1), recv, (partner, my_col)))

    def on_hub(do):
        pl.when(is_hub)(do)

    def on_edge(do):
        pl.when(jnp.logical_not(is_hub))(do)

    pack(0)
    pl.semaphore_wait(barrier, 3 * rows - 1)
    on_edge(gathers[0].start)
    seating.wait()

    def entry(row, slot, column):
        return tab[row * 8 + slot, column]

    def origin(row, slot):
        code = entry(row, slot, 0)
        return code >> 4, code & 15

    my_stay = entry(my_row, 0, 2)
    near_stay = entry(partner, 0, 2)
    my_base = entry(my_row, 0, 1)

    def fill_leaving():
        for i in range(SEND):
            leaving[i] = cells[jnp.minimum(my_stay + i, cap - 1)]

    @pl.when(is_hub)
    def _():
        fill_leaving()
        for flight in reaches[:EARLY]:
            flight.start()
        swap.start()

    for c in range(1, PARTS):
        pack(c)
        on_edge(gathers[c].start)

    @pl.when(jnp.logical_not(is_hub))
    def _():
        fill_leaving()
        for flight in gathers:
            flight.wait_send()
        swap.start()

    def seat_of(place):
        return jnp.where((place >> 4) == hub, 1, 0), jnp.minimum(place & 15, cap - 1)

    def choose(c):
        kind, side, half = chunks[c]
        gathers[c].wait_recv()
        for rel in (3, 2, 0):
            for s in range(OUT):
                q, k = seat_of(entry(served[rel], s, 4 + 2 * side + kind) & 63)
                picks[c][rel][s] = packed[c][q, k]
            sends[c][rel].start()

    def merge(c):
        kind, side, half = chunks[c]
        sends[c][3].wait_recv()
        for s in range(OUT):
            place = entry(partner, s, 4 + 2 * side + kind) & 63
            q, k = seat_of(place)
            picks[c][1][s] = jnp.where((place >> 5) == pair, packed[c][q, k], merged[c][s])
        sends[c][1].start()

    @pl.when(is_hub)
    def _():
        for c in range(PARTS + LAG):
            if c == RELAY:
                for i in range(EARLY):
                    reaches[i].wait_recv()
                    passes[i].start()
            if c < PARTS:
                choose(c)
            if c >= LAG:
                merge(c - LAG)

    hub_flag = jnp.where(is_hub, 1, 0)

    def whose(slot, column, shift):
        code = (tab[rows * 8 + slot, column] >> shift) & 63
        return jnp.where((code >> 5) == pair, 0, 1)

    def await_chunk(c):
        sends[c][0].wait_recv()
        on_hub(sends[c][2].wait_recv)

    swap.wait_recv()

    @pl.when(is_hub)
    def _():
        hub_row, edge_row = served[2], served[3]
        onward = entry(edge_row, 0, 8)
        last = entry(edge_row, 0, 3) - onward
        hub_base = entry(hub_row, 0, 1)
        for i in range(SEND):
            k = jnp.where(
                i < onward,
                entry(edge_row, jnp.clip(last + i, 0, 7), 0),
                entry(hub_row, jnp.clip(hub_base + i - onward, 0, 7), 0),
            )
            far_out[i][...] = beside[jnp.clip((k & 15) - near_stay, 0, SEND - 1)]

    for c in range(4):
        await_chunk(c)
    corner_group = tile_lane >> 4
    for s in range(OUT):
        low, high = whose(s, 0, 0) * hub_flag, whose(s, 2, 0) * hub_flag
        tiles = []
        for half in range(2):
            got = []
            for side, far, at in ((0, low, 8 - NEED), (1, high, 0)):
                c = 2 * half + side
                first, last = chosen[c][far, s, 0], chosen[c][far, s, 1]
                got.append(unpack_face(first, last, at, 1, 0, tile_row))
            tiles.append([jnp.where(tile_row >= 4, a, b) for a, b in zip(*got)])
            for f in range(5):
                halo[s, f, half] = tiles[half][f]
        for side in range(SIDES):
            source = tiles[0] if side else tiles[parts - 1]
            made = jnp.zeros((8, LANES), jnp.float32)
            for f in range(5):
                one = 0 if side else LANES - edge
                two = edge if side else LANES - 2 * edge
                inner = (tile_row == 3) | (tile_row == 4)
                tile = jnp.where(
                    inner,
                    turned(turned(source[f], 4, 0), edge * f - two, 1),
                    turned(source[f], edge * f - one, 1),
                )
                made = jnp.where(corner_group == f, tile, made)
            edge_packed[side][1, s] = made
    for side in range(SIDES):
        on_edge(edge_gathers[side].start)

    def choose_corner(side):
        edge_gathers[side].wait_recv()
        for rel in (2, 3, 1, 0):
            for s in range(OUT):
                place = (entry(served[rel], s, 5 + 2 * side) >> 6) & 63
                q, k = seat_of(place)
                edge_picks[side][rel][s] = edge_packed[side][q, jnp.minimum(k, OUT - 1)]
            edge_sends[side][rel].start()

    @pl.when(is_hub)
    def _():
        for side in range(SIDES):
            choose_corner(side)

    @pl.when(is_hub)
    def _():
        for i in range(SEND):
            crossings[i].start()
            if EARLY <= i + AHEAD < SEND:
                reaches[i + AHEAD].start()

    for c in range(4, PARTS):
        await_chunk(c)
    for side in range(SIDES):
        for far in range(2):
            edge_sends[side][2 * far].wait_recv()

    filled = entry(my_row, 0, 3)
    onward = entry(pair * (rows - 1), 0, 8)
    far_stay = entry(rows - 1 - hub, 0, 2)
    first_far = jnp.where(is_hub, my_base - onward, filled - onward)

    def run(turn, carry):
        s = lax.rem(turn + OUT - 1, OUT)
        at_row, k = origin(my_row, s)
        mine = cells[jnp.minimum(k, cap - 1)]
        near = beside[jnp.clip(k - near_stay, 0, SEND - 1)]
        far_hub = at_row == rows - 1 - hub
        now[:, :edge, :flat] = jnp.where(at_row == my_row, mine, near)
        far_edge = at_row == (1 - pair) * (rows - 1)
        for i in range(SEND):

            @pl.when((s == i + 1) & is_hub)
            def _():
                crossings[i].wait_recv()
                if i < FORWARD:
                    relays[i].start()

            if i < FORWARD:

                @pl.when((s == i + LATE) & jnp.logical_not(is_hub))
                def _():
                    crossings[i].wait_recv()

            if i >= EARLY:

                @pl.when((s == i) & is_hub)
                def _():
                    reaches[i].wait_recv()
                    passes[i].start()

            @pl.when((s == i + 1) & jnp.logical_not(is_hub))
            def _():
                reaches[i].wait_recv()

            @pl.when((s > i) & (s < OUT - 1))
            def _():
                here = now[:, :edge, :flat]
                chosen_far = far_hub & (k - far_stay == i)
                now[:, :edge, :flat] = jnp.where(chosen_far, across[i][...], here)

            ready = jnp.where(is_hub, i + 1, i + LATE if i < FORWARD else OUT)

            @pl.when((s >= ready) & (s < OUT - 1))
            def _():
                here = now[:, :edge, :flat]
                chosen_far = far_edge & (s - first_far == i)
                now[:, :edge, :flat] = jnp.where(chosen_far, far_in[i][...], here)

        for f in range(5):
            for half in range(2):
                now[f, edge:, half * LANES : (half + 1) * LANES] = halo[s, f, half]
        low, high = whose(s, 1, 0) * hub_flag, whose(s, 3, 0) * hub_flag
        for half in range(2):
            got = []
            for side, far, at in ((0, low, LANES - NEED * edge), (1, high, 0)):
                c = 4 + 2 * half + side
                first, last = chosen[c][far, s, 0], chosen[c][far, s, 1]
                got.append(unpack_face(first, last, at, edge, 1, tile_lane))
            for f in range(5):
                now[f, half * 8 : (half + 1) * 8, flat:] = jnp.where(
                    tile_lane >= LANES // 2, got[0][f], got[1][f]
                )
        low = edge_chosen[0][whose(s, 1, 6), s]
        high = edge_chosen[1][whose(s, 3, 6), s]
        for f in range(5):
            a = turned(low, LANES - edge - edge * f, 1)
            b = turned(turned(low, 4, 0), LANES - 2 * edge - edge * f, 1)
            c = turned(high, -edge * f, 1)
            d = turned(turned(high, 4, 0), edge - edge * f, 1)
            tile = jnp.where(tile_lane < edge, c, d)
            tile = jnp.where(tile_lane >= LANES // 2, b, tile)
            now[f, edge:, flat:] = jnp.where(tile_lane >= LANES - edge, a, tile)
        for f, field in enumerate(conserved([now[f] for f in range(5)])):
            start[f] = field
            now[f] = field
        for step in range(3):
            cons = tuple(now[f] for f in range(5))
            change = twice_change(cons, edge, flat, step == 2)
            if step == 2:
                cons = cut(cons, edge, flat)
            moved = [c - (0.5 * DT) * d for c, d in zip(cons, change)]
            if step == 1:
                moved = [0.75 * start[f] + 0.25 * moved[f] for f in range(5)]
            if step == 2:
                moved = [
                    (1.0 / 3.0) * start[f, :edge, :flat] + (2.0 / 3.0) * moved[f] for f in range(5)
                ]
                rho = moved[0]
                vel = [m / rho for m in moved[1:4]]
                p = 0.4 * (
                    moved[4] - 0.5 * rho * (vel[0] * vel[0] + vel[1] * vel[1] + vel[2] * vel[2])
                )
                for f, field in enumerate((rho, *vel, p)):
                    out[s, f] = jnp.where(s < filled, field, 0.0)
            else:
                for f in range(5):
                    now[f] = moved[f]
        return carry

    lax.fori_loop(0, OUT, run, 0)
    swap.wait_send()

    @pl.when(is_hub)
    def _():
        for group in (*sends, *edge_sends, crossings, relays, reaches, passes):
            for flight in group:
                flight.wait_send()

    @pl.when(jnp.logical_not(is_hub))
    def _():
        for flight in edge_gathers:
            flight.wait_send()


def wide_body(rows, cols, block_cells, slot_blocks):
    cap = slot_blocks.shape[1]
    edge, flat = block_cells.shape[2:]
    block = (5, edge, flat)
    f32 = lambda *shape: pltpu.VMEM(shape, jnp.float32)
    face_tiles = (2, 8, LANES)
    grown = (5, edge + 8, flat + LANES)
    scratch = [pltpu.VMEM((2, cols, LANES), jnp.int32)]
    scratch += [space((rows * 8 + 8, LANES), jnp.int32) for space in (pltpu.VMEM, pltpu.SMEM)]
    scratch += [f32(2, cap, *face_tiles) for _ in range(PARTS)]
    scratch += [f32(2, OUT, *face_tiles) for _ in range(PARTS)]
    scratch += [f32(OUT, *face_tiles) for _ in range(4 * PARTS)]
    scratch += [f32(OUT, *face_tiles) for _ in range(PARTS)]
    scratch += [f32(2, OUT, 8, LANES) for _ in range(4)]
    scratch += [f32(OUT, 8, LANES) for _ in range(8)]
    scratch += [f32(SEND, *block) for _ in range(2)]
    scratch += [f32(*block) for _ in range(3 * SEND)]
    scratch += [f32(OUT, 5, 2, 8, LANES), f32(*grown), f32(*grown)]
    scratch += [pltpu.SemaphoreType.DMA((n,)) for n in (6 * PARTS + 32, 4 * PARTS + 32, 1)]
    return pl.pallas_call(
        functools.partial(wide_kernel, rows, cols, cap),
        out_shape=jax.ShapeDtypeStruct((OUT, *block), jnp.float32),
        in_specs=[
            pl.BlockSpec(memory_space=pltpu.VMEM),
            pl.BlockSpec(memory_space=pltpu.VMEM),
        ],
        out_specs=pl.BlockSpec(memory_space=pltpu.VMEM),
        scratch_shapes=scratch,
        compiler_params=pltpu.CompilerParams(
            collective_id=0, has_side_effects=True, vmem_limit_bytes=40 << 20
        ),
    )(slot_blocks.T, block_cells)


def solution(mesh):
    rows, cols = mesh.shape["row"], mesh.shape["col"]
    local = wide_body if (rows, cols) == (4, 8) else body
    return jax.shard_map(
        functools.partial(local, rows, cols),
        mesh=mesh,
        in_specs=(P(("row", "col"), None, None, None), P()),
        out_specs=P(("row", "col"), None, None, None),
        check_vma=False,
    )
```
